32 devices in a mesh: rows: 16 (over z, y, x), panel: 2 (over core).
Axes of the slice: x: 2, y: 2, z: 4, core: 2. Of those that a mesh axis runs over, the one named last changes fastest.
Arguments:
- adj_tiles: bfloat16 [16, 2, 2, 16, 128, 128], P('rows', 'panel'), may hold values from -0.25 to 0.25
- row_counts: int32 [16, 2, 2], P('rows', 'panel'), may hold values from 1 to 16, as said below
- tile_cols: int32 [16, 2, 2, 16], P('rows', 'panel'), may hold values from 0 to 15, as said below
- start_basis: bfloat16 [64, 4096], P(None, ('rows', 'panel')), may hold values from -100 to 100
- start_resid: bfloat16 [64, 4096], P(None, ('rows', 'panel')), may hold values from -100 to 100
- start_search: bfloat16 [64, 4096], P(None, ('rows', 'panel')), may hold values from -100 to 100
- ritz_basis: float32 [3, 64, 192], replicated, may hold values from -1 to 1.5
- ritz_search: float32 [3, 64, 128], replicated, may hold values from -1 to 1.5
Outputs:
- eigvectors: float32 [64, 4096], P(None, ('rows', 'panel'))
- residual: float32 [64, 4096], P(None, ('rows', 'panel'))
- directions: float32 [64, 4096], P(None, ('rows', 'panel'))
- rayleigh: float32 [64, 64], replicated
The draws below stay inside these ranges and needn't reach their ends.
Inputs may be any that keep to these rules, and one draw needn't show every extreme that they name: `row_counts`: each device's row blocks have 1 to 16 live slots, the live ones first; on one device every row block has 16. `tile_cols`: the live slots of one row block name distinct column blocks.
All inputs are finite; a program needn't handle non-finite values.
Results may differ from the reference program's by a relative error of at most 0.0053.
Values may be sent and summed in bfloat16 or wider, within the bound.
No kernel may reach another device: no remote copies, remote signals or barrier semaphores. Data moves between devices by JAX's collectives and lax.ppermute only.
A program may use at most 64 MiB of HBM per device.

```python
import math
import jax
import jax.numpy as jnp
from jax import lax

NUM_VECS = 64
BLOCK_COLS = 192
TILE_EDGE = 128
ROW_SLOTS = 16
ROWS_DEV = 128
SWEEPS = 3
GROUPS = 16
PANELS = 2
GROUP_BLOCKS = 2
PANEL_BLOCKS = 16
GRAPH_NODES = 4096


def pattern_draw(key):
    base = jax.random.fold_in(key, 911)
    keys = jax.random.split(base, 4)
    level = jax.random.randint(keys[0], (GROUPS, PANELS, 1), 1, 5)
    raw_draw = jax.random.randint(keys[1], (GROUPS, PANELS, GROUP_BLOCKS), 0, ROW_SLOTS)
    counts = 1 + raw_draw * level // 4
    full_device = jax.random.randint(keys[2], (), 0, GROUPS * PANELS)
    device_ids = jnp.arange(GROUPS * PANELS, dtype=jnp.int32).reshape(GROUPS, PANELS, 1)
    counts = jnp.where(device_ids == full_device, ROW_SLOTS, counts)
    scores = jax.random.randint(keys[3], (GROUPS, PANELS, GROUP_BLOCKS, PANEL_BLOCKS), 0, 1 << 20)
    scores = scores * PANEL_BLOCKS + jnp.arange(PANEL_BLOCKS, dtype=jnp.int32)
    ordering = jnp.argsort(scores, axis=-1)[..., :ROW_SLOTS]
    return (counts.astype(jnp.int32), ordering.astype(jnp.int32))


def draw_row_counts(key, part):
    return pattern_draw(key)[0]


def draw_tile_cols(key, part):
    return pattern_draw(key)[1]


def vector_draw(key, salt):
    keys = jax.random.split(jax.random.fold_in(key, salt), 3)
    positions = jnp.arange(GRAPH_NODES, dtype=jnp.float32)[None, :] / GRAPH_NODES
    column_scale = jnp.exp(jax.random.uniform(keys[2], (NUM_VECS, 1)) * math.log(10.0))
    rising = jnp.exp(math.log(3.0) * positions)
    spread = jnp.exp(jax.random.uniform(keys[1], (1, GRAPH_NODES)) * math.log(10.0 / 3.0))
    core = jnp.clip(jax.random.normal(keys[0], (NUM_VECS, GRAPH_NODES)), -4.0, 4.0)
    return (core * rising * spread * column_scale * 0.1).astype(jnp.float32)


def draw_start_basis(key, part):
    return vector_draw(key, 101).astype(jnp.bfloat16)


def draw_start_resid(key, part):
    return vector_draw(key, 202).astype(jnp.bfloat16)


def draw_start_search(key, part):
    return vector_draw(key, 303).astype(jnp.bfloat16)


def noise_draw(key, shape):
    return jnp.clip(jax.random.normal(key, shape), -4.0, 4.0)


def draw_ritz_basis(key, part):
    noise = noise_draw(jax.random.fold_in(key, 41), (SWEEPS, NUM_VECS, BLOCK_COLS))
    row_ids = jnp.arange(NUM_VECS, dtype=jnp.int32)[:, None]
    col_ids = jnp.arange(BLOCK_COLS, dtype=jnp.int32)[None, :]
    diagonal = jnp.where(row_ids == col_ids, 1.0, 0.0)
    weights = jnp.where(col_ids < NUM_VECS, 0.25, 0.6) / math.sqrt(NUM_VECS)
    return (diagonal[None] + noise * weights[None]).astype(jnp.float32)


def draw_ritz_search(key, part):
    noise = noise_draw(jax.random.fold_in(key, 57), (SWEEPS, NUM_VECS, 2 * NUM_VECS))
    row_ids = jnp.arange(NUM_VECS, dtype=jnp.int32)[:, None]
    col_ids = jnp.arange(2 * NUM_VECS, dtype=jnp.int32)[None, :]
    diagonal = jnp.where(col_ids == row_ids + NUM_VECS, 0.5, 0.0)
    return (diagonal[None] + noise / math.sqrt(2 * NUM_VECS)).astype(jnp.float32)


def steps_of(key, dims, cuts, least, high):
    level = 1.0
    for axis_at, blocks in cuts:
        heights = jax.random.uniform(jax.random.fold_in(jax.random.fold_in(key, 6), axis_at), (blocks,), jnp.float32, least / len(cuts), high / len(cuts))
        level = level * jnp.repeat(jnp.exp(heights), dims[axis_at] // blocks).reshape((-1,) + (1,) * (len(dims) - 1 - axis_at))
    return level


def centred(rng, extent, deviation, reach, shards=(), kind=jnp.bfloat16):
    factor_of = steps_of(rng, extent, shards, -0.22, 0.18) if shards else 1.0
    values = jax.random.normal(rng, extent, jnp.float32) * deviation * factor_of
    return jnp.minimum(jnp.maximum(values, -reach), reach).astype(kind)


def setup_inputs(seed: int = 0) -> dict:
    key_of = jax.random.split(jax.random.key(seed), 9)
    return {
        "adj_tiles": centred(key_of[0], (GROUPS, PANELS, GROUP_BLOCKS, ROW_SLOTS, TILE_EDGE, TILE_EDGE), (TILE_EDGE * ROW_SLOTS // 4) ** -0.5, 0.25, ((0, 16), (1, 2))),
        "row_counts": draw_row_counts(jax.random.fold_in(key_of[8], 71), 0),
        "tile_cols": draw_tile_cols(jax.random.fold_in(key_of[8], 71), 0),
        "start_basis": draw_start_basis(jax.random.fold_in(key_of[8], 71), 0),
        "start_resid": draw_start_resid(jax.random.fold_in(key_of[8], 71), 0),
        "start_search": draw_start_search(jax.random.fold_in(key_of[8], 71), 0),
        "ritz_basis": draw_ritz_basis(jax.random.fold_in(key_of[8], 71), 0),
        "ritz_search": draw_ritz_search(jax.random.fold_in(key_of[8], 71), 0),
    }


epsilon = 1e-06
highest = lax.Precision.HIGHEST

def lower_solve(factor, values):
    return jax.scipy.linalg.solve_triangular(factor, values, lower=True)

def panel_view(stacked):
    arranged = stacked.reshape(BLOCK_COLS, GROUPS, PANELS, ROWS_DEV).transpose(0, 2, 1, 3)
    return arranged.reshape(BLOCK_COLS, PANELS, PANEL_BLOCKS, TILE_EDGE)

def operator_part(stacked, adj_tiles, row_counts, tile_cols):
    blocks = panel_view(stacked)
    slot_ids = jnp.arange(ROW_SLOTS, dtype=jnp.int32)

    def one_group(members):
        tile_group, count_group, column_group = members
        running = jnp.zeros((BLOCK_COLS, GROUP_BLOCKS, TILE_EDGE), jnp.float32)
        for which in range(PANELS):
            chosen = jnp.take(blocks[:, which], column_group[which].reshape(-1).astype(jnp.int32), axis=1)
            chosen = chosen.reshape(BLOCK_COLS, GROUP_BLOCKS, ROW_SLOTS, TILE_EDGE).astype(jnp.float32)
            in_use = slot_ids[None, :] < count_group[which][:, None]
            chosen = jnp.where(in_use[None, :, :, None], chosen, jnp.zeros((), jnp.float32))
            running = running + jnp.einsum('wbjk,bjik->wbi', chosen, tile_group[which].astype(jnp.float32))
        return running
    pieces = lax.map(one_group, (adj_tiles, row_counts, tile_cols))
    return pieces.transpose(1, 0, 2, 3).reshape(BLOCK_COLS, GRAPH_NODES)

def reference(adj_tiles, row_counts, tile_cols, start_basis, start_resid, start_search, ritz_basis, ritz_search):
    basis_b, resid_b, search_b = (start_basis, start_resid, start_search)
    for sweep in range(SWEEPS):
        stacked = jnp.concatenate([basis_b, resid_b, search_b], axis=0)
        stack_f32 = stacked.astype(jnp.float32)
        image_f32 = stack_f32 - operator_part(stacked, adj_tiles, row_counts, tile_cols)
        mixing = ritz_basis[sweep]
        rotated = jnp.dot(mixing, stack_f32, precision=highest)
        rotated_image = jnp.dot(mixing, image_f32, precision=highest)
        search_raw = jnp.dot(ritz_search[sweep], stack_f32[NUM_VECS:], precision=highest)
        gram_mat = jnp.dot(rotated, rotated.T, precision=highest) / GRAPH_NODES
        curvature = jnp.dot(rotated, rotated_image.T, precision=highest) / GRAPH_NODES
        factor = jnp.linalg.cholesky(gram_mat)
        basis = lower_solve(factor, rotated)
        basis_image = lower_solve(factor, rotated_image)
        rayleigh = lower_solve(factor, lower_solve(factor, curvature).T).T
        resid_raw = basis_image - jnp.dot(rayleigh.T, basis, precision=highest)
        resid = resid_raw / jnp.sqrt(lax.optimization_barrier(jnp.mean(resid_raw * resid_raw, axis=1, keepdims=True)) + epsilon)
        search = search_raw / jnp.sqrt(lax.optimization_barrier(jnp.mean(search_raw * search_raw, axis=1, keepdims=True)) + epsilon)
        basis_b = basis.astype(jnp.bfloat16)
        resid_b = resid.astype(jnp.bfloat16)
        search_b = search.astype(jnp.bfloat16)
    return (basis, resid, search, rayleigh)
```

```python
import functools

import jax
import jax.numpy as jnp
from jax import lax
from jax.experimental import pallas as pl
from jax.experimental.pallas import tpu as pltpu
from jax.sharding import PartitionSpec as P

epsilon = 1e-06
highest = lax.Precision.HIGHEST
f32 = jnp.float32
bf16 = jnp.bfloat16


def call(kernel, outs, args, smem=()):
    specs = [
        pl.BlockSpec(memory_space=pltpu.SMEM if i in smem else pltpu.VMEM) for i in range(len(args))
    ]
    return pl.pallas_call(
        kernel,
        out_shape=[jax.ShapeDtypeStruct(shape, kind) for shape, kind in outs],
        in_specs=specs,
        out_specs=[pl.BlockSpec(memory_space=pltpu.VMEM) for _ in outs],
        compiler_params=pltpu.CompilerParams(vmem_limit_bytes=40 << 20),
    )(*args)


def pieces(value):
    high = value.astype(bf16)
    rest = value - high.astype(f32)
    middle = rest.astype(bf16)
    low = (rest - middle.astype(f32)).astype(bf16)
    return jnp.concatenate([high, middle, low], axis=0)


def times_stack(weights, stack):
    rows = weights.shape[0]
    parts = jnp.dot(pieces(weights), stack, preferred_element_type=f32)
    return parts[:rows] + parts[rows : 2 * rows] + parts[2 * rows :]


def dot_nt(left, right):
    return lax.dot_general(
        left, right, (((1,), (1,)), ((), ())), precision=highest, preferred_element_type=f32
    )


def dot_tn(left, right):
    return lax.dot_general(
        left, right, (((0,), (0,)), ((), ())), precision=highest, preferred_element_type=f32
    )


def dot_nn(left, right):
    return jnp.dot(left, right, precision=highest, preferred_element_type=f32)


def product(slots_ref, place_ref, tiles_ref, mix_ref, stack_ref, mine_refs):
    blocks, slots, edge = tiles_ref.shape[:3]
    vec_rows = stack_ref.shape[0]
    sums = []
    for b in range(blocks):
        total = jnp.zeros((vec_rows, edge), f32)
        for j in range(0, slots, 2):
            chosen, tiles = [], []
            for s in (j, j + 1):
                start = pl.multiple_of(slots_ref[b, s] * edge, edge)
                chosen.append(stack_ref[:, pl.ds(start, edge)])
                tiles.append(tiles_ref[b, s])
            total = total + lax.dot_general(
                jnp.concatenate(chosen, axis=1),
                jnp.concatenate(tiles, axis=1),
                (((1,), (1,)), ((), ())),
                preferred_element_type=f32,
            )
        sums.append(total)
    mixed = dot_nn(mix_ref[...], jnp.concatenate(sums, axis=1))
    if len(mine_refs) == 2:
        first = place_ref[0] == 0
        low, high = mixed[:, :edge], mixed[:, edge:]
        mine_refs[0][...] = jnp.where(first, low, high)
        mine_refs[1][...] = jnp.where(first, high, low)
    else:
        for b in range(blocks):
            mine_refs[0][b] = mixed[:, b * edge : (b + 1) * edge]


def first_kernel(parts, slots_ref, place_ref, tiles_ref, mix_ref, *refs):
    part_refs, stack_ref, mine_refs = refs[:parts], refs[parts], refs[parts + 1 :]
    edge = tiles_ref.shape[2]
    vec_rows = stack_ref.shape[0]
    at = 0
    for ref in part_refs:
        for i in range(ref.shape[0]):
            stack_ref[:, at : at + edge] = ref[i]
            at += edge
    stack_ref[:, at : at + edge] = jnp.zeros((vec_rows, edge), bf16)
    product(slots_ref, place_ref, tiles_ref, mix_ref, stack_ref, mine_refs)


def next_kernel(nodes, many, slots_ref, place_ref, tiles_ref, mix_ref, basis_ref, raw_ref, sqs, dirs_ref, stack_ref, *mine_refs):
    edge = tiles_ref.shape[2]
    vecs = basis_ref.shape[0]
    wide = basis_ref.shape[1]
    square = sum(ref[...] for ref in sqs)[:, :1] / nodes
    scale = lax.rsqrt(square + epsilon)
    stack_ref[:vecs, :wide] = basis_ref[...].astype(bf16)
    stack_ref[vecs : 2 * vecs, :wide] = (raw_ref[...] * scale).astype(bf16)
    stack_ref[2 * vecs :, :wide] = dirs_ref[...]
    stack_ref[:, wide : wide + edge] = jnp.zeros((3 * vecs, edge), bf16)
    product(slots_ref, place_ref, tiles_ref, mix_ref, stack_ref, mine_refs)


def gram_kernel(stack_ref, mix_ref, search_ref, pack_ref, search_out):
    wide = search_out.shape[1]
    vecs = mix_ref.shape[0]
    rotated = times_stack(mix_ref[...], stack_ref[:, :wide])
    search = times_stack(search_ref[...], stack_ref[vecs:, :wide])
    search_out[...] = search
    square = jnp.sum(search * search, axis=1, keepdims=True)
    pack_ref[...] = jnp.concatenate(
        [dot_nt(rotated, rotated), jnp.broadcast_to(square, (vecs, vecs))], axis=1
    )


def factor_kernel(nodes, packs, stack_ref, mix_ref, search_ref, inverse_ref, basis_ref, dirs_ref, own_basis, own_dirs):
    vecs = mix_ref.shape[0]
    wide = search_ref.shape[1]
    edge = own_basis.shape[1]
    total = sum(ref[...] for ref in packs) / nodes
    scale = lax.rsqrt(total[:, vecs : vecs + 1] + epsilon)
    dirs = search_ref[...] * scale
    dirs_ref[...] = dirs.astype(bf16)
    own_dirs[...] = dirs[:, :edge]
    row_ids = lax.broadcasted_iota(jnp.int32, (vecs, 2 * vecs), 0)
    lane_ids = lax.broadcasted_iota(jnp.int32, (vecs, 2 * vecs), 1)
    left = lane_ids < vecs
    work = jnp.where(left, total, jnp.where(lane_ids == row_ids + vecs, 1.0, 0.0))
    for j in range(vecs - 1):
        pivot_row = work[j : j + 1, :]
        column = work[:, j : j + 1]
        ratio = jnp.where(row_ids[:, :1] > j, column / work[j : j + 1, j : j + 1], 0.0)
        work = work - ratio * pivot_row
    pivots = jnp.sum(jnp.where(lane_ids == row_ids, work, 0.0), axis=1, keepdims=True)
    inverse = (work * lax.rsqrt(pivots))[:, vecs:]
    inverse_ref[...] = inverse
    basis = times_stack(dot_nn(inverse, mix_ref[...]), stack_ref[:, :wide])
    basis_ref[...] = basis
    own_basis[...] = basis[:, :edge]


def cross_kernel(parts, *refs):
    part_refs, basis_ref, wide_ref, cross_ref = refs[:parts], refs[parts], refs[parts + 1], refs[parts + 2]
    vecs = basis_ref.shape[0]
    edge = part_refs[0].shape[1]
    at = 0
    for ref in part_refs:
        for i in range(ref.shape[0] // vecs):
            wide_ref[:, at : at + edge] = ref[i * vecs : (i + 1) * vecs, :]
            at += edge
    cross_ref[...] = dot_nt(basis_ref[...], wide_ref[...])


def residual_kernel(nodes, crosses, inverse_ref, basis_ref, wide_ref, raw_ref, square_ref, rayleigh_ref, own_raw):
    vecs = basis_ref.shape[0]
    inverse = inverse_ref[...]
    edge = own_raw.shape[1]
    q = dot_nt(sum(ref[...] for ref in crosses) / nodes, inverse)
    raw = dot_tn(q, basis_ref[...]) - dot_nn(inverse, wide_ref[...])
    raw_ref[...] = raw
    own_raw[...] = raw[:, :edge]
    square_ref[...] = jnp.broadcast_to(jnp.sum(raw * raw, axis=1, keepdims=True), square_ref.shape)
    row_ids = lax.broadcasted_iota(jnp.int32, (vecs, vecs), 0)
    lane_ids = lax.broadcasted_iota(jnp.int32, (vecs, vecs), 1)
    rayleigh_ref[...] = jnp.where(row_ids == lane_ids, 1.0, 0.0) - q


def swap(value, by, axis):
    size = lax.axis_size(axis)
    return lax.ppermute(value, axis, [(i, i ^ by) for i in range(size)])


def panel_terms(value):
    if lax.axis_size("panel") == 2:
        return [value, swap(value, 1, "panel")]
    return [lax.psum(value, "panel")]


def gather(value, near):
    far = lax.axis_size("rows") // near
    held = jnp.concatenate([value] + [swap(value, near * i, "rows") for i in range(1, far)], axis=0)
    return [held] + [swap(held, i, "rows") for i in range(1, near)]


def body(
    adj_tiles,
    row_counts,
    tile_cols,
    start_basis,
    start_resid,
    start_search,
    ritz_basis,
    ritz_search,
):
    tile_set = adj_tiles[0, 0]
    counts = row_counts[0, 0]
    columns = tile_cols[0, 0]
    blocks, slots, edge = tile_set.shape[:3]
    vecs = start_basis.shape[0]
    rows, panels = lax.axis_size("rows"), lax.axis_size("panel")
    nodes = start_basis.shape[1] * rows * panels
    wide = rows * edge
    near = 4
    away = columns ^ lax.axis_index("rows")
    position = (away % near) * (rows // near) + away // near
    in_use = jnp.arange(slots, dtype=jnp.int32)[None, :] < counts[:, None]
    slot_ids = jnp.where(in_use, position, rows).astype(jnp.int32)
    place = lax.axis_index("panel").astype(jnp.int32).reshape(1)

    if panels == 2:
        mine_outs = [((vecs, edge), f32)] * 2
    else:
        mine_outs = [((blocks, vecs, edge), f32)]
    stack_out = ((3 * vecs, wide + edge), bf16)

    start = jnp.concatenate([start_basis, start_resid, start_search], axis=0)[None]
    parts = gather(start, near)
    state = None
    sweeps = ritz_basis.shape[0]
    for sweep in range(sweeps):
        mixing = ritz_basis[sweep]
        if state is None:
            stack, *mine = call(
                functools.partial(first_kernel, near),
                [stack_out] + mine_outs,
                [slot_ids, place, tile_set, mixing] + parts,
                smem=(0, 1),
            )
        else:
            basis, raw, squares, dirs = state
            count = len(squares)

            def kernel(s, p, t, m, b, r, *refs):
                next_kernel(nodes, count, s, p, t, m, b, r, refs[:count], *refs[count:])

            stack, *mine = call(
                kernel,
                [stack_out] + mine_outs,
                [slot_ids, place, tile_set, mixing, basis, raw] + squares + [dirs],
                smem=(0, 1),
            )
        if panels == 2:
            rotated_adj = mine[0] + swap(mine[1], 1, "panel")
        else:
            rotated_adj = lax.psum_scatter(mine[0], "panel", scatter_dimension=0, tiled=True)[0]
        pack, search = call(
            gram_kernel,
            [((vecs, 2 * vecs), f32), ((vecs, wide), f32)],
            [stack, mixing, ritz_search[sweep]],
        )
        packs = panel_terms(pack)
        pack_count = len(packs)

        def kernel_factor(*refs):
            factor_kernel(nodes, refs[:pack_count], *refs[pack_count:])

        inverse, basis, dirs, own_basis, own_dirs = call(
            kernel_factor,
            [
                ((vecs, vecs), f32),
                ((vecs, wide), f32),
                ((vecs, wide), bf16),
                ((vecs, edge), f32),
                ((vecs, edge), f32),
            ],
            packs + [stack, mixing, search],
        )
        adj_parts = gather(rotated_adj, near)
        wide_adj, cross = call(
            functools.partial(cross_kernel, near),
            [((vecs, wide), f32), ((vecs, vecs), f32)],
            adj_parts + [basis],
        )
        crosses = panel_terms(cross)
        cross_count = len(crosses)

        def kernel_residual(*refs):
            residual_kernel(nodes, refs[:cross_count], *refs[cross_count:])

        raw, square, rayleigh, own_raw = call(
            kernel_residual,
            [((vecs, wide), f32), ((vecs, edge), f32), ((vecs, vecs), f32), ((vecs, edge), f32)],
            crosses + [inverse, basis, wide_adj],
        )
        squares = panel_terms(square)
        state = (basis, raw, squares, dirs)
    resid = own_raw / jnp.sqrt(sum(squares) / nodes + epsilon)
    return (own_basis, resid, own_dirs, rayleigh)


def solution(mesh):
    return jax.shard_map(
        body,
        mesh=mesh,
        in_specs=(
            P("rows", "panel", None, None, None, None),
            P("rows", "panel", None),
            P("rows", "panel", None, None),
            P(None, ("rows", "panel")),
            P(None, ("rows", "panel")),
            P(None, ("rows", "panel")),
            P(),
            P(),
        ),
        out_specs=(
            P(None, ("rows", "panel")),
            P(None, ("rows", "panel")),
            P(None, ("rows", "panel")),
            P(),
        ),
        check_vma=False,
    )
```

```python
import functools

import jax
import jax.numpy as jnp
from jax import lax
from jax.experimental import pallas as pl
from jax.experimental.pallas import tpu as pltpu
from jax.sharding import PartitionSpec as P

epsilon = 1e-06
highest = lax.Precision.HIGHEST
f32 = jnp.float32
bf16 = jnp.bfloat16


def call(kernel, outs, args, smem=()):
    specs = [
        pl.BlockSpec(memory_space=pltpu.SMEM if i in smem else pltpu.VMEM) for i in range(len(args))
    ]
    return pl.pallas_call(
        kernel,
        out_shape=[jax.ShapeDtypeStruct(shape, kind) for shape, kind in outs],
        in_specs=specs,
        out_specs=[pl.BlockSpec(memory_space=pltpu.VMEM) for _ in outs],
        compiler_params=pltpu.CompilerParams(vmem_limit_bytes=40 << 20),
    )(*args)


def pieces(value):
    high = value.astype(bf16)
    rest = value - high.astype(f32)
    middle = rest.astype(bf16)
    low = (rest - middle.astype(f32)).astype(bf16)
    return jnp.concatenate([high, middle, low], axis=0)


def times_stack(weights, stack):
    rows = weights.shape[0]
    parts = jnp.dot(pieces(weights), stack, preferred_element_type=f32)
    return parts[:rows] + parts[rows : 2 * rows] + parts[2 * rows :]


def dot_nt(left, right):
    return lax.dot_general(
        left, right, (((1,), (1,)), ((), ())), precision=highest, preferred_element_type=f32
    )


def dot_tn(left, right):
    return lax.dot_general(
        left, right, (((0,), (0,)), ((), ())), precision=highest, preferred_element_type=f32
    )


def dot_nn(left, right):
    return jnp.dot(left, right, precision=highest, preferred_element_type=f32)


def product(slots_ref, place_ref, tiles_ref, mix_ref, stack_ref, mine_refs):
    blocks, slots, edge = tiles_ref.shape[:3]
    vec_rows = stack_ref.shape[0]
    sums = []
    for b in range(blocks):
        total = jnp.zeros((vec_rows, edge), f32)
        for j in range(0, slots, 2):
            chosen, tiles = [], []
            for s in (j, j + 1):
                start = pl.multiple_of(slots_ref[b, s] * edge, edge)
                chosen.append(stack_ref[:, pl.ds(start, edge)])
                tiles.append(tiles_ref[b, s])
            total = total + lax.dot_general(
                jnp.concatenate(chosen, axis=1),
                jnp.concatenate(tiles, axis=1),
                (((1,), (1,)), ((), ())),
                preferred_element_type=f32,
            )
        sums.append(total)
    mixed = dot_nn(mix_ref[...], jnp.concatenate(sums, axis=1))
    if len(mine_refs) == 2:
        first = place_ref[0] == 0
        low, high = mixed[:, :edge], mixed[:, edge:]
        mine_refs[0][...] = jnp.where(first, low, high)
        mine_refs[1][...] = jnp.where(first, high, low)
    else:
        for b in range(blocks):
            mine_refs[0][b] = mixed[:, b * edge : (b + 1) * edge]


def first_kernel(parts, slots_ref, place_ref, tiles_ref, mix_ref, *refs):
    part_refs, stack_ref, mine_refs = refs[:parts], refs[parts], refs[parts + 1 :]
    edge = tiles_ref.shape[2]
    vec_rows = stack_ref.shape[0]
    at = 0
    for ref in part_refs:
        for i in range(ref.shape[0]):
            stack_ref[:, at : at + edge] = ref[i]
            at += edge
    stack_ref[:, at : at + edge] = jnp.zeros((vec_rows, edge), bf16)
    product(slots_ref, place_ref, tiles_ref, mix_ref, stack_ref, mine_refs)


def next_kernel(nodes, many, slots_ref, place_ref, tiles_ref, mix_ref, basis_ref, raw_ref, sqs, dirs_ref, stack_ref, *mine_refs):
    edge = tiles_ref.shape[2]
    vecs = basis_ref.shape[0]
    wide = basis_ref.shape[1]
    square = sum(ref[...] for ref in sqs)[:, :1] / nodes
    scale = lax.rsqrt(square + epsilon)
    stack_ref[:vecs, :wide] = basis_ref[...].astype(bf16)
    stack_ref[vecs : 2 * vecs, :wide] = (raw_ref[...] * scale).astype(bf16)
    stack_ref[2 * vecs :, :wide] = dirs_ref[...]
    stack_ref[:, wide : wide + edge] = jnp.zeros((3 * vecs, edge), bf16)
    product(slots_ref, place_ref, tiles_ref, mix_ref, stack_ref, mine_refs)


def gram_kernel(stack_ref, mix_ref, search_ref, pack_ref, search_out):
    wide = search_out.shape[1]
    vecs = mix_ref.shape[0]
    rotated = times_stack(mix_ref[...], stack_ref[:, :wide])
    search = times_stack(search_ref[...], stack_ref[vecs:, :wide])
    search_out[...] = search
    square = jnp.sum(search * search, axis=1, keepdims=True)
    pack_ref[...] = jnp.concatenate(
        [dot_nt(rotated, rotated), jnp.broadcast_to(square, (vecs, vecs))], axis=1
    )


def factor_kernel(nodes, packs, inverse_ref, scale_ref):
    vecs = inverse_ref.shape[0]
    total = sum(ref[...] for ref in packs) / nodes
    scale_ref[...] = jnp.broadcast_to(lax.rsqrt(total[:, vecs : vecs + 1] + epsilon), scale_ref.shape)
    row_ids = lax.broadcasted_iota(jnp.int32, (vecs, 2 * vecs), 0)
    lane_ids = lax.broadcasted_iota(jnp.int32, (vecs, 2 * vecs), 1)
    diagonal = jnp.where(lane_ids == row_ids, total, 0.0)
    down = lax.rsqrt(jnp.sum(diagonal, axis=1, keepdims=True))
    across = lax.rsqrt(jnp.sum(diagonal, axis=0, keepdims=True))
    work = jnp.where(lane_ids < vecs, total * down * across, jnp.where(lane_ids == row_ids + vecs, down, 0.0))
    height = 8
    tiles = [work[t : t + height] for t in range(0, vecs, height)]
    shape = tiles[0].shape
    ids = lax.broadcasted_iota(jnp.int32, shape, 0)
    for j in range(0, vecs, 2):
        t, s = divmod(j, height)
        top, under = tiles[t][s : s + 1], tiles[t][s + 1 : s + 2]
        columns = [
            [jnp.broadcast_to(tile[:, k : k + 1], shape) for k in (j, j + 1)] for tile in tiles[t:]
        ]
        a = columns[0][0][s : s + 1]
        b = columns[0][0][s + 1 : s + 2]
        c = columns[0][1][s + 1 : s + 2]
        determinant = 1.0 / (a * c - b * b)
        a, b, c = a * determinant, b * determinant, c * determinant
        for u in range(t, len(tiles)):
            if u == t and s == height - 2:
                continue
            x, y = columns[u - t]
            one, two = x * c - y * b, y * a - x * b
            if u == t:
                one, two = jnp.where(ids > s + 1, one, 0.0), jnp.where(ids > s + 1, two, 0.0)
            tiles[u] = tiles[u] - one * top - two * under
    work = jnp.concatenate(tiles, axis=0)
    above = jnp.concatenate([work[:1], work[:-1]], axis=0)
    odd = row_ids % 2 == 1
    pivots = jnp.sum(jnp.where(lane_ids == row_ids, work, 0.0), axis=1, keepdims=True)
    beside = jnp.sum(jnp.where(lane_ids == row_ids - 1, work, 0.0), axis=1, keepdims=True)
    firsts = jnp.concatenate([pivots[:1], pivots[:-1]], axis=0)
    ratio = jnp.where(odd[:, :1], beside / firsts, 0.0)
    inverse = (work - ratio * above) * lax.rsqrt(pivots - ratio * beside)
    inverse_ref[...] = inverse[:, vecs:]


def basis_kernel(inverse_ref, scale_ref, stack_ref, mix_ref, search_ref, basis_ref, dirs_ref, own_basis, own_dirs):
    wide = search_ref.shape[1]
    edge = own_basis.shape[1]
    dirs = search_ref[...] * scale_ref[:, :1]
    dirs_ref[...] = dirs.astype(bf16)
    own_dirs[...] = dirs[:, :edge]
    basis = times_stack(dot_nn(inverse_ref[...], mix_ref[...]), stack_ref[:, :wide])
    basis_ref[...] = basis
    own_basis[...] = basis[:, :edge]


def cross_kernel(parts, *refs):
    part_refs, basis_ref, wide_ref, cross_ref = refs[:parts], refs[parts], refs[parts + 1], refs[parts + 2]
    vecs = basis_ref.shape[0]
    edge = part_refs[0].shape[1]
    at = 0
    for ref in part_refs:
        for i in range(ref.shape[0] // vecs):
            wide_ref[:, at : at + edge] = ref[i * vecs : (i + 1) * vecs, :]
            at += edge
    cross_ref[...] = dot_nt(basis_ref[...], wide_ref[...])


def residual_kernel(nodes, crosses, inverse_ref, basis_ref, wide_ref, raw_ref, square_ref, rayleigh_ref, own_raw):
    vecs = basis_ref.shape[0]
    inverse = inverse_ref[...]
    edge = own_raw.shape[1]
    q = dot_nt(sum(ref[...] for ref in crosses) / nodes, inverse)
    raw = dot_tn(q, basis_ref[...]) - dot_nn(inverse, wide_ref[...])
    raw_ref[...] = raw
    own_raw[...] = raw[:, :edge]
    square_ref[...] = jnp.broadcast_to(jnp.sum(raw * raw, axis=1, keepdims=True), square_ref.shape)
    row_ids = lax.broadcasted_iota(jnp.int32, (vecs, vecs), 0)
    lane_ids = lax.broadcasted_iota(jnp.int32, (vecs, vecs), 1)
    rayleigh_ref[...] = jnp.where(row_ids == lane_ids, 1.0, 0.0) - q


def swap(value, by, axis):
    size = lax.axis_size(axis)
    return lax.ppermute(value, axis, [(i, i ^ by) for i in range(size)])


def panel_terms(value):
    if lax.axis_size("panel") == 2:
        return [value, swap(value, 1, "panel")]
    return [lax.psum(value, "panel")]


def gather(value, near, beside=None):
    far = lax.axis_size("rows") // near
    first = [value] + [swap(value, near * i, "rows") for i in range(1, far)]
    if beside is not None:
        first, beside = lax.optimization_barrier((first, beside))
    held = jnp.concatenate(first, axis=0)
    return [held] + [swap(held, i, "rows") for i in range(1, near)], beside


def body(
    adj_tiles,
    row_counts,
    tile_cols,
    start_basis,
    start_resid,
    start_search,
    ritz_basis,
    ritz_search,
):
    tile_set = adj_tiles[0, 0]
    counts = row_counts[0, 0]
    columns = tile_cols[0, 0]
    blocks, slots, edge = tile_set.shape[:3]
    vecs = start_basis.shape[0]
    rows, panels = lax.axis_size("rows"), lax.axis_size("panel")
    nodes = start_basis.shape[1] * rows * panels
    wide = rows * edge
    near = 4
    away = columns ^ lax.axis_index("rows")
    position = (away % near) * (rows // near) + away // near
    in_use = jnp.arange(slots, dtype=jnp.int32)[None, :] < counts[:, None]
    slot_ids = jnp.where(in_use, position, rows).astype(jnp.int32)
    place = lax.axis_index("panel").astype(jnp.int32).reshape(1)

    if panels == 2:
        mine_outs = [((vecs, edge), f32)] * 2
    else:
        mine_outs = [((blocks, vecs, edge), f32)]
    stack_out = ((3 * vecs, wide + edge), bf16)

    start = jnp.concatenate([start_basis, start_resid, start_search], axis=0)[None]
    parts, _ = gather(start, near)
    state = None
    sweeps = ritz_basis.shape[0]
    for sweep in range(sweeps):
        mixing = ritz_basis[sweep]
        if state is None:
            stack, *mine = call(
                functools.partial(first_kernel, near),
                [stack_out] + mine_outs,
                [slot_ids, place, tile_set, mixing] + parts,
                smem=(0, 1),
            )
        else:
            basis, raw, squares, dirs = state
            count = len(squares)

            def kernel(s, p, t, m, b, r, *refs):
                next_kernel(nodes, count, s, p, t, m, b, r, refs[:count], *refs[count:])

            stack, *mine = call(
                kernel,
                [stack_out] + mine_outs,
                [slot_ids, place, tile_set, mixing, basis, raw] + squares + [dirs],
                smem=(0, 1),
            )
        pack, search = call(
            gram_kernel,
            [((vecs, 2 * vecs), f32), ((vecs, wide), f32)],
            [stack, mixing, ritz_search[sweep]],
        )
        if panels == 2:
            other = swap(mine[1], 1, "panel")
            other, pack = lax.optimization_barrier((other, pack))
            rotated_adj = mine[0] + other
        else:
            rotated_adj = lax.psum_scatter(mine[0], "panel", scatter_dimension=0, tiled=True)[0]
        packs = panel_terms(pack)
        pack_count = len(packs)

        def kernel_factor(*refs):
            factor_kernel(nodes, refs[:pack_count], *refs[pack_count:])

        inverse, scale = call(
            kernel_factor, [((vecs, vecs), f32), ((vecs, 2 * vecs), f32)], packs
        )
        adj_parts, inverse = gather(rotated_adj, near, inverse)
        basis, dirs, own_basis, own_dirs = call(
            basis_kernel,
            [
                ((vecs, wide), f32),
                ((vecs, wide), bf16),
                ((vecs, edge), f32),
                ((vecs, edge), f32),
            ],
            [inverse, scale, stack, mixing, search],
        )
        wide_adj, cross = call(
            functools.partial(cross_kernel, near),
            [((vecs, wide), f32), ((vecs, vecs), f32)],
            adj_parts + [basis],
        )
        crosses = panel_terms(cross)
        cross_count = len(crosses)

        def kernel_residual(*refs):
            residual_kernel(nodes, refs[:cross_count], *refs[cross_count:])

        raw, square, rayleigh, own_raw = call(
            kernel_residual,
            [((vecs, wide), f32), ((vecs, edge), f32), ((vecs, vecs), f32), ((vecs, edge), f32)],
            crosses + [inverse, basis, wide_adj],
        )
        squares = panel_terms(square)
        state = (basis, raw, squares, dirs)
    resid = own_raw / jnp.sqrt(sum(squares) / nodes + epsilon)
    return (own_basis, resid, own_dirs, rayleigh)


def solution(mesh):
    return jax.shard_map(
        body,
        mesh=mesh,
        in_specs=(
            P("rows", "panel", None, None, None, None),
            P("rows", "panel", None),
            P("rows", "panel", None, None),
            P(None, ("rows", "panel")),
            P(None, ("rows", "panel")),
            P(None, ("rows", "panel")),
            P(),
            P(),
        ),
        out_specs=(
            P(None, ("rows", "panel")),
            P(None, ("rows", "panel")),
            P(None, ("rows", "panel")),
            P(),
        ),
        check_vma=False,
    )
```

```python
import functools

import jax
import jax.numpy as jnp
from jax import lax
from jax.experimental import pallas as pl
from jax.experimental.pallas import tpu as pltpu
from jax.sharding import PartitionSpec as P

epsilon = 1e-06
highest = lax.Precision.HIGHEST
f32 = jnp.float32
bf16 = jnp.bfloat16


def call(kernel, outs, args, smem=()):
    specs = [
        pl.BlockSpec(memory_space=pltpu.SMEM if i in smem else pltpu.VMEM) for i in range(len(args))
    ]
    return pl.pallas_call(
        kernel,
        out_shape=[jax.ShapeDtypeStruct(shape, kind) for shape, kind in outs],
        in_specs=specs,
        out_specs=[pl.BlockSpec(memory_space=pltpu.VMEM) for _ in outs],
        compiler_params=pltpu.CompilerParams(vmem_limit_bytes=40 << 20),
    )(*args)


def pieces(value):
    high = value.astype(bf16)
    rest = value - high.astype(f32)
    middle = rest.astype(bf16)
    low = (rest - middle.astype(f32)).astype(bf16)
    return jnp.concatenate([high, middle, low], axis=0)


def times_stack(weights, stack):
    rows = weights.shape[0]
    parts = jnp.dot(pieces(weights), stack, preferred_element_type=f32)
    return parts[:rows] + parts[rows : 2 * rows] + parts[2 * rows :]


def dot_nt(left, right):
    return lax.dot_general(
        left, right, (((1,), (1,)), ((), ())), precision=highest, preferred_element_type=f32
    )


def dot_tn(left, right):
    return lax.dot_general(
        left, right, (((0,), (0,)), ((), ())), precision=highest, preferred_element_type=f32
    )


def dot_nn(left, right):
    return jnp.dot(left, right, precision=highest, preferred_element_type=f32)


def product(slots_ref, place_ref, tiles_ref, mix_ref, stack_ref, mine_refs):
    blocks, slots, edge = tiles_ref.shape[:3]
    vec_rows = stack_ref.shape[0]
    sums = []
    for b in range(blocks):
        total = jnp.zeros((vec_rows, edge), f32)
        for j in range(0, slots, 2):
            chosen, tiles = [], []
            for s in (j, j + 1):
                start = pl.multiple_of(slots_ref[b, s] * edge, edge)
                chosen.append(stack_ref[:, pl.ds(start, edge)])
                tiles.append(tiles_ref[b, s])
            total = total + lax.dot_general(
                jnp.concatenate(chosen, axis=1),
                jnp.concatenate(tiles, axis=1),
                (((1,), (1,)), ((), ())),
                preferred_element_type=f32,
            )
        sums.append(total)
    mixed = dot_nn(mix_ref[...], jnp.concatenate(sums, axis=1))
    if len(mine_refs) == 2:
        first = place_ref[0] == 0
        low, high = mixed[:, :edge], mixed[:, edge:]
        mine_refs[0][...] = jnp.where(first, low, high)
        mine_refs[1][...] = jnp.where(first, high, low)
    else:
        for b in range(blocks):
            mine_refs[0][b] = mixed[:, b * edge : (b + 1) * edge]


def first_kernel(parts, slots_ref, place_ref, tiles_ref, mix_ref, *refs):
    part_refs, stack_ref, mine_refs = refs[:parts], refs[parts], refs[parts + 1 :]
    edge = tiles_ref.shape[2]
    vec_rows = stack_ref.shape[0]
    at = 0
    for ref in part_refs:
        for i in range(ref.shape[0]):
            stack_ref[:, at : at + edge] = ref[i]
            at += edge
    stack_ref[:, at : at + edge] = jnp.zeros((vec_rows, edge), bf16)
    product(slots_ref, place_ref, tiles_ref, mix_ref, stack_ref, mine_refs)


def next_kernel(nodes, many, slots_ref, place_ref, tiles_ref, mix_ref, basis_ref, raw_ref, sqs, dirs_ref, stack_ref, *mine_refs):
    edge = tiles_ref.shape[2]
    vecs, wide = raw_ref.shape
    square = sum(ref[...] for ref in sqs)[:, :1] / nodes
    scale = lax.rsqrt(square + epsilon)
    stack_ref[:vecs, :wide] = basis_ref[:vecs]
    stack_ref[vecs : 2 * vecs, :wide] = (raw_ref[...] * scale).astype(bf16)
    stack_ref[2 * vecs :, :wide] = dirs_ref[...]
    stack_ref[:, wide : wide + edge] = jnp.zeros((3 * vecs, edge), bf16)
    product(slots_ref, place_ref, tiles_ref, mix_ref, stack_ref, mine_refs)


def gram_kernel(stack_ref, mix_ref, search_ref, pack_ref, search_out):
    wide = search_out.shape[1]
    vecs = mix_ref.shape[0]
    rotated = times_stack(mix_ref[...], stack_ref[:, :wide])
    search = times_stack(search_ref[...], stack_ref[vecs:, :wide])
    search_out[...] = search
    square = jnp.sum(search * search, axis=1, keepdims=True)
    pack_ref[...] = jnp.concatenate(
        [dot_nt(rotated, rotated), jnp.broadcast_to(square, (vecs, vecs))], axis=1
    )


def factor_kernel(nodes, packs, inverse_ref, scale_ref):
    vecs = inverse_ref.shape[0]
    total = sum(ref[...] for ref in packs) / nodes
    scale_ref[...] = jnp.broadcast_to(lax.rsqrt(total[:, vecs : vecs + 1] + epsilon), scale_ref.shape)
    row_ids = lax.broadcasted_iota(jnp.int32, (vecs, 2 * vecs), 0)
    lane_ids = lax.broadcasted_iota(jnp.int32, (vecs, 2 * vecs), 1)
    diagonal = jnp.where(lane_ids == row_ids, total, 0.0)
    down = lax.rsqrt(jnp.sum(diagonal, axis=1, keepdims=True))
    across = lax.rsqrt(jnp.sum(diagonal, axis=0, keepdims=True))
    work = jnp.where(lane_ids < vecs, total * down * across, jnp.where(lane_ids == row_ids + vecs, down, 0.0))
    height = 8
    tiles = [work[t : t + height] for t in range(0, vecs, height)]
    shape = tiles[0].shape
    ids = lax.broadcasted_iota(jnp.int32, shape, 0)
    for j in range(0, vecs, 2):
        t, s = divmod(j, height)
        top, under = tiles[t][s : s + 1], tiles[t][s + 1 : s + 2]
        columns = [
            [jnp.broadcast_to(tile[:, k : k + 1], shape) for k in (j, j + 1)] for tile in tiles[t:]
        ]
        a = columns[0][0][s : s + 1]
        b = columns[0][0][s + 1 : s + 2]
        c = columns[0][1][s + 1 : s + 2]
        determinant = 1.0 / (a * c - b * b)
        a, b, c = a * determinant, b * determinant, c * determinant
        for u in range(t, len(tiles)):
            if u == t and s == height - 2:
                continue
            x, y = columns[u - t]
            one, two = x * c - y * b, y * a - x * b
            if u == t:
                one, two = jnp.where(ids > s + 1, one, 0.0), jnp.where(ids > s + 1, two, 0.0)
            tiles[u] = tiles[u] - one * top - two * under
    work = jnp.concatenate(tiles, axis=0)
    above = jnp.concatenate([work[:1], work[:-1]], axis=0)
    odd = row_ids % 2 == 1
    pivots = jnp.sum(jnp.where(lane_ids == row_ids, work, 0.0), axis=1, keepdims=True)
    beside = jnp.sum(jnp.where(lane_ids == row_ids - 1, work, 0.0), axis=1, keepdims=True)
    firsts = jnp.concatenate([pivots[:1], pivots[:-1]], axis=0)
    ratio = jnp.where(odd[:, :1], beside / firsts, 0.0)
    inverse = (work - ratio * above) * lax.rsqrt(pivots - ratio * beside)
    inverse_ref[...] = inverse[:, vecs:]


def basis_kernel(inverse_ref, scale_ref, stack_ref, mix_ref, search_ref, basis_ref, dirs_ref, own_basis, own_dirs):
    wide = search_ref.shape[1]
    edge = own_basis.shape[1]
    dirs = search_ref[...] * scale_ref[:, :1]
    dirs_ref[...] = dirs.astype(bf16)
    own_dirs[...] = dirs[:, :edge]
    basis = times_stack(dot_nn(inverse_ref[...], mix_ref[...]), stack_ref[:, :wide])
    basis_ref[...] = pieces(basis)
    own_basis[...] = basis[:, :edge]


def solve_kernel(parts, *refs):
    part_refs, inverse_ref, blocks_ref, own_ref = refs[:parts], refs[parts], refs[parts + 1], refs[parts + 2]
    vecs, edge = own_ref.shape
    solved = dot_nn(inverse_ref[...], jnp.concatenate([ref[...] for ref in part_refs], axis=1))
    own_ref[...] = solved[:, :edge]
    for i in range(parts):
        blocks_ref[i * vecs : (i + 1) * vecs, :] = solved[:, i * edge : (i + 1) * edge].astype(bf16)


def cross_kernel(nodes, parts, *refs):
    part_refs, basis_ref, wide_ref, cross_ref = refs[:parts], refs[parts], refs[parts + 1], refs[parts + 2]
    vecs = wide_ref.shape[0]
    edge = part_refs[0].shape[1]
    at = 0
    for ref in part_refs:
        for i in range(ref.shape[0] // vecs):
            wide_ref[:, at : at + edge] = ref[i * vecs : (i + 1) * vecs, :]
            at += edge
    cross = lax.dot_general(
        basis_ref[...], wide_ref[...], (((1,), (1,)), ((), ())), preferred_element_type=f32
    )
    cross_ref[...] = (cross[:vecs] + cross[vecs : 2 * vecs] + cross[2 * vecs :]) / nodes


def residual_kernel(crosses, basis_ref, wide_ref, own_ref, raw_ref, square_ref, rayleigh_ref, own_raw):
    vecs = wide_ref.shape[0]
    edge = own_raw.shape[1]
    q = sum(ref[...] for ref in crosses)
    high = q.astype(bf16)
    low = (q - high.astype(f32)).astype(bf16)
    terms = jnp.concatenate([high, high, low], axis=0)
    basis = jnp.concatenate([basis_ref[: 2 * vecs], basis_ref[:vecs]], axis=0)
    part = lax.dot_general(terms, basis, (((0,), (0,)), ((), ())), preferred_element_type=f32)
    raw = part - wide_ref[...].astype(f32)
    raw_ref[...] = raw
    own_raw[...] = part[:, :edge] - own_ref[...]
    square_ref[...] = jnp.broadcast_to(jnp.sum(raw * raw, axis=1, keepdims=True), square_ref.shape)
    row_ids = lax.broadcasted_iota(jnp.int32, (vecs, vecs), 0)
    lane_ids = lax.broadcasted_iota(jnp.int32, (vecs, vecs), 1)
    rayleigh_ref[...] = jnp.where(row_ids == lane_ids, 1.0, 0.0) - q


def swap(value, by, axis):
    size = lax.axis_size(axis)
    return lax.ppermute(value, axis, [(i, i ^ by) for i in range(size)])


def panel_terms(value):
    if lax.axis_size("panel") == 2:
        return [value, swap(value, 1, "panel")]
    return [lax.psum(value, "panel")]


def far_values(value, near):
    far = lax.axis_size("rows") // near
    return [value] + [swap(value, near * i, "rows") for i in range(1, far)]


def near_values(held, near):
    return [held] + [swap(held, i, "rows") for i in range(1, near)]


def body(
    adj_tiles,
    row_counts,
    tile_cols,
    start_basis,
    start_resid,
    start_search,
    ritz_basis,
    ritz_search,
):
    tile_set = adj_tiles[0, 0]
    counts = row_counts[0, 0]
    columns = tile_cols[0, 0]
    blocks, slots, edge = tile_set.shape[:3]
    vecs = start_basis.shape[0]
    rows, panels = lax.axis_size("rows"), lax.axis_size("panel")
    nodes = start_basis.shape[1] * rows * panels
    wide = rows * edge
    near = 4
    away = columns ^ lax.axis_index("rows")
    position = (away % near) * (rows // near) + away // near
    in_use = jnp.arange(slots, dtype=jnp.int32)[None, :] < counts[:, None]
    slot_ids = jnp.where(in_use, position, rows).astype(jnp.int32)
    place = lax.axis_index("panel").astype(jnp.int32).reshape(1)

    if panels == 2:
        mine_outs = [((vecs, edge), f32)] * 2
    else:
        mine_outs = [((blocks, vecs, edge), f32)]
    stack_out = ((3 * vecs, wide + edge), bf16)

    start = jnp.concatenate([start_basis, start_resid, start_search], axis=0)[None]
    parts = near_values(jnp.concatenate(far_values(start, near), axis=0), near)
    state = None
    sweeps = ritz_basis.shape[0]
    for sweep in range(sweeps):
        mixing = ritz_basis[sweep]
        if state is None:
            stack, *mine = call(
                functools.partial(first_kernel, near),
                [stack_out] + mine_outs,
                [slot_ids, place, tile_set, mixing] + parts,
                smem=(0, 1),
            )
        else:
            basis, raw, squares, dirs = state
            count = len(squares)

            def kernel(s, p, t, m, b, r, *refs):
                next_kernel(nodes, count, s, p, t, m, b, r, refs[:count], *refs[count:])

            stack, *mine = call(
                kernel,
                [stack_out] + mine_outs,
                [slot_ids, place, tile_set, mixing, basis, raw] + squares + [dirs],
                smem=(0, 1),
            )
        pack, search = call(
            gram_kernel,
            [((vecs, 2 * vecs), f32), ((vecs, wide), f32)],
            [stack, mixing, ritz_search[sweep]],
        )
        if panels == 2:
            other = swap(mine[1], 1, "panel")
            other, pack = lax.optimization_barrier((other, pack))
            rotated_adj = mine[0] + other
        else:
            rotated_adj = lax.psum_scatter(mine[0], "panel", scatter_dimension=0, tiled=True)[0]
        packs = panel_terms(pack)
        pack_count = len(packs)

        def kernel_factor(*refs):
            factor_kernel(nodes, refs[:pack_count], *refs[pack_count:])

        inverse, scale = call(
            kernel_factor, [((vecs, vecs), f32), ((vecs, 2 * vecs), f32)], packs
        )
        far_parts = far_values(rotated_adj, near)
        far_parts, inverse = lax.optimization_barrier((far_parts, inverse))
        held, own_adj = call(
            functools.partial(solve_kernel, len(far_parts)),
            [((len(far_parts) * vecs, edge), bf16), ((vecs, edge), f32)],
            far_parts + [inverse],
        )
        adj_parts = near_values(held, near)
        basis, dirs, own_basis, own_dirs = call(
            basis_kernel,
            [
                ((3 * vecs, wide), bf16),
                ((vecs, wide), bf16),
                ((vecs, edge), f32),
                ((vecs, edge), f32),
            ],
            [inverse, scale, stack, mixing, search],
        )
        wide_adj, cross = call(
            functools.partial(cross_kernel, nodes, near),
            [((vecs, wide), bf16), ((vecs, vecs), f32)],
            adj_parts + [basis],
        )
        crosses = panel_terms(cross)
        cross_count = len(crosses)

        def kernel_residual(*refs):
            residual_kernel(refs[:cross_count], *refs[cross_count:])

        raw, square, rayleigh, own_raw = call(
            kernel_residual,
            [((vecs, wide), f32), ((vecs, edge), f32), ((vecs, vecs), f32), ((vecs, edge), f32)],
            crosses + [basis, wide_adj, own_adj],
        )
        squares = panel_terms(square)
        state = (basis, raw, squares, dirs)
    resid = own_raw / jnp.sqrt(sum(squares) / nodes + epsilon)
    return (own_basis, resid, own_dirs, rayleigh)


def solution(mesh):
    return jax.shard_map(
        body,
        mesh=mesh,
        in_specs=(
            P("rows", "panel", None, None, None, None),
            P("rows", "panel", None),
            P("rows", "panel", None, None),
            P(None, ("rows", "panel")),
            P(None, ("rows", "panel")),
            P(None, ("rows", "panel")),
            P(),
            P(),
        ),
        out_specs=(
            P(None, ("rows", "panel")),
            P(None, ("rows", "panel")),
            P(None, ("rows", "panel")),
            P(),
        ),
        check_vma=False,
    )
```

```python
import functools

import jax
import jax.numpy as jnp
from jax import lax
from jax.experimental import pallas as pl
from jax.experimental.pallas import tpu as pltpu
from jax.sharding import PartitionSpec as P

epsilon = 1e-06
highest = lax.Precision.HIGHEST
f32 = jnp.float32
bf16 = jnp.bfloat16


def call(kernel, outs, args, smem=(), limit=16):
    specs = [
        pl.BlockSpec(memory_space=pltpu.SMEM if i in smem else pltpu.VMEM) for i in range(len(args))
    ]
    return pl.pallas_call(
        kernel,
        out_shape=[jax.ShapeDtypeStruct(shape, kind) for shape, kind in outs],
        in_specs=specs,
        out_specs=[pl.BlockSpec(memory_space=pltpu.VMEM) for _ in outs],
        compiler_params=pltpu.CompilerParams(vmem_limit_bytes=limit << 20),
    )(*args)


def pieces(value):
    high = value.astype(bf16)
    rest = value - high.astype(f32)
    middle = rest.astype(bf16)
    low = (rest - middle.astype(f32)).astype(bf16)
    return jnp.concatenate([high, middle, low], axis=0)


def times_stack(weights, stack):
    rows = weights.shape[0]
    parts = jnp.dot(pieces(weights), stack, preferred_element_type=f32)
    return parts[:rows] + parts[rows : 2 * rows] + parts[2 * rows :]


def dot_nt(left, right):
    return lax.dot_general(
        left, right, (((1,), (1,)), ((), ())), precision=highest, preferred_element_type=f32
    )


def dot_tn(left, right):
    return lax.dot_general(
        left, right, (((0,), (0,)), ((), ())), precision=highest, preferred_element_type=f32
    )


def dot_nn(left, right):
    return jnp.dot(left, right, precision=highest, preferred_element_type=f32)


def layout_kernel(slots_ref, tiles_ref, dense_ref):
    blocks, slots, edge = tiles_ref.shape[:3]
    many = dense_ref.shape[0] // edge
    dense_ref[...] = jnp.zeros_like(dense_ref)
    for b in range(blocks):
        for s in range(slots):

            @pl.when(slots_ref[b, s] < many)
            def _():
                start = pl.multiple_of(slots_ref[b, s] * edge, edge)
                dense_ref[pl.ds(start, edge), b * edge : (b + 1) * edge] = tiles_ref[b, s].T


def product(place_ref, dense_ref, mix_ref, stack, mine_refs):
    edge = mine_refs[0].shape[-1]
    mixed = dot_nn(mix_ref[...], jnp.dot(stack, dense_ref[...], preferred_element_type=f32))
    if len(mine_refs) == 2:
        first = place_ref[0] == 0
        low, high = mixed[:, :edge], mixed[:, edge:]
        mine_refs[0][...] = jnp.where(first, low, high)
        mine_refs[1][...] = jnp.where(first, high, low)
    else:
        for b in range(mine_refs[0].shape[0]):
            mine_refs[0][b] = mixed[:, b * edge : (b + 1) * edge]


def first_kernel(parts, place_ref, dense_ref, mix_ref, *refs):
    part_refs, stack_ref, mine_refs = refs[:parts], refs[parts], refs[parts + 1 :]
    edge = mine_refs[0].shape[-1]
    at = 0
    for ref in part_refs:
        for i in range(ref.shape[0]):
            stack_ref[:, at : at + edge] = ref[i]
            at += edge
    product(place_ref, dense_ref, mix_ref, stack_ref[...], mine_refs)


def next_kernel(nodes, place_ref, dense_ref, mix_ref, basis_ref, raw_ref, sqs, dirs_ref, stack_ref, *mine_refs):
    vecs = raw_ref.shape[0]
    square = sum(ref[...] for ref in sqs)[:, :1] / nodes
    scale = lax.rsqrt(square + epsilon)
    stack_ref[:vecs] = basis_ref[:vecs]
    stack_ref[vecs : 2 * vecs] = (raw_ref[...] * scale).astype(bf16)
    stack_ref[2 * vecs :] = dirs_ref[...]
    product(place_ref, dense_ref, mix_ref, stack_ref[...], mine_refs)


def gram_kernel(stack_ref, mix_ref, search_ref, pack_ref, search_out):
    wide = search_out.shape[1]
    vecs = mix_ref.shape[0]
    rotated = times_stack(mix_ref[...], stack_ref[...])
    search = times_stack(search_ref[...], stack_ref[vecs:])
    search_out[...] = search
    square = jnp.sum(search * search, axis=1, keepdims=True)
    pack_ref[...] = jnp.concatenate(
        [dot_nt(rotated, rotated), jnp.broadcast_to(square, (vecs, vecs))], axis=1
    )


def factor_kernel(nodes, packs, inverse_ref, scale_ref):
    vecs = inverse_ref.shape[0]
    total = sum(ref[...] for ref in packs) / nodes
    scale_ref[...] = jnp.broadcast_to(lax.rsqrt(total[:, vecs : vecs + 1] + epsilon), scale_ref.shape)
    row_ids = lax.broadcasted_iota(jnp.int32, (vecs, 2 * vecs), 0)
    lane_ids = lax.broadcasted_iota(jnp.int32, (vecs, 2 * vecs), 1)
    diagonal = jnp.where(lane_ids == row_ids, total, 0.0)
    down = lax.rsqrt(jnp.sum(diagonal, axis=1, keepdims=True))
    across = lax.rsqrt(jnp.sum(diagonal, axis=0, keepdims=True))
    work = jnp.where(lane_ids < vecs, total * down * across, jnp.where(lane_ids == row_ids + vecs, down, 0.0))
    height = 8
    tiles = [work[t : t + height] for t in range(0, vecs, height)]
    shape = tiles[0].shape
    ids = lax.broadcasted_iota(jnp.int32, shape, 0)
    for j in range(0, vecs, 2):
        t, s = divmod(j, height)
        top, under = tiles[t][s : s + 1], tiles[t][s + 1 : s + 2]
        columns = [
            [jnp.broadcast_to(tile[:, k : k + 1], shape) for k in (j, j + 1)] for tile in tiles[t:]
        ]
        a = columns[0][0][s : s + 1]
        b = columns[0][0][s + 1 : s + 2]
        c = columns[0][1][s + 1 : s + 2]
        determinant = 1.0 / (a * c - b * b)
        a, b, c = a * determinant, b * determinant, c * determinant
        for u in range(t, len(tiles)):
            if u == t and s == height - 2:
                continue
            x, y = columns[u - t]
            one, two = x * c - y * b, y * a - x * b
            if u == t:
                one, two = jnp.where(ids > s + 1, one, 0.0), jnp.where(ids > s + 1, two, 0.0)
            tiles[u] = tiles[u] - one * top - two * under
    work = jnp.concatenate(tiles, axis=0)
    above = jnp.concatenate([work[:1], work[:-1]], axis=0)
    odd = row_ids % 2 == 1
    pivots = jnp.sum(jnp.where(lane_ids == row_ids, work, 0.0), axis=1, keepdims=True)
    beside = jnp.sum(jnp.where(lane_ids == row_ids - 1, work, 0.0), axis=1, keepdims=True)
    firsts = jnp.concatenate([pivots[:1], pivots[:-1]], axis=0)
    ratio = jnp.where(odd[:, :1], beside / firsts, 0.0)
    inverse = (work - ratio * above) * lax.rsqrt(pivots - ratio * beside)
    inverse_ref[...] = inverse[:, vecs:]


def basis_kernel(inverse_ref, scale_ref, stack_ref, mix_ref, search_ref, basis_ref, dirs_ref, own_basis, own_dirs):
    wide = search_ref.shape[1]
    edge = own_basis.shape[1]
    dirs = search_ref[...] * scale_ref[:, :1]
    dirs_ref[...] = dirs.astype(bf16)
    own_dirs[...] = dirs[:, :edge]
    basis = times_stack(dot_nn(inverse_ref[...], mix_ref[...]), stack_ref[...])
    basis_ref[...] = pieces(basis)
    own_basis[...] = basis[:, :edge]


def solve_kernel(parts, *refs):
    part_refs, inverse_ref, blocks_ref, own_ref = refs[:parts], refs[parts], refs[parts + 1], refs[parts + 2]
    vecs, edge = own_ref.shape
    solved = dot_nn(inverse_ref[...], jnp.concatenate([ref[...] for ref in part_refs], axis=1))
    own_ref[...] = solved[:, :edge]
    for i in range(parts):
        blocks_ref[i * vecs : (i + 1) * vecs, :] = solved[:, i * edge : (i + 1) * edge].astype(bf16)


def cross_kernel(nodes, parts, *refs):
    part_refs, basis_ref, wide_ref, cross_ref = refs[:parts], refs[parts], refs[parts + 1], refs[parts + 2]
    vecs = wide_ref.shape[0]
    edge = part_refs[0].shape[1]
    at = 0
    for ref in part_refs:
        for i in range(ref.shape[0] // vecs):
            wide_ref[:, at : at + edge] = ref[i * vecs : (i + 1) * vecs, :]
            at += edge
    cross = lax.dot_general(
        basis_ref[...], wide_ref[...], (((1,), (1,)), ((), ())), preferred_element_type=f32
    )
    cross_ref[...] = (cross[:vecs] + cross[vecs : 2 * vecs] + cross[2 * vecs :]) / nodes


def residual_kernel(crosses, basis_ref, wide_ref, own_ref, raw_ref, square_ref, rayleigh_ref, own_raw):
    vecs = wide_ref.shape[0]
    edge = own_raw.shape[1]
    q = sum(ref[...] for ref in crosses)
    high = q.astype(bf16)
    low = (q - high.astype(f32)).astype(bf16)
    terms = jnp.concatenate([high, high, low], axis=0)
    basis = jnp.concatenate([basis_ref[: 2 * vecs], basis_ref[:vecs]], axis=0)
    part = lax.dot_general(terms, basis, (((0,), (0,)), ((), ())), preferred_element_type=f32)
    raw = part - wide_ref[...].astype(f32)
    raw_ref[...] = raw
    own_raw[...] = part[:, :edge] - own_ref[...]
    square_ref[...] = jnp.broadcast_to(jnp.sum(raw * raw, axis=1, keepdims=True), square_ref.shape)
    row_ids = lax.broadcasted_iota(jnp.int32, (vecs, vecs), 0)
    lane_ids = lax.broadcasted_iota(jnp.int32, (vecs, vecs), 1)
    rayleigh_ref[...] = jnp.where(row_ids == lane_ids, 1.0, 0.0) - q


def swap(value, by, axis):
    size = lax.axis_size(axis)
    return lax.ppermute(value, axis, [(i, i ^ by) for i in range(size)])


def panel_terms(value):
    if lax.axis_size("panel") == 2:
        return [value, swap(value, 1, "panel")]
    return [lax.psum(value, "panel")]


def far_values(value, near):
    far = lax.axis_size("rows") // near
    return [value] + [swap(value, near * i, "rows") for i in range(1, far)]


def near_values(held, near):
    return [held] + [swap(held, i, "rows") for i in range(1, near)]


def body(
    adj_tiles,
    row_counts,
    tile_cols,
    start_basis,
    start_resid,
    start_search,
    ritz_basis,
    ritz_search,
):
    tile_set = adj_tiles[0, 0]
    counts = row_counts[0, 0]
    columns = tile_cols[0, 0]
    blocks, slots, edge = tile_set.shape[:3]
    vecs = start_basis.shape[0]
    rows, panels = lax.axis_size("rows"), lax.axis_size("panel")
    nodes = start_basis.shape[1] * rows * panels
    wide = rows * edge
    near = 4
    away = columns ^ lax.axis_index("rows")
    position = (away % near) * (rows // near) + away // near
    in_use = jnp.arange(slots, dtype=jnp.int32)[None, :] < counts[:, None]
    slot_ids = jnp.where(in_use, position, rows).astype(jnp.int32)
    place = lax.axis_index("panel").astype(jnp.int32).reshape(1)

    if panels == 2:
        mine_outs = [((vecs, edge), f32)] * 2
    else:
        mine_outs = [((blocks, vecs, edge), f32)]
    stack_out = ((3 * vecs, wide), bf16)
    limit = 16 if wide <= 4096 else 56
    dense, = call(
        layout_kernel, [((wide, blocks * edge), bf16)], [slot_ids, tile_set], smem=(0,), limit=limit
    )

    start = jnp.concatenate([start_basis, start_resid, start_search], axis=0)[None]
    parts = near_values(jnp.concatenate(far_values(start, near), axis=0), near)
    parts, dense = lax.optimization_barrier((parts, dense))
    state = None
    sweeps = ritz_basis.shape[0]
    for sweep in range(sweeps):
        mixing = ritz_basis[sweep]
        if state is None:
            stack, *mine = call(
                functools.partial(first_kernel, near),
                [stack_out] + mine_outs,
                [place, dense, mixing] + parts,
                smem=(0,),
                limit=limit,
            )
        else:
            basis, raw, squares, dirs = state
            count = len(squares)

            def kernel(p, t, m, b, r, *refs):
                next_kernel(nodes, p, t, m, b, r, refs[:count], *refs[count:])

            stack, *mine = call(
                kernel,
                [stack_out] + mine_outs,
                [place, dense, mixing, basis, raw] + squares + [dirs],
                smem=(0,),
                limit=limit,
            )
        pack, search = call(
            gram_kernel,
            [((vecs, 2 * vecs), f32), ((vecs, wide), f32)],
            [stack, mixing, ritz_search[sweep]],
            limit=limit,
        )
        if panels == 2:
            other = swap(mine[1], 1, "panel")
            other, pack = lax.optimization_barrier((other, pack))
            rotated_adj = mine[0] + other
        else:
            rotated_adj = lax.psum_scatter(mine[0], "panel", scatter_dimension=0, tiled=True)[0]
        packs = panel_terms(pack)
        pack_count = len(packs)

        def kernel_factor(*refs):
            factor_kernel(nodes, refs[:pack_count], *refs[pack_count:])

        inverse, scale = call(
            kernel_factor, [((vecs, vecs), f32), ((vecs, 2 * vecs), f32)], packs
        )
        far_parts = far_values(rotated_adj, near)
        far_parts, inverse = lax.optimization_barrier((far_parts, inverse))
        held, own_adj = call(
            functools.partial(solve_kernel, len(far_parts)),
            [((len(far_parts) * vecs, edge), bf16), ((vecs, edge), f32)],
            far_parts + [inverse],
            limit=limit,
        )
        adj_parts = near_values(held, near)
        basis, dirs, own_basis, own_dirs = call(
            basis_kernel,
            [
                ((3 * vecs, wide), bf16),
                ((vecs, wide), bf16),
                ((vecs, edge), f32),
                ((vecs, edge), f32),
            ],
            [inverse, scale, stack, mixing, search],
            limit=limit,
        )
        wide_adj, cross = call(
            functools.partial(cross_kernel, nodes, near),
            [((vecs, wide), bf16), ((vecs, vecs), f32)],
            adj_parts + [basis],
            limit=limit,
        )
        crosses = panel_terms(cross)
        cross_count = len(crosses)

        def kernel_residual(*refs):
            residual_kernel(refs[:cross_count], *refs[cross_count:])

        raw, square, rayleigh, own_raw = call(
            kernel_residual,
            [((vecs, wide), f32), ((vecs, edge), f32), ((vecs, vecs), f32), ((vecs, edge), f32)],
            crosses + [basis, wide_adj, own_adj],
            limit=limit,
        )
        squares = panel_terms(square)
        state = (basis, raw, squares, dirs)
    resid = own_raw / jnp.sqrt(sum(squares) / nodes + epsilon)
    return (own_basis, resid, own_dirs, rayleigh)


def solution(mesh):
    return jax.shard_map(
        body,
        mesh=mesh,
        in_specs=(
            P("rows", "panel", None, None, None, None),
            P("rows", "panel", None),
            P("rows", "panel", None, None),
            P(None, ("rows", "panel")),
            P(None, ("rows", "panel")),
            P(None, ("rows", "panel")),
            P(),
            P(),
        ),
        out_specs=(
            P(None, ("rows", "panel")),
            P(None, ("rows", "panel")),
            P(None, ("rows", "panel")),
            P(),
        ),
        check_vma=False,
    )
```

```python
import functools

import jax
import jax.numpy as jnp
from jax import lax
from jax.experimental import pallas as pl
from jax.experimental.pallas import tpu as pltpu
from jax.sharding import PartitionSpec as P

epsilon = 1e-06
highest = lax.Precision.HIGHEST
f32 = jnp.float32
bf16 = jnp.bfloat16


def call(kernel, outs, args, smem=(), limit=16, scratch=()):
    specs = [
        pl.BlockSpec(memory_space=pltpu.SMEM if i in smem else pltpu.VMEM) for i in range(len(args))
    ]
    return pl.pallas_call(
        kernel,
        out_shape=[jax.ShapeDtypeStruct(shape, kind) for shape, kind in outs],
        in_specs=specs,
        out_specs=[pl.BlockSpec(memory_space=pltpu.VMEM) for _ in outs],
        scratch_shapes=[pltpu.VMEM(shape, kind) for shape, kind in scratch],
        compiler_params=pltpu.CompilerParams(vmem_limit_bytes=limit << 20),
    )(*args)


def pieces(value):
    high = value.astype(bf16)
    rest = value - high.astype(f32)
    middle = rest.astype(bf16)
    low = (rest - middle.astype(f32)).astype(bf16)
    return jnp.concatenate([high, middle, low], axis=0)


def times_stack(weights, stack):
    rows = weights.shape[0]
    parts = jnp.dot(pieces(weights), stack, preferred_element_type=f32)
    return parts[:rows] + parts[rows : 2 * rows] + parts[2 * rows :]


def dot_nt(left, right):
    return lax.dot_general(
        left, right, (((1,), (1,)), ((), ())), precision=highest, preferred_element_type=f32
    )


def dot_tn(left, right):
    return lax.dot_general(
        left, right, (((0,), (0,)), ((), ())), precision=highest, preferred_element_type=f32
    )


def dot_nn(left, right):
    return jnp.dot(left, right, precision=highest, preferred_element_type=f32)


def layout_kernel(slots_ref, tiles_ref, dense_ref):
    blocks, slots, edge = tiles_ref.shape[:3]
    many = dense_ref.shape[0] // edge
    dense_ref[...] = jnp.zeros_like(dense_ref)
    for b in range(blocks):
        for s in range(slots):

            @pl.when(slots_ref[b, s] < many)
            def _():
                start = pl.multiple_of(slots_ref[b, s] * edge, edge)
                dense_ref[pl.ds(start, edge), b * edge : (b + 1) * edge] = tiles_ref[b, s].T


def product(place_ref, dense_ref, mix_ref, stack, mine_refs):
    edge = mine_refs[0].shape[-1]
    mixed = dot_nn(mix_ref[...], jnp.dot(stack, dense_ref[...], preferred_element_type=f32))
    if len(mine_refs) == 2:
        first = place_ref[0] == 0
        low, high = mixed[:, :edge], mixed[:, edge:]
        mine_refs[0][...] = jnp.where(first, low, high)
        mine_refs[1][...] = jnp.where(first, high, low)
    else:
        for b in range(mine_refs[0].shape[0]):
            mine_refs[0][b] = mixed[:, b * edge : (b + 1) * edge]


def first_kernel(parts, place_ref, dense_ref, mix_ref, *refs):
    part_refs, stack_ref, mine_refs = refs[:parts], refs[parts], refs[parts + 1 :]
    edge = mine_refs[0].shape[-1]
    at = 0
    for ref in part_refs:
        for i in range(ref.shape[0]):
            stack_ref[:, at : at + edge] = ref[i]
            at += edge
    product(place_ref, dense_ref, mix_ref, stack_ref[...], mine_refs)


def residual_terms(crosses, gram_ref):
    both = sum(ref[...] for ref in crosses)
    vecs = both.shape[0]
    q = both[:, :vecs]
    taken = q * (2.0 * q - dot_nn(gram_ref[...], q))
    square = both[:, vecs : vecs + 1] - jnp.sum(taken.T, axis=1, keepdims=True)
    return q, lax.rsqrt(jnp.maximum(square, 0.0) + epsilon)


def next_kernel(place_ref, dense_ref, mix_ref, crosses, gram_ref, basis_ref, wide_ref, dirs_ref, stack_ref, *mine_refs):
    vecs = wide_ref.shape[0]
    q, scale = residual_terms(crosses, gram_ref)
    high = q.astype(bf16)
    low = (q - high.astype(f32)).astype(bf16)
    terms = jnp.concatenate([high, high, low], axis=0)
    basis = jnp.concatenate([basis_ref[: 2 * vecs], basis_ref[:vecs]], axis=0)
    part = lax.dot_general(terms, basis, (((0,), (0,)), ((), ())), preferred_element_type=f32)
    stack_ref[:vecs] = basis_ref[:vecs]
    stack_ref[vecs : 2 * vecs] = ((part - wide_ref[...].astype(f32)) * scale).astype(bf16)
    stack_ref[2 * vecs :] = dirs_ref[...]
    product(place_ref, dense_ref, mix_ref, stack_ref[...], mine_refs)


def last_kernel(crosses, gram_ref, basis_ref, own_ref, resid_ref, rayleigh_ref):
    vecs = own_ref.shape[0]
    q, scale = residual_terms(crosses, gram_ref)
    resid_ref[...] = (dot_tn(q, basis_ref[...]) - own_ref[...]) * scale
    row_ids = lax.broadcasted_iota(jnp.int32, (vecs, vecs), 0)
    lane_ids = lax.broadcasted_iota(jnp.int32, (vecs, vecs), 1)
    rayleigh_ref[...] = jnp.where(row_ids == lane_ids, 1.0, 0.0) - q


def gram_kernel(stack_ref, mix_ref, search_ref, pack_ref, search_out):
    wide = search_out.shape[1]
    vecs = mix_ref.shape[0]
    rotated = times_stack(mix_ref[...], stack_ref[...])
    search = times_stack(search_ref[...], stack_ref[vecs:])
    search_out[...] = search
    square = jnp.sum(search * search, axis=1, keepdims=True)
    pack_ref[...] = jnp.concatenate(
        [dot_nt(rotated, rotated), jnp.broadcast_to(square, (vecs, vecs))], axis=1
    )


def factor_kernel(nodes, packs, inverse_ref, scale_ref):
    vecs = inverse_ref.shape[0]
    total = sum(ref[...] for ref in packs) / nodes
    scale_ref[...] = jnp.broadcast_to(lax.rsqrt(total[:, vecs : vecs + 1] + epsilon), scale_ref.shape)
    row_ids = lax.broadcasted_iota(jnp.int32, (vecs, 2 * vecs), 0)
    lane_ids = lax.broadcasted_iota(jnp.int32, (vecs, 2 * vecs), 1)
    diagonal = jnp.where(lane_ids == row_ids, total, 0.0)
    down = lax.rsqrt(jnp.sum(diagonal, axis=1, keepdims=True))
    across = lax.rsqrt(jnp.sum(diagonal, axis=0, keepdims=True))
    work = jnp.where(lane_ids < vecs, total * down * across, jnp.where(lane_ids == row_ids + vecs, down, 0.0))
    height = 8
    tiles = [work[t : t + height] for t in range(0, vecs, height)]
    shape = tiles[0].shape
    ids = lax.broadcasted_iota(jnp.int32, shape, 0)
    for j in range(0, vecs, 2):
        t, s = divmod(j, height)
        top, under = tiles[t][s : s + 1], tiles[t][s + 1 : s + 2]
        columns = [
            [jnp.broadcast_to(tile[:, k : k + 1], shape) for k in (j, j + 1)] for tile in tiles[t:]
        ]
        a = columns[0][0][s : s + 1]
        b = columns[0][0][s + 1 : s + 2]
        c = columns[0][1][s + 1 : s + 2]
        determinant = 1.0 / (a * c - b * b)
        a, b, c = a * determinant, b * determinant, c * determinant
        for u in range(t, len(tiles)):
            if u == t and s == height - 2:
                continue
            x, y = columns[u - t]
            one, two = x * c - y * b, y * a - x * b
            if u == t:
                one, two = jnp.where(ids > s + 1, one, 0.0), jnp.where(ids > s + 1, two, 0.0)
            tiles[u] = tiles[u] - one * top - two * under
    work = jnp.concatenate(tiles, axis=0)
    above = jnp.concatenate([work[:1], work[:-1]], axis=0)
    odd = row_ids % 2 == 1
    pivots = jnp.sum(jnp.where(lane_ids == row_ids, work, 0.0), axis=1, keepdims=True)
    beside = jnp.sum(jnp.where(lane_ids == row_ids - 1, work, 0.0), axis=1, keepdims=True)
    firsts = jnp.concatenate([pivots[:1], pivots[:-1]], axis=0)
    ratio = jnp.where(odd[:, :1], beside / firsts, 0.0)
    inverse = (work - ratio * above) * lax.rsqrt(pivots - ratio * beside)
    inverse_ref[...] = inverse[:, vecs:]


def basis_kernel(nodes, packs, inverse_ref, scale_ref, stack_ref, mix_ref, search_ref, basis_ref, gram_ref, dirs_ref, *own_basis):
    vecs = mix_ref.shape[0]
    inverse = inverse_ref[...]
    total = sum(ref[...] for ref in packs)[:, :vecs] / nodes
    gram_ref[...] = dot_nt(dot_nn(inverse, total), inverse)
    edge = dirs_ref.shape[1]
    dirs_ref[...] = (search_ref[:, :edge] * scale_ref[:, :1]).astype(dirs_ref.dtype)
    basis = times_stack(dot_nn(inverse, mix_ref[...]), stack_ref[...])
    basis_ref[...] = pieces(basis)
    if own_basis:
        own_basis[0][...] = basis[:, :edge]


def solve_kernel(parts, *refs):
    part_refs, inverse_ref, blocks_ref, own_ref = refs[:parts], refs[parts], refs[parts + 1], refs[parts + 2 :]
    vecs, edge = part_refs[0].shape
    solved = dot_nn(inverse_ref[...], jnp.concatenate([ref[...] for ref in part_refs], axis=1))
    if own_ref:
        own_ref[0][...] = solved[:, :edge]
    for i in range(parts):
        blocks_ref[i * vecs : (i + 1) * vecs, :] = solved[:, i * edge : (i + 1) * edge].astype(bf16)


def cross_kernel(nodes, parts, *refs):
    part_refs, basis_ref, cross_ref, wide_ref = refs[:parts], refs[parts], refs[parts + 1], refs[parts + 2]
    vecs = wide_ref.shape[0]
    edge = part_refs[0].shape[1]
    at = 0
    for ref in part_refs:
        for i in range(ref.shape[0] // vecs):
            wide_ref[:, at : at + edge] = ref[i * vecs : (i + 1) * vecs, :]
            at += edge
    cross = lax.dot_general(
        basis_ref[...], wide_ref[...], (((1,), (1,)), ((), ())), preferred_element_type=f32
    )
    cross = cross[:vecs] + cross[vecs : 2 * vecs] + cross[2 * vecs :]
    values = wide_ref[...].astype(f32)
    square = jnp.sum(values * values, axis=1, keepdims=True)
    cross_ref[...] = jnp.concatenate([cross, jnp.broadcast_to(square, cross.shape)], axis=1) / nodes


def swap(value, by, axis):
    size = lax.axis_size(axis)
    return lax.ppermute(value, axis, [(i, i ^ by) for i in range(size)])


def panel_terms(value):
    if lax.axis_size("panel") == 2:
        return [value, swap(value, 1, "panel")]
    return [lax.psum(value, "panel")]


def far_values(value, near):
    far = lax.axis_size("rows") // near
    return [value] + [swap(value, near * i, "rows") for i in range(1, far)]


def near_values(held, near):
    return [held] + [swap(held, i, "rows") for i in range(1, near)]


def body(
    adj_tiles,
    row_counts,
    tile_cols,
    start_basis,
    start_resid,
    start_search,
    ritz_basis,
    ritz_search,
):
    tile_set = adj_tiles[0, 0]
    counts = row_counts[0, 0]
    columns = tile_cols[0, 0]
    blocks, slots, edge = tile_set.shape[:3]
    vecs = start_basis.shape[0]
    rows, panels = lax.axis_size("rows"), lax.axis_size("panel")
    nodes = start_basis.shape[1] * rows * panels
    wide = rows * edge
    near = 4
    away = columns ^ lax.axis_index("rows")
    position = (away % near) * (rows // near) + away // near
    in_use = jnp.arange(slots, dtype=jnp.int32)[None, :] < counts[:, None]
    slot_ids = jnp.where(in_use, position, rows).astype(jnp.int32)
    place = lax.axis_index("panel").astype(jnp.int32).reshape(1)

    if panels == 2:
        mine_outs = [((vecs, edge), f32)] * 2
    else:
        mine_outs = [((blocks, vecs, edge), f32)]
    stack_out = ((3 * vecs, wide), bf16)
    limit = 16 if wide <= 4096 else 56
    dense, = call(
        layout_kernel, [((wide, blocks * edge), bf16)], [slot_ids, tile_set], smem=(0,), limit=limit
    )

    start = jnp.concatenate([start_basis, start_resid, start_search], axis=0)[None]
    parts = near_values(jnp.concatenate(far_values(start, near), axis=0), near)
    parts, dense = lax.optimization_barrier((parts, dense))
    state = None
    sweeps = ritz_basis.shape[0]
    for sweep in range(sweeps):
        last = sweep == sweeps - 1
        mixing = ritz_basis[sweep]
        if state is None:
            stack, *mine = call(
                functools.partial(first_kernel, near),
                [stack_out] + mine_outs,
                [place, dense, mixing] + parts,
                smem=(0,),
                limit=limit,
            )
        else:
            crosses, gram, basis, wide_adj, dirs = state
            count = len(crosses)

            def kernel(p, t, m, *refs):
                next_kernel(p, t, m, refs[:count], *refs[count:])

            stack, *mine = call(
                kernel,
                [stack_out] + mine_outs,
                [place, dense, mixing] + crosses + [gram, basis] + wide_adj + [dirs],
                smem=(0,),
                limit=limit,
            )
        pack, search = call(
            gram_kernel,
            [((vecs, 2 * vecs), f32), ((vecs, wide), f32)],
            [stack, mixing, ritz_search[sweep]],
            limit=limit,
        )
        if panels == 2:
            other = swap(mine[1], 1, "panel")
            other, pack = lax.optimization_barrier((other, pack))
            rotated_adj = mine[0] + other
        else:
            rotated_adj = lax.psum_scatter(mine[0], "panel", scatter_dimension=0, tiled=True)[0]
        packs = panel_terms(pack)
        pack_count = len(packs)

        def kernel_factor(*refs):
            factor_kernel(nodes, refs[:pack_count], *refs[pack_count:])

        inverse, scale = call(
            kernel_factor, [((vecs, vecs), f32), ((vecs, 2 * vecs), f32)], packs
        )
        far_parts = far_values(rotated_adj, near)
        far_parts, inverse = lax.optimization_barrier((far_parts, inverse))
        held, *own_adj = call(
            functools.partial(solve_kernel, len(far_parts)),
            [((len(far_parts) * vecs, edge), bf16)] + [((vecs, edge), f32)] * last,
            far_parts + [inverse],
            limit=limit,
        )
        adj_parts = near_values(held, near)

        def kernel_basis(*refs):
            basis_kernel(nodes, refs[:pack_count], *refs[pack_count:])

        basis, gram, dirs, *own_basis = call(
            kernel_basis,
            [
                ((3 * vecs, wide), bf16),
                ((vecs, vecs), f32),
                ((vecs, edge), f32) if last else ((vecs, wide), bf16),
            ]
            + [((vecs, edge), f32)] * last,
            packs + [inverse, scale, stack, mixing, search],
            limit=limit,
        )
        wide_out = [((vecs, wide), bf16)]
        cross, *wide_adj = call(
            functools.partial(cross_kernel, nodes, near),
            [((vecs, 2 * vecs), f32)] + ([] if last else wide_out),
            adj_parts + [basis],
            limit=limit,
            scratch=wide_out if last else [],
        )
        crosses = panel_terms(cross)
        state = (crosses, gram, basis, wide_adj, dirs)
    count = len(crosses)

    def kernel_last(*refs):
        last_kernel(refs[:count], *refs[count:])

    resid, rayleigh = call(
        kernel_last,
        [((vecs, edge), f32), ((vecs, vecs), f32)],
        crosses + [gram] + own_basis + own_adj,
    )
    return (own_basis[0], resid, dirs, rayleigh)


def solution(mesh):
    return jax.shard_map(
        body,
        mesh=mesh,
        in_specs=(
            P("rows", "panel", None, None, None, None),
            P("rows", "panel", None),
            P("rows", "panel", None, None),
            P(None, ("rows", "panel")),
            P(None, ("rows", "panel")),
            P(None, ("rows", "panel")),
            P(),
            P(),
        ),
        out_specs=(
            P(None, ("rows", "panel")),
            P(None, ("rows", "panel")),
            P(None, ("rows", "panel")),
            P(),
        ),
        check_vma=False,
    )
```

```python
import functools

import jax
import jax.numpy as jnp
from jax import lax
from jax.experimental import pallas as pl
from jax.experimental.pallas import tpu as pltpu
from jax.sharding import PartitionSpec as P

epsilon = 1e-06
highest = lax.Precision.HIGHEST
f32 = jnp.float32
bf16 = jnp.bfloat16


def call(kernel, outs, args, smem=(), limit=16, scratch=()):
    specs = [
        pl.BlockSpec(memory_space=pltpu.SMEM if i in smem else pltpu.VMEM) for i in range(len(args))
    ]
    return pl.pallas_call(
        kernel,
        out_shape=[jax.ShapeDtypeStruct(shape, kind) for shape, kind in outs],
        in_specs=specs,
        out_specs=[pl.BlockSpec(memory_space=pltpu.VMEM) for _ in outs],
        scratch_shapes=[pltpu.VMEM(shape, kind) for shape, kind in scratch],
        compiler_params=pltpu.CompilerParams(vmem_limit_bytes=limit << 20),
    )(*args)


def pieces(value):
    high = value.astype(bf16)
    rest = value - high.astype(f32)
    middle = rest.astype(bf16)
    low = (rest - middle.astype(f32)).astype(bf16)
    return jnp.concatenate([high, middle, low], axis=0)


def times_stack(weights, stack):
    rows = weights.shape[0]
    parts = jnp.dot(pieces(weights), stack, preferred_element_type=f32)
    return parts[:rows] + parts[rows : 2 * rows] + parts[2 * rows :]


def dot_nt(left, right):
    return lax.dot_general(
        left, right, (((1,), (1,)), ((), ())), precision=highest, preferred_element_type=f32
    )


def dot_tn(left, right):
    return lax.dot_general(
        left, right, (((0,), (0,)), ((), ())), precision=highest, preferred_element_type=f32
    )


def dot_nn(left, right):
    return jnp.dot(left, right, precision=highest, preferred_element_type=f32)


def layout_kernel(slots_ref, tiles_ref, dense_ref):
    blocks, slots, edge = tiles_ref.shape[:3]
    many = dense_ref.shape[0] // edge
    dense_ref[...] = jnp.zeros_like(dense_ref)
    for b in range(blocks):
        for s in range(slots):

            @pl.when(slots_ref[b, s] < many)
            def _():
                start = pl.multiple_of(slots_ref[b, s] * edge, edge)
                dense_ref[pl.ds(start, edge), b * edge : (b + 1) * edge] = tiles_ref[b, s].T


def product(place_ref, dense_ref, mix_ref, stack, mine_refs):
    edge = mine_refs[0].shape[-1]
    mixed = dot_nn(mix_ref[...], jnp.dot(stack, dense_ref[...], preferred_element_type=f32))
    if len(mine_refs) == 2:
        first = place_ref[0] == 0
        low, high = mixed[:, :edge], mixed[:, edge:]
        mine_refs[0][...] = jnp.where(first, low, high)
        mine_refs[1][...] = jnp.where(first, high, low)
    else:
        for b in range(mine_refs[0].shape[0]):
            mine_refs[0][b] = mixed[:, b * edge : (b + 1) * edge]


def first_kernel(parts, place_ref, dense_ref, mix_ref, *refs):
    part_refs, stack_ref, mine_refs = refs[:parts], refs[parts], refs[parts + 1 :]
    edge = mine_refs[0].shape[-1]
    at = 0
    for ref in part_refs:
        for i in range(ref.shape[0]):
            stack_ref[:, at : at + edge] = ref[i]
            at += edge
    product(place_ref, dense_ref, mix_ref, stack_ref[...], mine_refs)


def residual_terms(crosses, gram_ref):
    both = sum(ref[...] for ref in crosses)
    vecs = both.shape[0]
    q = both[:, :vecs]
    taken = q * (2.0 * q - dot_nn(gram_ref[...], q))
    square = both[:, vecs : vecs + 1] - jnp.sum(taken.T, axis=1, keepdims=True)
    return q, lax.rsqrt(jnp.maximum(square, 0.0) + epsilon)


def next_kernel(place_ref, dense_ref, mix_ref, crosses, gram_ref, basis_ref, wide_ref, dirs_ref, stack_ref, *mine_refs):
    vecs = wide_ref.shape[0]
    q, scale = residual_terms(crosses, gram_ref)
    high = q.astype(bf16)
    low = (q - high.astype(f32)).astype(bf16)
    terms = jnp.concatenate([high, high, low], axis=0)
    basis = jnp.concatenate([basis_ref[: 2 * vecs], basis_ref[:vecs]], axis=0)
    part = lax.dot_general(terms, basis, (((0,), (0,)), ((), ())), preferred_element_type=f32)
    stack_ref[:vecs] = basis_ref[:vecs]
    stack_ref[vecs : 2 * vecs] = ((part - wide_ref[...].astype(f32)) * scale).astype(bf16)
    stack_ref[2 * vecs :] = dirs_ref[...]
    product(place_ref, dense_ref, mix_ref, stack_ref[...], mine_refs)


def last_kernel(crosses, gram_ref, basis_ref, own_ref, resid_ref, rayleigh_ref):
    vecs = own_ref.shape[0]
    q, scale = residual_terms(crosses, gram_ref)
    resid_ref[...] = (dot_tn(q, basis_ref[...]) - own_ref[...]) * scale
    row_ids = lax.broadcasted_iota(jnp.int32, (vecs, vecs), 0)
    lane_ids = lax.broadcasted_iota(jnp.int32, (vecs, vecs), 1)
    rayleigh_ref[...] = jnp.where(row_ids == lane_ids, 1.0, 0.0) - q


def gram_kernel(stack_ref, mix_ref, search_ref, pack_ref, search_out):
    wide = search_out.shape[1]
    vecs = mix_ref.shape[0]
    rotated = times_stack(mix_ref[...], stack_ref[...])
    search = times_stack(search_ref[...], stack_ref[vecs:])
    search_out[...] = search
    square = jnp.sum(search * search, axis=1, keepdims=True)
    pack_ref[...] = jnp.concatenate(
        [dot_nt(rotated, rotated), jnp.broadcast_to(square, (vecs, vecs))], axis=1
    )


def factor_kernel(nodes, packs, inverse_ref, scale_ref):
    vecs = inverse_ref.shape[0]
    total = sum(ref[...] for ref in packs) / nodes
    scale_ref[...] = lax.rsqrt(jnp.maximum(total, 0.0) + epsilon)
    row_ids = lax.broadcasted_iota(jnp.int32, (vecs, 2 * vecs), 0)
    lane_ids = lax.broadcasted_iota(jnp.int32, (vecs, 2 * vecs), 1)
    diagonal = jnp.where(lane_ids == row_ids, total, 0.0)
    across = lax.rsqrt(jnp.sum(diagonal, axis=0, keepdims=True))
    height, step = 8, 4
    shape = (height, 2 * vecs)
    ids = lax.broadcasted_iota(jnp.int32, shape, 0)
    lanes = lax.broadcasted_iota(jnp.int32, shape, 1)

    def lane(tile, index):
        return jnp.take_along_axis(tile, index, axis=1)

    tiles = []
    for t in range(0, vecs, height):
        tile = total[t : t + height]
        down = lax.rsqrt(lane(tile, ids + t))
        unit = jnp.where(lanes == ids + (t + vecs), down, 0.0)
        tiles.append(jnp.where(lanes < vecs, tile * down * across, unit))
    done = [None] * len(tiles)
    for j in range(0, vecs, step):
        t, s = divmod(j, height)
        rows = [jnp.broadcast_to(tiles[t][s + m : s + m + 1], shape) for m in range(step)]
        columns = [
            [lane(tile, jnp.full(shape, k, jnp.int32)) for k in range(j, j + step)] for tile in tiles[t:]
        ]

        def pivot(m, n):
            return jnp.broadcast_to(columns[0][n][s + m : s + m + 1], shape)

        p00, p10, p11 = pivot(0, 0), pivot(1, 0), pivot(1, 1)
        q20, q21, q30, q31 = pivot(2, 0), pivot(2, 1), pivot(3, 0), pivot(3, 1)
        w22, w32, w33 = pivot(2, 2), pivot(3, 2), pivot(3, 3)
        scale = 1.0 / (p00 * p11 - p10 * p10)
        i00, i10, i11 = p11 * scale, -p10 * scale, p00 * scale
        e20, e21 = q20 * i00 + q21 * i10, q20 * i10 + q21 * i11
        e30, e31 = q30 * i00 + q31 * i10, q30 * i10 + q31 * i11
        s22 = w22 - (e20 * q20 + e21 * q21)
        s32 = w32 - (e30 * q20 + e31 * q21)
        s33 = w33 - (e30 * q30 + e31 * q31)
        scale = 1.0 / (s22 * s33 - s32 * s32)
        u22, u32, u33 = s33 * scale, -s32 * scale, s22 * scale
        below2 = rows[2] - (e20 * rows[0] + e21 * rows[1])
        below3 = rows[3] - (e30 * rows[0] + e31 * rows[1])
        y2, y3 = below2 * u22 + below3 * u32, below2 * u32 + below3 * u33
        z0 = rows[0] - (y2 * q20 + y3 * q30)
        z1 = rows[1] - (y2 * q21 + y3 * q31)
        y0, y1 = z0 * i00 + z1 * i10, z0 * i10 + z1 * i11
        for u in range(t, len(tiles)):
            if u == t and s + step == height:
                continue
            x0, x1, x2, x3 = columns[u - t]
            less = (x0 * y0 + x1 * y1) + (x2 * y2 + x3 * y3)
            if u == t:
                less = jnp.where(ids >= s + step, less, 0.0)
            tiles[u] = tiles[u] - less
        ratio = p10 / p00
        finished = [rows[0], rows[1] - ratio * rows[0], below2, below3 - (s32 / s22) * below2]
        roots = [p00, p11 - ratio * p10, s22, s33 - (s32 / s22) * s32]
        for m in range(step):
            value = finished[m] * lax.rsqrt(roots[m])
            done[t] = value if done[t] is None else jnp.where(ids >= s + m, value, done[t])
    inverse_ref[...] = jnp.concatenate(done, axis=0)[:, vecs:]


def basis_kernel(nodes, packs, inverse_ref, scale_ref, stack_ref, mix_ref, search_ref, basis_ref, gram_ref, dirs_ref, *own_basis):
    vecs = mix_ref.shape[0]
    inverse = inverse_ref[...]
    total = sum(ref[...] for ref in packs)[:, :vecs] / nodes
    gram_ref[...] = dot_nt(dot_nn(inverse, total), inverse)
    edge = dirs_ref.shape[1]
    dirs_ref[...] = (search_ref[:, :edge] * scale_ref[:, vecs : vecs + 1]).astype(dirs_ref.dtype)
    basis = times_stack(dot_nn(inverse, mix_ref[...]), stack_ref[...])
    basis_ref[...] = pieces(basis)
    if own_basis:
        own_basis[0][...] = basis[:, :edge]


def solve_kernel(parts, *refs):
    part_refs, inverse_ref, blocks_ref, own_ref = refs[:parts], refs[parts], refs[parts + 1], refs[parts + 2 :]
    vecs, edge = part_refs[0].shape
    solved = dot_nn(inverse_ref[...], jnp.concatenate([ref[...] for ref in part_refs], axis=1))
    if own_ref:
        own_ref[0][...] = solved[:, :edge]
    for i in range(parts):
        blocks_ref[i * vecs : (i + 1) * vecs, :] = solved[:, i * edge : (i + 1) * edge].astype(bf16)


def cross_kernel(nodes, parts, *refs):
    part_refs, basis_ref, cross_ref, wide_ref = refs[:parts], refs[parts], refs[parts + 1], refs[parts + 2]
    vecs = wide_ref.shape[0]
    edge = part_refs[0].shape[1]
    at = 0
    for ref in part_refs:
        for i in range(ref.shape[0] // vecs):
            wide_ref[:, at : at + edge] = ref[i * vecs : (i + 1) * vecs, :]
            at += edge
    cross = lax.dot_general(
        basis_ref[...], wide_ref[...], (((1,), (1,)), ((), ())), preferred_element_type=f32
    )
    cross = cross[:vecs] + cross[vecs : 2 * vecs] + cross[2 * vecs :]
    values = wide_ref[...].astype(f32)
    square = jnp.sum(values * values, axis=1, keepdims=True)
    cross_ref[...] = jnp.concatenate([cross, jnp.broadcast_to(square, cross.shape)], axis=1) / nodes


def swap(value, by, axis):
    size = lax.axis_size(axis)
    return lax.ppermute(value, axis, [(i, i ^ by) for i in range(size)])


def panel_terms(value):
    if lax.axis_size("panel") == 2:
        return [value, swap(value, 1, "panel")]
    return [lax.psum(value, "panel")]


def far_values(value, near):
    far = lax.axis_size("rows") // near
    return [value] + [swap(value, near * i, "rows") for i in range(1, far)]


def near_values(held, near):
    return [held] + [swap(held, i, "rows") for i in range(1, near)]


def body(
    adj_tiles,
    row_counts,
    tile_cols,
    start_basis,
    start_resid,
    start_search,
    ritz_basis,
    ritz_search,
):
    tile_set = adj_tiles[0, 0]
    counts = row_counts[0, 0]
    columns = tile_cols[0, 0]
    blocks, slots, edge = tile_set.shape[:3]
    vecs = start_basis.shape[0]
    rows, panels = lax.axis_size("rows"), lax.axis_size("panel")
    nodes = start_basis.shape[1] * rows * panels
    wide = rows * edge
    near = 4
    away = columns ^ lax.axis_index("rows")
    position = (away % near) * (rows // near) + away // near
    in_use = jnp.arange(slots, dtype=jnp.int32)[None, :] < counts[:, None]
    slot_ids = jnp.where(in_use, position, rows).astype(jnp.int32)
    place = lax.axis_index("panel").astype(jnp.int32).reshape(1)

    if panels == 2:
        mine_outs = [((vecs, edge), f32)] * 2
    else:
        mine_outs = [((blocks, vecs, edge), f32)]
    stack_out = ((3 * vecs, wide), bf16)
    limit = 16 if wide <= 4096 else 56
    dense, = call(
        layout_kernel, [((wide, blocks * edge), bf16)], [slot_ids, tile_set], smem=(0,), limit=limit
    )

    start = jnp.concatenate([start_basis, start_resid, start_search], axis=0)[None]
    parts = near_values(jnp.concatenate(far_values(start, near), axis=0), near)
    parts, dense = lax.optimization_barrier((parts, dense))
    state = None
    sweeps = ritz_basis.shape[0]
    for sweep in range(sweeps):
        last = sweep == sweeps - 1
        mixing = ritz_basis[sweep]
        if state is None:
            stack, *mine = call(
                functools.partial(first_kernel, near),
                [stack_out] + mine_outs,
                [place, dense, mixing] + parts,
                smem=(0,),
                limit=limit,
            )
        else:
            crosses, gram, basis, wide_adj, dirs = state
            count = len(crosses)

            def kernel(p, t, m, *refs):
                next_kernel(p, t, m, refs[:count], *refs[count:])

            stack, *mine = call(
                kernel,
                [stack_out] + mine_outs,
                [place, dense, mixing] + crosses + [gram, basis] + wide_adj + [dirs],
                smem=(0,),
                limit=limit,
            )
        pack, search = call(
            gram_kernel,
            [((vecs, 2 * vecs), f32), ((vecs, wide), f32)],
            [stack, mixing, ritz_search[sweep]],
            limit=limit,
        )
        if panels == 2:
            other = swap(mine[1], 1, "panel")
            other, pack = lax.optimization_barrier((other, pack))
            rotated_adj = mine[0] + other
        else:
            rotated_adj = lax.psum_scatter(mine[0], "panel", scatter_dimension=0, tiled=True)[0]
        packs = panel_terms(pack)
        pack_count = len(packs)

        def kernel_factor(*refs):
            factor_kernel(nodes, refs[:pack_count], *refs[pack_count:])

        inverse, scale = call(
            kernel_factor, [((vecs, vecs), f32), ((vecs, 2 * vecs), f32)], packs
        )
        far_parts = far_values(rotated_adj, near)
        far_parts, inverse = lax.optimization_barrier((far_parts, inverse))
        held, *own_adj = call(
            functools.partial(solve_kernel, len(far_parts)),
            [((len(far_parts) * vecs, edge), bf16)] + [((vecs, edge), f32)] * last,
            far_parts + [inverse],
            limit=limit,
        )
        adj_parts = near_values(held, near)

        def kernel_basis(*refs):
            basis_kernel(nodes, refs[:pack_count], *refs[pack_count:])

        basis, gram, dirs, *own_basis = call(
            kernel_basis,
            [
                ((3 * vecs, wide), bf16),
                ((vecs, vecs), f32),
                ((vecs, edge), f32) if last else ((vecs, wide), bf16),
            ]
            + [((vecs, edge), f32)] * last,
            packs + [inverse, scale, stack, mixing, search],
            limit=limit,
        )
        wide_out = [((vecs, wide), bf16)]
        cross, *wide_adj = call(
            functools.partial(cross_kernel, nodes, near),
            [((vecs, 2 * vecs), f32)] + ([] if last else wide_out),
            adj_parts + [basis],
            limit=limit,
            scratch=wide_out if last else [],
        )
        crosses = panel_terms(cross)
        state = (crosses, gram, basis, wide_adj, dirs)
    count = len(crosses)

    def kernel_last(*refs):
        last_kernel(refs[:count], *refs[count:])

    resid, rayleigh = call(
        kernel_last,
        [((vecs, edge), f32), ((vecs, vecs), f32)],
        crosses + [gram] + own_basis + own_adj,
    )
    return (own_basis[0], resid, dirs, rayleigh)


def solution(mesh):
    return jax.shard_map(
        body,
        mesh=mesh,
        in_specs=(
            P("rows", "panel", None, None, None, None),
            P("rows", "panel", None),
            P("rows", "panel", None, None),
            P(None, ("rows", "panel")),
            P(None, ("rows", "panel")),
            P(None, ("rows", "panel")),
            P(),
            P(),
        ),
        out_specs=(
            P(None, ("rows", "panel")),
            P(None, ("rows", "panel")),
            P(None, ("rows", "panel")),
            P(),
        ),
        check_vma=False,
    )
```

```python
import functools

import jax
import jax.numpy as jnp
from jax import lax
from jax.experimental import pallas as pl
from jax.experimental.pallas import tpu as pltpu
from jax.sharding import PartitionSpec as P

epsilon = 1e-06
highest = lax.Precision.HIGHEST
f32 = jnp.float32
bf16 = jnp.bfloat16


def call(kernel, outs, args, smem=(), limit=16):
    specs = [
        pl.BlockSpec(memory_space=pltpu.SMEM if i in smem else pltpu.VMEM) for i in range(len(args))
    ]
    return pl.pallas_call(
        kernel,
        out_shape=[jax.ShapeDtypeStruct(shape, kind) for shape, kind in outs],
        in_specs=specs,
        out_specs=[pl.BlockSpec(memory_space=pltpu.VMEM) for _ in outs],
        compiler_params=pltpu.CompilerParams(vmem_limit_bytes=limit << 20),
    )(*args)


def pieces(value):
    high = value.astype(bf16)
    rest = value - high.astype(f32)
    middle = rest.astype(bf16)
    low = (rest - middle.astype(f32)).astype(bf16)
    return jnp.concatenate([high, middle, low], axis=0)


def halves(value):
    high = value.astype(bf16)
    return high, (value - high.astype(f32)).astype(bf16)


def times_stack(weights, stack):
    rows = weights.shape[0]
    parts = jnp.dot(pieces(weights), stack, preferred_element_type=f32)
    return parts[:rows] + parts[rows : 2 * rows] + parts[2 * rows :]


def dot_nt(left, right):
    return lax.dot_general(
        left, right, (((1,), (1,)), ((), ())), precision=highest, preferred_element_type=f32
    )


def dot_tn(left, right):
    return lax.dot_general(
        left, right, (((0,), (0,)), ((), ())), precision=highest, preferred_element_type=f32
    )


def dot_nn(left, right):
    return jnp.dot(left, right, precision=highest, preferred_element_type=f32)


def layout_kernel(slots_ref, tiles_ref, dense_ref):
    blocks, slots, edge = tiles_ref.shape[:3]
    many = dense_ref.shape[0] // edge
    dense_ref[...] = jnp.zeros_like(dense_ref)
    for b in range(blocks):
        for s in range(slots):

            @pl.when(slots_ref[b, s] < many)
            def _():
                start = pl.multiple_of(slots_ref[b, s] * edge, edge)
                dense_ref[pl.ds(start, edge), b * edge : (b + 1) * edge] = tiles_ref[b, s].T


def product(place_ref, dense_ref, mix_ref, stack, mine_refs):
    edge = mine_refs[0].shape[-1]
    vecs = mix_ref.shape[0]
    high, low = halves(jnp.dot(stack, dense_ref[...], preferred_element_type=f32))
    weights = jnp.concatenate(halves(mix_ref[...]), axis=0)
    mixed = jnp.dot(weights, high, preferred_element_type=f32)
    mixed = mixed[:vecs] + mixed[vecs:] + jnp.dot(weights[:vecs], low, preferred_element_type=f32)
    if len(mine_refs) == 2:
        first = place_ref[0] == 0
        low, high = mixed[:, :edge], mixed[:, edge:]
        mine_refs[0][...] = jnp.where(first, low, high)
        mine_refs[1][...] = jnp.where(first, high, low)
    else:
        for b in range(mine_refs[0].shape[0]):
            mine_refs[0][b] = mixed[:, b * edge : (b + 1) * edge]


def first_kernel(parts, place_ref, dense_ref, mix_ref, *refs):
    part_refs, stack_ref, mine_refs = refs[:parts], refs[parts], refs[parts + 1 :]
    edge = mine_refs[0].shape[-1]
    at = 0
    for ref in part_refs:
        for i in range(ref.shape[0]):
            stack_ref[:, at : at + edge] = ref[i]
            at += edge
    product(place_ref, dense_ref, mix_ref, stack_ref[...], mine_refs)


def residual_scale(q, square):
    return lax.rsqrt(jnp.maximum(square - jnp.sum((q * q).T, axis=1, keepdims=True), 0.0) + epsilon)


def next_kernel(place_ref, dense_ref, mix_ref, crosses, basis_ref, wide_ref, dirs_ref, stack_ref, *mine_refs):
    vecs = wide_ref.shape[0]
    both = sum(ref[...] for ref in crosses)
    q = both[:, :vecs]
    scale = residual_scale(q, both[:, vecs : vecs + 1])
    high, low = halves(q)
    terms = jnp.concatenate([high, high, low], axis=0)
    basis = jnp.concatenate([basis_ref[: 2 * vecs], basis_ref[:vecs]], axis=0)
    part = lax.dot_general(terms, basis, (((0,), (0,)), ((), ())), preferred_element_type=f32)
    stack_ref[:vecs] = basis_ref[:vecs]
    stack_ref[vecs : 2 * vecs] = ((part - wide_ref[...].astype(f32)) * scale).astype(bf16)
    stack_ref[2 * vecs :] = dirs_ref[...]
    product(place_ref, dense_ref, mix_ref, stack_ref[...], mine_refs)


def gram_kernel(stack_ref, mix_ref, search_ref, pack_ref, search_out, *own_rotated):
    vecs, edge = mix_ref.shape[0], search_out.shape[1]
    rotated = times_stack(mix_ref[...], stack_ref[...])
    search = times_stack(search_ref[...], stack_ref[vecs:])
    search_out[...] = search[:, :edge]
    if own_rotated:
        own_rotated[0][...] = rotated[:, :edge]
    square = jnp.sum(search * search, axis=1, keepdims=True)
    pack_ref[...] = jnp.concatenate(
        [dot_nt(rotated, rotated), jnp.broadcast_to(square, (vecs, vecs))], axis=1
    )


def factor_kernel(nodes, packs, inverse_ref, scale_ref):
    vecs = inverse_ref.shape[0]
    total = sum(ref[...] for ref in packs) / nodes
    scale_ref[...] = lax.rsqrt(jnp.maximum(total, 0.0) + epsilon)
    row_ids = lax.broadcasted_iota(jnp.int32, (vecs, 2 * vecs), 0)
    lane_ids = lax.broadcasted_iota(jnp.int32, (vecs, 2 * vecs), 1)
    diagonal = jnp.where(lane_ids == row_ids, total, 0.0)
    across = lax.rsqrt(jnp.sum(diagonal, axis=0, keepdims=True))
    height, step = 8, 4
    shape = (height, 2 * vecs)
    ids = lax.broadcasted_iota(jnp.int32, shape, 0)
    lanes = lax.broadcasted_iota(jnp.int32, shape, 1)

    def lane(tile, index):
        return jnp.take_along_axis(tile, index, axis=1)

    tiles = []
    for t in range(0, vecs, height):
        tile = total[t : t + height]
        down = lax.rsqrt(lane(tile, ids + t))
        unit = jnp.where(lanes == ids + (t + vecs), down, 0.0)
        tiles.append(jnp.where(lanes < vecs, tile * down * across, unit))
    done = [None] * len(tiles)
    for j in range(0, vecs, step):
        t, s = divmod(j, height)
        rows = [jnp.broadcast_to(tiles[t][s + m : s + m + 1], shape) for m in range(step)]
        columns = [
            [lane(tile, jnp.full(shape, k, jnp.int32)) for k in range(j, j + step)] for tile in tiles[t:]
        ]

        def pivot(m, n):
            return jnp.broadcast_to(columns[0][n][s + m : s + m + 1], shape)

        p00, p10, p11 = pivot(0, 0), pivot(1, 0), pivot(1, 1)
        q20, q21, q30, q31 = pivot(2, 0), pivot(2, 1), pivot(3, 0), pivot(3, 1)
        w22, w32, w33 = pivot(2, 2), pivot(3, 2), pivot(3, 3)
        scale = 1.0 / (p00 * p11 - p10 * p10)
        i00, i10, i11 = p11 * scale, -p10 * scale, p00 * scale
        e20, e21 = q20 * i00 + q21 * i10, q20 * i10 + q21 * i11
        e30, e31 = q30 * i00 + q31 * i10, q30 * i10 + q31 * i11
        s22 = w22 - (e20 * q20 + e21 * q21)
        s32 = w32 - (e30 * q20 + e31 * q21)
        s33 = w33 - (e30 * q30 + e31 * q31)
        scale = 1.0 / (s22 * s33 - s32 * s32)
        u22, u32, u33 = s33 * scale, -s32 * scale, s22 * scale
        below2 = rows[2] - (e20 * rows[0] + e21 * rows[1])
        below3 = rows[3] - (e30 * rows[0] + e31 * rows[1])
        y2, y3 = below2 * u22 + below3 * u32, below2 * u32 + below3 * u33
        z0 = rows[0] - (y2 * q20 + y3 * q30)
        z1 = rows[1] - (y2 * q21 + y3 * q31)
        y0, y1 = z0 * i00 + z1 * i10, z0 * i10 + z1 * i11
        for u in range(t, len(tiles)):
            if u == t and s + step == height:
                continue
            x0, x1, x2, x3 = columns[u - t]
            less = (x0 * y0 + x1 * y1) + (x2 * y2 + x3 * y3)
            if u == t:
                less = jnp.where(ids >= s + step, less, 0.0)
            tiles[u] = tiles[u] - less
        ratio = p10 / p00
        finished = [rows[0], rows[1] - ratio * rows[0], below2, below3 - (s32 / s22) * below2]
        roots = [p00, p11 - ratio * p10, s22, s33 - (s32 / s22) * s32]
        for m in range(step):
            value = finished[m] * lax.rsqrt(roots[m])
            done[t] = value if done[t] is None else jnp.where(ids >= s + m, value, done[t])
    inverse_ref[...] = jnp.concatenate(done, axis=0)[:, vecs:]


def basis_kernel(inverse_ref, scale_ref, stack_ref, mix_ref, search_ref, basis_ref, dirs_ref):
    vecs = mix_ref.shape[0]
    dirs_ref[...] = (search_ref[...] * scale_ref[:, vecs : vecs + 1]).astype(bf16)
    basis = times_stack(dot_nn(inverse_ref[...], mix_ref[...]), stack_ref[...])
    basis_ref[...] = pieces(basis)


def terms_kernel(rotated_ref, adj_ref, terms_ref):
    adj = adj_ref[...]
    terms_ref[...] = jnp.concatenate([dot_nt(rotated_ref[...], adj), dot_nt(adj, adj)], axis=1)


def own_kernel(inverse_ref, scale_ref, rotated_ref, search_ref, basis_ref, dirs_ref):
    vecs = inverse_ref.shape[0]
    basis_ref[...] = dot_nn(inverse_ref[...], rotated_ref[...])
    dirs_ref[...] = search_ref[...] * scale_ref[:, vecs : vecs + 1]


def last_kernel(nodes, terms, inverse_ref, rotated_ref, adj_ref, resid_ref, rayleigh_ref):
    vecs = inverse_ref.shape[0]
    inverse = inverse_ref[...]
    total = sum(ref[...] for ref in terms) / nodes
    q = dot_nt(dot_nn(inverse, total[:, :vecs]), inverse)
    square = jnp.sum(dot_nn(inverse, total[:, vecs:]) * inverse, axis=1, keepdims=True)
    raw = dot_nn(dot_tn(q, inverse), rotated_ref[...]) - dot_nn(inverse, adj_ref[...])
    resid_ref[...] = raw * residual_scale(q, square)
    row_ids = lax.broadcasted_iota(jnp.int32, (vecs, vecs), 0)
    lane_ids = lax.broadcasted_iota(jnp.int32, (vecs, vecs), 1)
    rayleigh_ref[...] = jnp.where(row_ids == lane_ids, 1.0, 0.0) - q


def solve_kernel(parts, *refs):
    part_refs, inverse_ref, blocks_ref = refs[:parts], refs[parts], refs[parts + 1]
    vecs, edge = part_refs[0].shape
    solved = dot_nn(inverse_ref[...], jnp.concatenate([ref[...] for ref in part_refs], axis=1))
    for i in range(parts):
        blocks_ref[i * vecs : (i + 1) * vecs, :] = solved[:, i * edge : (i + 1) * edge].astype(bf16)


def cross_kernel(nodes, parts, *refs):
    part_refs, basis_ref, cross_ref, wide_ref = refs[:parts], refs[parts], refs[parts + 1], refs[parts + 2]
    vecs = wide_ref.shape[0]
    edge = part_refs[0].shape[1]
    at = 0
    for ref in part_refs:
        for i in range(ref.shape[0] // vecs):
            wide_ref[:, at : at + edge] = ref[i * vecs : (i + 1) * vecs, :]
            at += edge
    cross = lax.dot_general(
        basis_ref[...], wide_ref[...], (((1,), (1,)), ((), ())), preferred_element_type=f32
    )
    cross = cross[:vecs] + cross[vecs : 2 * vecs] + cross[2 * vecs :]
    values = wide_ref[...].astype(f32)
    square = jnp.sum(values * values, axis=1, keepdims=True)
    cross_ref[...] = jnp.concatenate([cross, jnp.broadcast_to(square, cross.shape)], axis=1) / nodes


def swap(value, by, axis):
    size = lax.axis_size(axis)
    return lax.ppermute(value, axis, [(i, i ^ by) for i in range(size)])


def panel_terms(value):
    if lax.axis_size("panel") == 2:
        return [value, swap(value, 1, "panel")]
    return [lax.psum(value, "panel")]


def far_values(value, near):
    far = lax.axis_size("rows") // near
    return [value] + [swap(value, near * i, "rows") for i in range(1, far)]


def near_values(held, near):
    return [held] + [swap(held, i, "rows") for i in range(1, near)]


def body(
    adj_tiles,
    row_counts,
    tile_cols,
    start_basis,
    start_resid,
    start_search,
    ritz_basis,
    ritz_search,
):
    tile_set = adj_tiles[0, 0]
    counts = row_counts[0, 0]
    columns = tile_cols[0, 0]
    blocks, slots, edge = tile_set.shape[:3]
    vecs = start_basis.shape[0]
    rows, panels = lax.axis_size("rows"), lax.axis_size("panel")
    nodes = start_basis.shape[1] * rows * panels
    wide = rows * edge
    near = 4
    away = columns ^ lax.axis_index("rows")
    position = (away % near) * (rows // near) + away // near
    in_use = jnp.arange(slots, dtype=jnp.int32)[None, :] < counts[:, None]
    slot_ids = jnp.where(in_use, position, rows).astype(jnp.int32)
    place = lax.axis_index("panel").astype(jnp.int32).reshape(1)

    if panels == 2:
        mine_outs = [((vecs, edge), f32)] * 2
    else:
        mine_outs = [((blocks, vecs, edge), f32)]
    stack_out = ((3 * vecs, wide), bf16)
    limit = 16 if wide <= 4096 else 56
    dense, = call(
        layout_kernel, [((wide, blocks * edge), bf16)], [slot_ids, tile_set], smem=(0,), limit=limit
    )

    start = jnp.concatenate([start_basis, start_resid, start_search], axis=0)[None]
    parts = near_values(jnp.concatenate(far_values(start, near), axis=0), near)
    parts, dense = lax.optimization_barrier((parts, dense))
    state = None
    sweeps = ritz_basis.shape[0]
    for sweep in range(sweeps):
        last = sweep == sweeps - 1
        mixing = ritz_basis[sweep]
        if state is None:
            stack, *mine = call(
                functools.partial(first_kernel, near),
                [stack_out] + mine_outs,
                [place, dense, mixing] + parts,
                smem=(0,),
                limit=limit,
            )
        else:
            crosses, basis, wide_adj, dirs = state
            count = len(crosses)

            def kernel(p, t, m, *refs):
                next_kernel(p, t, m, refs[:count], *refs[count:])

            stack, *mine = call(
                kernel,
                [stack_out] + mine_outs,
                [place, dense, mixing] + crosses + [basis, wide_adj, dirs],
                smem=(0,),
                limit=limit,
            )
        own_out = ((vecs, edge), f32)
        pack, search, *rotated = call(
            gram_kernel,
            [((vecs, 2 * vecs), f32)] + ([own_out, own_out] if last else [((vecs, wide), f32)]),
            [stack, mixing, ritz_search[sweep]],
            limit=limit,
        )
        if panels == 2:
            other = swap(mine[1], 1, "panel")
            other, pack = lax.optimization_barrier((other, pack))
            rotated_adj = mine[0] + other
        else:
            rotated_adj = lax.psum_scatter(mine[0], "panel", scatter_dimension=0, tiled=True)[0]
        packs = panel_terms(pack)
        pack_count = len(packs)

        def kernel_factor(*refs):
            factor_kernel(nodes, refs[:pack_count], *refs[pack_count:])

        inverse, scale = call(
            kernel_factor, [((vecs, vecs), f32), ((vecs, 2 * vecs), f32)], packs
        )
        if last:
            break
        far_parts = far_values(rotated_adj, near)
        far_parts, inverse = lax.optimization_barrier((far_parts, inverse))
        held, = call(
            functools.partial(solve_kernel, len(far_parts)),
            [((len(far_parts) * vecs, edge), bf16)],
            far_parts + [inverse],
            limit=limit,
        )
        adj_parts = near_values(held, near)
        basis, dirs = call(
            basis_kernel,
            [((3 * vecs, wide), bf16), ((vecs, wide), bf16)],
            [inverse, scale, stack, mixing, search],
            limit=limit,
        )
        cross, wide_adj = call(
            functools.partial(cross_kernel, nodes, near),
            [((vecs, 2 * vecs), f32), ((vecs, wide), bf16)],
            adj_parts + [basis],
            limit=limit,
        )
        state = (panel_terms(cross), basis, wide_adj, dirs)

    rotated = rotated[0]
    terms, = call(terms_kernel, [((vecs, 2 * vecs), f32)], [rotated, rotated_adj])
    far_parts, inverse = lax.optimization_barrier((far_values(terms, near), inverse))
    own_basis, own_dirs = call(own_kernel, [own_out, own_out], [inverse, scale, rotated, search])
    terms = panel_terms(sum(near_values(sum(far_parts), near)))
    count = len(terms)

    def kernel_last(*refs):
        last_kernel(nodes, refs[:count], *refs[count:])

    resid, rayleigh = call(
        kernel_last, [own_out, ((vecs, vecs), f32)], terms + [inverse, rotated, rotated_adj]
    )
    return (own_basis, resid, own_dirs, rayleigh)


def solution(mesh):
    return jax.shard_map(
        body,
        mesh=mesh,
        in_specs=(
            P("rows", "panel", None, None, None, None),
            P("rows", "panel", None),
            P("rows", "panel", None, None),
            P(None, ("rows", "panel")),
            P(None, ("rows", "panel")),
            P(None, ("rows", "panel")),
            P(),
            P(),
        ),
        out_specs=(
            P(None, ("rows", "panel")),
            P(None, ("rows", "panel")),
            P(None, ("rows", "panel")),
            P(),
        ),
        check_vma=False,
    )
```

```python
import functools

import jax
import jax.numpy as jnp
from jax import lax
from jax.experimental import pallas as pl
from jax.experimental.pallas import tpu as pltpu
from jax.sharding import PartitionSpec as P

epsilon = 1e-06
highest = lax.Precision.HIGHEST
f32 = jnp.float32
bf16 = jnp.bfloat16


def call(kernel, outs, args, smem=(), limit=16):
    specs = [
        pl.BlockSpec(memory_space=pltpu.SMEM if i in smem else pltpu.VMEM) for i in range(len(args))
    ]
    return pl.pallas_call(
        kernel,
        out_shape=[jax.ShapeDtypeStruct(shape, kind) for shape, kind in outs],
        in_specs=specs,
        out_specs=[pl.BlockSpec(memory_space=pltpu.VMEM) for _ in outs],
        compiler_params=pltpu.CompilerParams(vmem_limit_bytes=limit << 20),
    )(*args)


def pieces(value):
    high = value.astype(bf16)
    rest = value - high.astype(f32)
    middle = rest.astype(bf16)
    low = (rest - middle.astype(f32)).astype(bf16)
    return jnp.concatenate([high, middle, low], axis=0)


def halves(value):
    high = value.astype(bf16)
    return high, (value - high.astype(f32)).astype(bf16)


def times_stack(weights, stack):
    rows = weights.shape[0]
    parts = jnp.dot(pieces(weights), stack, preferred_element_type=f32)
    return parts[:rows] + parts[rows : 2 * rows] + parts[2 * rows :]


def dot_nt(left, right):
    return lax.dot_general(
        left, right, (((1,), (1,)), ((), ())), precision=highest, preferred_element_type=f32
    )


def dot_tn(left, right):
    return lax.dot_general(
        left, right, (((0,), (0,)), ((), ())), precision=highest, preferred_element_type=f32
    )


def dot_nn(left, right):
    return jnp.dot(left, right, precision=highest, preferred_element_type=f32)


def layout_kernel(slots_ref, tiles_ref, dense_ref):
    blocks, slots, edge = tiles_ref.shape[:3]
    many = dense_ref.shape[0] // edge
    dense_ref[...] = jnp.zeros_like(dense_ref)
    for b in range(blocks):
        for s in range(slots):

            @pl.when(slots_ref[b, s] < many)
            def _():
                start = pl.multiple_of(slots_ref[b, s] * edge, edge)
                dense_ref[pl.ds(start, edge), b * edge : (b + 1) * edge] = tiles_ref[b, s].T


def product(place_ref, dense_ref, mix_ref, stack, mine_refs):
    edge = mine_refs[0].shape[-1]
    vecs = mix_ref.shape[0]
    high, low = halves(jnp.dot(stack, dense_ref[...], preferred_element_type=f32))
    weights = jnp.concatenate(halves(mix_ref[...]), axis=0)
    mixed = jnp.dot(weights, high, preferred_element_type=f32)
    mixed = mixed[:vecs] + mixed[vecs:] + jnp.dot(weights[:vecs], low, preferred_element_type=f32)
    if len(mine_refs) == 2:
        first = place_ref[0] == 0
        low, high = mixed[:, :edge], mixed[:, edge:]
        mine_refs[0][...] = jnp.where(first, low, high)
        mine_refs[1][...] = jnp.where(first, high, low)
    else:
        for b in range(mine_refs[0].shape[0]):
            mine_refs[0][b] = mixed[:, b * edge : (b + 1) * edge]


def first_kernel(parts, place_ref, dense_ref, mix_ref, *refs):
    part_refs, stack_ref, mine_refs = refs[:parts], refs[parts], refs[parts + 1 :]
    edge = mine_refs[0].shape[-1]
    at = 0
    for ref in part_refs:
        for i in range(ref.shape[0]):
            stack_ref[:, at : at + edge] = ref[i]
            at += edge
    product(place_ref, dense_ref, mix_ref, stack_ref[...], mine_refs)


def residual_scale(q, square):
    return lax.rsqrt(jnp.maximum(square - jnp.sum((q * q).T, axis=1, keepdims=True), 0.0) + epsilon)


def next_kernel(place_ref, dense_ref, mix_ref, crosses, basis_ref, wide_ref, dirs_ref, stack_ref, *mine_refs):
    vecs = wide_ref.shape[0]
    both = sum(ref[...] for ref in crosses)
    q = both[:, :vecs]
    scale = residual_scale(q, both[:, vecs : vecs + 1])
    high, low = halves(q)
    terms = jnp.concatenate([high, high, low], axis=0)
    basis = jnp.concatenate([basis_ref[: 2 * vecs], basis_ref[:vecs]], axis=0)
    part = lax.dot_general(terms, basis, (((0,), (0,)), ((), ())), preferred_element_type=f32)
    stack_ref[:vecs] = basis_ref[:vecs]
    stack_ref[vecs : 2 * vecs] = ((part - wide_ref[...].astype(f32)) * scale).astype(bf16)
    stack_ref[2 * vecs :] = dirs_ref[...]
    product(place_ref, dense_ref, mix_ref, stack_ref[...], mine_refs)


def gram_kernel(stack_ref, mix_ref, search_ref, pack_ref, search_out, *own_rotated):
    vecs, edge = mix_ref.shape[0], search_out.shape[1]
    rotated = times_stack(mix_ref[...], stack_ref[...])
    search = times_stack(search_ref[...], stack_ref[vecs:])
    search_out[...] = search[:, :edge]
    if own_rotated:
        own_rotated[0][...] = rotated[:, :edge]
    square = jnp.sum(search * search, axis=1, keepdims=True)
    pack_ref[...] = jnp.concatenate(
        [dot_nt(rotated, rotated), jnp.broadcast_to(square, (vecs, vecs))], axis=1
    )


def factor_kernel(nodes, packs, inverse_ref, scale_ref):
    vecs = inverse_ref.shape[0]
    total = sum(ref[...] for ref in packs) / nodes
    scale_ref[...] = lax.rsqrt(jnp.maximum(total, 0.0) + epsilon)
    row_ids = lax.broadcasted_iota(jnp.int32, (vecs, 2 * vecs), 0)
    lane_ids = lax.broadcasted_iota(jnp.int32, (vecs, 2 * vecs), 1)
    diagonal = jnp.where(lane_ids == row_ids, total, 0.0)
    across = lax.rsqrt(jnp.sum(diagonal, axis=0, keepdims=True))
    height, step = 8, 4
    shape = (height, 2 * vecs)
    ids = lax.broadcasted_iota(jnp.int32, shape, 0)
    lanes = lax.broadcasted_iota(jnp.int32, shape, 1)

    def lane(tile, index):
        return jnp.take_along_axis(tile, index, axis=1)

    tiles = []
    for t in range(0, vecs, height):
        tile = total[t : t + height]
        down = lax.rsqrt(lane(tile, ids + t))
        unit = jnp.where(lanes == ids + (t + vecs), down, 0.0)
        tiles.append(jnp.where(lanes < vecs, tile * down * across, unit))
    done = [None] * len(tiles)
    for j in range(0, vecs, step):
        t, s = divmod(j, height)
        rows = [jnp.broadcast_to(tiles[t][s + m : s + m + 1], shape) for m in range(step)]
        columns = [
            [lane(tile, jnp.full(shape, k, jnp.int32)) for k in range(j, j + step)] for tile in tiles[t:]
        ]

        def pivot(m, n):
            return jnp.broadcast_to(columns[0][n][s + m : s + m + 1], shape)

        p00, p10, p11 = pivot(0, 0), pivot(1, 0), pivot(1, 1)
        q20, q21, q30, q31 = pivot(2, 0), pivot(2, 1), pivot(3, 0), pivot(3, 1)
        w22, w32, w33 = pivot(2, 2), pivot(3, 2), pivot(3, 3)
        scale = 1.0 / (p00 * p11 - p10 * p10)
        i00, i10, i11 = p11 * scale, -p10 * scale, p00 * scale
        e20, e21 = q20 * i00 + q21 * i10, q20 * i10 + q21 * i11
        e30, e31 = q30 * i00 + q31 * i10, q30 * i10 + q31 * i11
        s22 = w22 - (e20 * q20 + e21 * q21)
        s32 = w32 - (e30 * q20 + e31 * q21)
        s33 = w33 - (e30 * q30 + e31 * q31)
        scale = 1.0 / (s22 * s33 - s32 * s32)
        u22, u32, u33 = s33 * scale, -s32 * scale, s22 * scale
        below2 = rows[2] - (e20 * rows[0] + e21 * rows[1])
        below3 = rows[3] - (e30 * rows[0] + e31 * rows[1])
        y2, y3 = below2 * u22 + below3 * u32, below2 * u32 + below3 * u33
        z0 = rows[0] - (y2 * q20 + y3 * q30)
        z1 = rows[1] - (y2 * q21 + y3 * q31)
        y0, y1 = z0 * i00 + z1 * i10, z0 * i10 + z1 * i11
        for u in range(t, len(tiles)):
            if u == t and s + step == height:
                continue
            x0, x1, x2, x3 = columns[u - t]
            less = (x0 * y0 + x1 * y1) + (x2 * y2 + x3 * y3)
            if u == t:
                less = jnp.where(ids >= s + step, less, 0.0)
            tiles[u] = tiles[u] - less
        ratio = p10 / p00
        finished = [rows[0], rows[1] - ratio * rows[0], below2, below3 - (s32 / s22) * below2]
        roots = [p00, p11 - ratio * p10, s22, s33 - (s32 / s22) * s32]
        for m in range(step):
            value = finished[m] * lax.rsqrt(roots[m])
            done[t] = value if done[t] is None else jnp.where(ids >= s + m, value, done[t])
    inverse_ref[...] = jnp.concatenate(done, axis=0)[:, vecs:]


def basis_kernel(inverse_ref, scale_ref, stack_ref, mix_ref, search_ref, basis_ref, dirs_ref):
    vecs = mix_ref.shape[0]
    dirs_ref[...] = (search_ref[...] * scale_ref[:, vecs : vecs + 1]).astype(bf16)
    basis = times_stack(dot_nn(inverse_ref[...], mix_ref[...]), stack_ref[...])
    basis_ref[...] = pieces(basis)


def terms_kernel(rotated_ref, adj_ref, terms_ref):
    adj = adj_ref[...]
    terms_ref[...] = jnp.concatenate([dot_nt(rotated_ref[...], adj), dot_nt(adj, adj)], axis=1)


def own_kernel(inverse_ref, scale_ref, rotated_ref, adj_ref, search_ref, basis_ref, dirs_ref, both_ref):
    vecs, edge = rotated_ref.shape
    both = dot_nn(inverse_ref[...], jnp.concatenate([rotated_ref[...], adj_ref[...]], axis=1))
    both_ref[...] = both
    basis_ref[...] = both[:, :edge]
    dirs_ref[...] = search_ref[...] * scale_ref[:, vecs : vecs + 1]


def last_kernel(nodes, terms, inverse_ref, both_ref, resid_ref, rayleigh_ref):
    vecs, edge = resid_ref.shape
    inverse = inverse_ref[...]
    total = sum(ref[...] for ref in terms) / nodes
    turned = dot_nn(inverse, total[:, :vecs])
    square = jnp.sum(dot_nn(inverse, total[:, vecs:]) * inverse, axis=1, keepdims=True)
    q = dot_nt(turned, inverse)
    raw = dot_tn(q, both_ref[:, :edge]) - both_ref[:, edge:]
    resid_ref[...] = raw * residual_scale(q, square)
    row_ids = lax.broadcasted_iota(jnp.int32, (vecs, vecs), 0)
    lane_ids = lax.broadcasted_iota(jnp.int32, (vecs, vecs), 1)
    rayleigh_ref[...] = jnp.where(row_ids == lane_ids, 1.0, 0.0) - q


def solve_kernel(parts, *refs):
    part_refs, inverse_ref, blocks_ref = refs[:parts], refs[parts], refs[parts + 1]
    vecs, edge = part_refs[0].shape
    solved = dot_nn(inverse_ref[...], jnp.concatenate([ref[...] for ref in part_refs], axis=1))
    for i in range(parts):
        blocks_ref[i * vecs : (i + 1) * vecs, :] = solved[:, i * edge : (i + 1) * edge].astype(bf16)


def cross_kernel(nodes, parts, *refs):
    part_refs, basis_ref, cross_ref, wide_ref = refs[:parts], refs[parts], refs[parts + 1], refs[parts + 2]
    vecs = wide_ref.shape[0]
    edge = part_refs[0].shape[1]
    at = 0
    for ref in part_refs:
        for i in range(ref.shape[0] // vecs):
            wide_ref[:, at : at + edge] = ref[i * vecs : (i + 1) * vecs, :]
            at += edge
    cross = lax.dot_general(
        basis_ref[...], wide_ref[...], (((1,), (1,)), ((), ())), preferred_element_type=f32
    )
    cross = cross[:vecs] + cross[vecs : 2 * vecs] + cross[2 * vecs :]
    values = wide_ref[...].astype(f32)
    square = jnp.sum(values * values, axis=1, keepdims=True)
    cross_ref[...] = jnp.concatenate([cross, jnp.broadcast_to(square, cross.shape)], axis=1) / nodes


def swap(value, by, axis):
    size = lax.axis_size(axis)
    return lax.ppermute(value, axis, [(i, i ^ by) for i in range(size)])


def panel_terms(value):
    if lax.axis_size("panel") == 2:
        return [value, swap(value, 1, "panel")]
    return [lax.psum(value, "panel")]


def far_values(value, near):
    far = lax.axis_size("rows") // near
    return [value] + [swap(value, near * i, "rows") for i in range(1, far)]


def near_values(held, near):
    return [held] + [swap(held, i, "rows") for i in range(1, near)]


def body(
    adj_tiles,
    row_counts,
    tile_cols,
    start_basis,
    start_resid,
    start_search,
    ritz_basis,
    ritz_search,
):
    tile_set = adj_tiles[0, 0]
    counts = row_counts[0, 0]
    columns = tile_cols[0, 0]
    blocks, slots, edge = tile_set.shape[:3]
    vecs = start_basis.shape[0]
    rows, panels = lax.axis_size("rows"), lax.axis_size("panel")
    nodes = start_basis.shape[1] * rows * panels
    wide = rows * edge
    near = 4
    away = columns ^ lax.axis_index("rows")
    position = (away % near) * (rows // near) + away // near
    in_use = jnp.arange(slots, dtype=jnp.int32)[None, :] < counts[:, None]
    slot_ids = jnp.where(in_use, position, rows).astype(jnp.int32)
    place = lax.axis_index("panel").astype(jnp.int32).reshape(1)

    if panels == 2:
        mine_outs = [((vecs, edge), f32)] * 2
    else:
        mine_outs = [((blocks, vecs, edge), f32)]
    stack_out = ((3 * vecs, wide), bf16)
    limit = 16 if wide <= 4096 else 56

    start = jnp.concatenate([start_basis, start_resid, start_search], axis=0)[None]
    sweeps = ritz_basis.shape[0]
    held = jnp.concatenate(far_values(start, near), axis=0)
    held, slot_ids, tile_set, ritz_basis, ritz_search = lax.optimization_barrier(
        (held, slot_ids, tile_set, ritz_basis, ritz_search)
    )
    parts = near_values(held, near)
    dense, = call(
        layout_kernel, [((wide, blocks * edge), bf16)], [slot_ids, tile_set], smem=(0,), limit=limit
    )
    ritz = [(ritz_basis[sweep], ritz_search[sweep]) for sweep in range(sweeps)]
    parts, dense, ritz = lax.optimization_barrier((parts, dense, ritz))
    state = None
    for sweep in range(sweeps):
        last = sweep == sweeps - 1
        mixing, seeking = ritz[sweep]
        if state is None:
            stack, *mine = call(
                functools.partial(first_kernel, near),
                [stack_out] + mine_outs,
                [place, dense, mixing] + parts,
                smem=(0,),
                limit=limit,
            )
        else:
            crosses, basis, wide_adj, dirs = state
            count = len(crosses)

            def kernel(p, t, m, *refs):
                next_kernel(p, t, m, refs[:count], *refs[count:])

            stack, *mine = call(
                kernel,
                [stack_out] + mine_outs,
                [place, dense, mixing] + crosses + [basis, wide_adj, dirs],
                smem=(0,),
                limit=limit,
            )
        own_out = ((vecs, edge), f32)
        pack, search, *rotated = call(
            gram_kernel,
            [((vecs, 2 * vecs), f32)] + ([own_out, own_out] if last else [((vecs, wide), f32)]),
            [stack, mixing, seeking],
            limit=limit,
        )
        if panels == 2:
            other = swap(mine[1], 1, "panel")
            other, pack = lax.optimization_barrier((other, pack))
            rotated_adj = mine[0] + other
        else:
            rotated_adj = lax.psum_scatter(mine[0], "panel", scatter_dimension=0, tiled=True)[0]
        packs = panel_terms(pack)
        pack_count = len(packs)

        def kernel_factor(*refs):
            factor_kernel(nodes, refs[:pack_count], *refs[pack_count:])

        inverse, scale = call(
            kernel_factor, [((vecs, vecs), f32), ((vecs, 2 * vecs), f32)], packs
        )
        if last:
            break
        far_parts = far_values(rotated_adj, near)
        far_parts, inverse = lax.optimization_barrier((far_parts, inverse))
        held, = call(
            functools.partial(solve_kernel, len(far_parts)),
            [((len(far_parts) * vecs, edge), bf16)],
            far_parts + [inverse],
            limit=limit,
        )
        adj_parts = near_values(held, near)
        basis, dirs = call(
            basis_kernel,
            [((3 * vecs, wide), bf16), ((vecs, wide), bf16)],
            [inverse, scale, stack, mixing, search],
            limit=limit,
        )
        cross, wide_adj = call(
            functools.partial(cross_kernel, nodes, near),
            [((vecs, 2 * vecs), f32), ((vecs, wide), bf16)],
            adj_parts + [basis],
            limit=limit,
        )
        state = (panel_terms(cross), basis, wide_adj, dirs)

    rotated = rotated[0]
    terms, = call(terms_kernel, [((vecs, 2 * vecs), f32)], [rotated, rotated_adj])
    far_parts, inverse = lax.optimization_barrier((far_values(terms, near), inverse))
    own_basis, own_dirs, both = call(
        own_kernel,
        [own_out, own_out, ((vecs, 2 * edge), f32)],
        [inverse, scale, rotated, rotated_adj, search],
    )
    terms = panel_terms(sum(near_values(sum(far_parts), near)))
    count = len(terms)

    def kernel_last(*refs):
        last_kernel(nodes, refs[:count], *refs[count:])

    resid, rayleigh = call(
        kernel_last, [own_out, ((vecs, vecs), f32)], terms + [inverse, both]
    )
    return (own_basis, resid, own_dirs, rayleigh)


def solution(mesh):
    return jax.shard_map(
        body,
        mesh=mesh,
        in_specs=(
            P("rows", "panel", None, None, None, None),
            P("rows", "panel", None),
            P("rows", "panel", None, None),
            P(None, ("rows", "panel")),
            P(None, ("rows", "panel")),
            P(None, ("rows", "panel")),
            P(),
            P(),
        ),
        out_specs=(
            P(None, ("rows", "panel")),
            P(None, ("rows", "panel")),
            P(None, ("rows", "panel")),
            P(),
        ),
        check_vma=False,
    )
```

```python
import functools

import jax
import jax.numpy as jnp
from jax import lax
from jax.experimental import pallas as pl
from jax.experimental.pallas import tpu as pltpu
from jax.sharding import PartitionSpec as P

epsilon = 1e-06
highest = lax.Precision.HIGHEST
f32 = jnp.float32
bf16 = jnp.bfloat16


def call(kernel, outs, args, smem=(), limit=16, scratch=()):
    specs = [
        pl.BlockSpec(memory_space=pltpu.SMEM if i in smem else pltpu.VMEM) for i in range(len(args))
    ]
    return pl.pallas_call(
        kernel,
        out_shape=[jax.ShapeDtypeStruct(shape, kind) for shape, kind in outs],
        in_specs=specs,
        out_specs=[pl.BlockSpec(memory_space=pltpu.VMEM) for _ in outs],
        scratch_shapes=[pltpu.VMEM(shape, kind) for shape, kind in scratch],
        compiler_params=pltpu.CompilerParams(vmem_limit_bytes=limit << 20),
    )(*args)


def pieces(value):
    high = value.astype(bf16)
    rest = value - high.astype(f32)
    middle = rest.astype(bf16)
    low = (rest - middle.astype(f32)).astype(bf16)
    return jnp.concatenate([high, middle, low], axis=0)


def halves(value):
    high = value.astype(bf16)
    return high, (value - high.astype(f32)).astype(bf16)


def times_stack(weights, stack):
    rows = weights.shape[0]
    parts = jnp.dot(pieces(weights), stack, preferred_element_type=f32)
    return parts[:rows] + parts[rows : 2 * rows] + parts[2 * rows :]


def dot_nt(left, right):
    return lax.dot_general(
        left, right, (((1,), (1,)), ((), ())), precision=highest, preferred_element_type=f32
    )


def dot_tn(left, right):
    return lax.dot_general(
        left, right, (((0,), (0,)), ((), ())), precision=highest, preferred_element_type=f32
    )


def dot_nn(left, right):
    return jnp.dot(left, right, precision=highest, preferred_element_type=f32)


def layout_kernel(slots_ref, tiles_ref, dense_ref):
    blocks, slots, edge = tiles_ref.shape[:3]
    many = dense_ref.shape[0] // edge
    dense_ref[...] = jnp.zeros_like(dense_ref)
    for b in range(blocks):
        for s in range(slots):

            @pl.when(slots_ref[b, s] < many)
            def _():
                start = pl.multiple_of(slots_ref[b, s] * edge, edge)
                dense_ref[pl.ds(start, edge), b * edge : (b + 1) * edge] = tiles_ref[b, s].T


def send_parts(place_ref, mix_ref, image, mine_refs):
    edge = mine_refs[0].shape[-1]
    vecs = mix_ref.shape[0]
    high, low = halves(image)
    weights = jnp.concatenate(halves(mix_ref[...]), axis=0)
    mixed = jnp.dot(weights, high, preferred_element_type=f32)
    mixed = mixed[:vecs] + mixed[vecs:] + jnp.dot(weights[:vecs], low, preferred_element_type=f32)
    if len(mine_refs) == 2:
        first = place_ref[0] == 0
        low, high = mixed[:, :edge], mixed[:, edge:]
        mine_refs[0][...] = jnp.where(first, low, high)
        mine_refs[1][...] = jnp.where(first, high, low)
    else:
        for b in range(mine_refs[0].shape[0]):
            mine_refs[0][b] = mixed[:, b * edge : (b + 1) * edge]


def first_kernel(parts, place_ref, dense_ref, mix_ref, *refs):
    part_refs, stack_ref, mine_refs = refs[:parts], refs[parts], refs[parts + 1 :]
    edge = mine_refs[0].shape[-1]
    at = 0
    for ref in part_refs:
        far = ref.shape[0]
        for i in range(far):
            stack_ref[:, at : at + edge] = ref[-i % far]
            at += edge
    image = jnp.dot(stack_ref[...], dense_ref[...], preferred_element_type=f32)
    send_parts(place_ref, mix_ref, image, mine_refs)


def residual_scale(q, square):
    return lax.rsqrt(jnp.maximum(square - jnp.sum((q * q).T, axis=1, keepdims=True), 0.0) + epsilon)


def cross_terms(crosses):
    both = sum(ref[...] for ref in crosses)
    vecs = both.shape[0]
    q = both[:, :vecs]
    scale = residual_scale(q, both[:, vecs : vecs + 1])
    at = vecs + vecs // 2
    return q, scale, lax.rsqrt(both[:, at : at + 1] + epsilon)


def ahead_kernel(basis_ref, wide_ref, search_ref, dense_ref, image_ref):
    vecs = wide_ref.shape[0]
    rows = jnp.concatenate([basis_ref[:vecs], wide_ref[...], search_ref[...].astype(bf16)], axis=0)
    image_ref[...] = jnp.dot(rows, dense_ref[...], preferred_element_type=f32)


def mix_kernel(place_ref, mix_ref, crosses, image_ref, *mine_refs):
    vecs = mix_ref.shape[0]
    q, scale, step = cross_terms(crosses)
    basis = image_ref[:vecs]
    raw = dot_tn(q, basis) - image_ref[vecs : 2 * vecs]
    image = jnp.concatenate([basis, raw * scale, image_ref[2 * vecs :] * step], axis=0)
    send_parts(place_ref, mix_ref, image, mine_refs)


def gram_terms(stack, mix_ref, pack_ref, search_refs):
    vecs = mix_ref.shape[0]
    rotated = times_stack(mix_ref[...], stack)
    square = jnp.zeros((vecs, vecs), f32)
    if search_refs:
        weights_ref, search_out, own_rotated = search_refs
        edge = search_out.shape[1]
        search = times_stack(weights_ref[...], stack[vecs:])
        search_out[...] = search[:, :edge]
        own_rotated[...] = rotated[:, :edge]
        square = jnp.broadcast_to(jnp.sum(search * search, axis=1, keepdims=True), square.shape)
    split = jnp.concatenate(halves(rotated), axis=0)
    gram = lax.dot_general(split, split, (((1,), (1,)), ((), ())), preferred_element_type=f32)
    gram = gram[:vecs] + gram[vecs:]
    pack_ref[...] = jnp.concatenate([gram[:, :vecs] + gram[:, vecs:], square], axis=1)


def gram_kernel(stack_ref, mix_ref, pack_ref):
    gram_terms(stack_ref[...], mix_ref, pack_ref, ())


def stack_kernel(last, mix_ref, crosses, basis_ref, wide_ref, found_ref, *refs):
    vecs = wide_ref.shape[0]
    if last:
        weights, pack_ref, outs, stack_ref = refs[:1], refs[1], refs[2:4], refs[4]
    else:
        weights, pack_ref, outs, stack_ref = (), refs[0], (), refs[1]
    q, scale, step = cross_terms(crosses)
    terms = jnp.concatenate([*halves(q), q.astype(bf16)], axis=0)
    basis = jnp.concatenate([basis_ref[:vecs], basis_ref[:vecs], basis_ref[vecs : 2 * vecs]], axis=0)
    part = lax.dot_general(terms, basis, (((0,), (0,)), ((), ())), preferred_element_type=f32)
    stack_ref[:vecs] = basis_ref[:vecs]
    stack_ref[vecs : 2 * vecs] = ((part - wide_ref[...].astype(f32)) * scale).astype(bf16)
    stack_ref[2 * vecs :] = (found_ref[...] * step).astype(bf16)
    gram_terms(stack_ref[...], mix_ref, pack_ref, (*weights, *outs))


def factor_kernel(nodes, packs, inverse_ref, *scale_ref):
    vecs = inverse_ref.shape[0]
    total = sum(ref[...] for ref in packs) / nodes
    if scale_ref:
        scale_ref[0][...] = lax.rsqrt(jnp.maximum(total, 0.0) + epsilon)
    row_ids = lax.broadcasted_iota(jnp.int32, (vecs, 2 * vecs), 0)
    lane_ids = lax.broadcasted_iota(jnp.int32, (vecs, 2 * vecs), 1)
    diagonal = jnp.where(lane_ids == row_ids, total, 0.0)
    across = lax.rsqrt(jnp.sum(diagonal, axis=0, keepdims=True))
    height, step = 8, 4
    shape = (height, 2 * vecs)
    ids = lax.broadcasted_iota(jnp.int32, shape, 0)
    lanes = lax.broadcasted_iota(jnp.int32, shape, 1)

    def lane(tile, index):
        return jnp.take_along_axis(tile, index, axis=1)

    tiles = []
    for t in range(0, vecs, height):
        tile = total[t : t + height]
        down = lax.rsqrt(lane(tile, ids + t))
        unit = jnp.where(lanes == ids + (t + vecs), down, 0.0)
        tiles.append(jnp.where(lanes < vecs, tile * down * across, unit))
    done = [None] * len(tiles)
    for j in range(0, vecs, step):
        t, s = divmod(j, height)
        rows = [jnp.broadcast_to(tiles[t][s + m : s + m + 1], shape) for m in range(step)]
        columns = [
            [lane(tile, jnp.full(shape, k, jnp.int32)) for k in range(j, j + step)] for tile in tiles[t:]
        ]

        def pivot(m, n):
            return jnp.broadcast_to(columns[0][n][s + m : s + m + 1], shape)

        p00, p10, p11 = pivot(0, 0), pivot(1, 0), pivot(1, 1)
        q20, q21, q30, q31 = pivot(2, 0), pivot(2, 1), pivot(3, 0), pivot(3, 1)
        w22, w32, w33 = pivot(2, 2), pivot(3, 2), pivot(3, 3)
        scale = 1.0 / (p00 * p11 - p10 * p10)
        i00, i10, i11 = p11 * scale, -p10 * scale, p00 * scale
        e20, e21 = q20 * i00 + q21 * i10, q20 * i10 + q21 * i11
        e30, e31 = q30 * i00 + q31 * i10, q30 * i10 + q31 * i11
        s22 = w22 - (e20 * q20 + e21 * q21)
        s32 = w32 - (e30 * q20 + e31 * q21)
        s33 = w33 - (e30 * q30 + e31 * q31)
        scale = 1.0 / (s22 * s33 - s32 * s32)
        u22, u32, u33 = s33 * scale, -s32 * scale, s22 * scale
        below2 = rows[2] - (e20 * rows[0] + e21 * rows[1])
        below3 = rows[3] - (e30 * rows[0] + e31 * rows[1])
        y2, y3 = below2 * u22 + below3 * u32, below2 * u32 + below3 * u33
        z0 = rows[0] - (y2 * q20 + y3 * q30)
        z1 = rows[1] - (y2 * q21 + y3 * q31)
        y0, y1 = z0 * i00 + z1 * i10, z0 * i10 + z1 * i11
        for u in range(t, len(tiles)):
            if u == t and s + step == height:
                continue
            x0, x1, x2, x3 = columns[u - t]
            less = (x0 * y0 + x1 * y1) + (x2 * y2 + x3 * y3)
            if u == t:
                less = jnp.where(ids >= s + step, less, 0.0)
            tiles[u] = tiles[u] - less
        ratio = p10 / p00
        finished = [rows[0], rows[1] - ratio * rows[0], below2, below3 - (s32 / s22) * below2]
        roots = [p00, p11 - ratio * p10, s22, s33 - (s32 / s22) * s32]
        for m in range(step):
            value = finished[m] * lax.rsqrt(roots[m])
            done[t] = value if done[t] is None else jnp.where(ids >= s + m, value, done[t])
    inverse_ref[...] = jnp.concatenate(done, axis=0)[:, vecs:]


def basis_kernel(inverse_ref, stack_ref, mix_ref, weights_ref, basis_ref, search_ref, square_ref):
    vecs = mix_ref.shape[0]
    search = times_stack(weights_ref[...], stack_ref[vecs:])
    search_ref[...] = search
    square_ref[...] = jnp.broadcast_to(jnp.sum(search * search, axis=1, keepdims=True), square_ref.shape)
    basis = times_stack(dot_nn(inverse_ref[...], mix_ref[...]), stack_ref[...])
    basis_ref[...] = pieces(basis)


def terms_kernel(rotated_ref, adj_ref, terms_ref):
    adj = adj_ref[...]
    terms_ref[...] = jnp.concatenate([dot_nt(rotated_ref[...], adj), dot_nt(adj, adj)], axis=1)


def own_kernel(inverse_ref, scale_ref, rotated_ref, adj_ref, search_ref, basis_ref, dirs_ref, both_ref):
    vecs, edge = rotated_ref.shape
    both = dot_nn(inverse_ref[...], jnp.concatenate([rotated_ref[...], adj_ref[...]], axis=1))
    both_ref[...] = both
    basis_ref[...] = both[:, :edge]
    dirs_ref[...] = search_ref[...] * scale_ref[:, vecs : vecs + 1]


def last_kernel(nodes, terms, inverse_ref, both_ref, resid_ref, rayleigh_ref):
    vecs, edge = resid_ref.shape
    inverse = inverse_ref[...]
    total = sum(ref[...] for ref in terms) / nodes
    turned = dot_nn(inverse, total[:, :vecs])
    square = jnp.sum(dot_nn(inverse, total[:, vecs:]) * inverse, axis=1, keepdims=True)
    q = dot_nt(turned, inverse)
    raw = dot_tn(q, both_ref[:, :edge]) - both_ref[:, edge:]
    resid_ref[...] = raw * residual_scale(q, square)
    row_ids = lax.broadcasted_iota(jnp.int32, (vecs, vecs), 0)
    lane_ids = lax.broadcasted_iota(jnp.int32, (vecs, vecs), 1)
    rayleigh_ref[...] = jnp.where(row_ids == lane_ids, 1.0, 0.0) - q


def solve_kernel(parts, *refs):
    part_refs, inverse_ref, blocks_ref = refs[:parts], refs[parts], refs[parts + 1]
    vecs, edge = part_refs[0].shape
    solved = dot_nn(inverse_ref[...], jnp.concatenate([ref[...] for ref in part_refs], axis=1))
    for i in range(parts):
        blocks_ref[i * vecs : (i + 1) * vecs, :] = solved[:, i * edge : (i + 1) * edge].astype(bf16)


def cross_kernel(nodes, parts, *refs):
    part_refs, (basis_ref, search_ref, cross_ref, wide_ref) = refs[:parts], refs[parts:]
    vecs = wide_ref.shape[0]
    edge = part_refs[0].shape[1]
    at = 0
    for ref in part_refs:
        for i in range(ref.shape[0] // vecs):
            wide_ref[:, at : at + edge] = ref[i * vecs : (i + 1) * vecs, :]
            at += edge
    cross = lax.dot_general(
        basis_ref[...], wide_ref[...], (((1,), (1,)), ((), ())), preferred_element_type=f32
    )
    cross = cross[:vecs] + cross[vecs : 2 * vecs] + cross[2 * vecs :]
    values = wide_ref[...].astype(f32)
    square = jnp.sum(values * values, axis=1, keepdims=True)
    half = (vecs, vecs // 2)
    squares = [jnp.broadcast_to(square, half), jnp.broadcast_to(search_ref[:, :1], half)]
    cross_ref[...] = jnp.concatenate([cross, *squares], axis=1) / nodes


def swap(value, by, axis):
    size = lax.axis_size(axis)
    return lax.ppermute(value, axis, [(i, i ^ by) for i in range(size)])


def panel_terms(value):
    if lax.axis_size("panel") == 2:
        return [value, swap(value, 1, "panel")]
    return [lax.psum(value, "panel")]


def far_values(value, near):
    far = lax.axis_size("rows") // near
    return [value] + [swap(value, near * i, "rows") for i in range(far - 1, 0, -1)]


def near_values(held, near):
    return [held] + [swap(held, i, "rows") for i in range(near - 1, 0, -1)]


def body(
    adj_tiles,
    row_counts,
    tile_cols,
    start_basis,
    start_resid,
    start_search,
    ritz_basis,
    ritz_search,
):
    tile_set = adj_tiles[0, 0]
    counts = row_counts[0, 0]
    columns = tile_cols[0, 0]
    blocks, slots, edge = tile_set.shape[:3]
    vecs = start_basis.shape[0]
    rows, panels = lax.axis_size("rows"), lax.axis_size("panel")
    nodes = start_basis.shape[1] * rows * panels
    wide = rows * edge
    near = 4
    away = columns ^ lax.axis_index("rows")
    far = rows // near
    position = (-away % near) * far + -(away // near) % far
    in_use = jnp.arange(slots, dtype=jnp.int32)[None, :] < counts[:, None]
    slot_ids = jnp.where(in_use, position, rows).astype(jnp.int32)
    place = lax.axis_index("panel").astype(jnp.int32).reshape(1)

    if panels == 2:
        mine_outs = [((vecs, edge), f32)] * 2
    else:
        mine_outs = [((blocks, vecs, edge), f32)]
    stack_out = ((3 * vecs, wide), bf16)
    limit = 16 if wide <= 4096 else 56

    start = jnp.concatenate([start_basis, start_resid, start_search], axis=0)[None]
    sweeps = ritz_basis.shape[0]
    first_parts = far_values(start, near)
    held = jnp.concatenate(first_parts[:1] + first_parts[:0:-1], axis=0)
    held, slot_ids, tile_set, ritz_basis, ritz_search = lax.optimization_barrier(
        (held, slot_ids, tile_set, ritz_basis, ritz_search)
    )
    parts = near_values(held, near)
    dense, = call(
        layout_kernel, [((wide, blocks * edge), bf16)], [slot_ids, tile_set], smem=(0,), limit=limit
    )
    ritz = [(ritz_basis[sweep], ritz_search[sweep]) for sweep in range(sweeps)]
    parts, dense, ritz = lax.optimization_barrier((parts, dense, ritz))
    state = None
    for sweep in range(sweeps):
        last = sweep == sweeps - 1
        mixing, seeking = ritz[sweep]
        if state is None:
            stack, *mine = call(
                functools.partial(first_kernel, near),
                [stack_out] + mine_outs,
                [place, dense, mixing] + parts,
                smem=(0,),
                limit=limit,
            )
        else:
            crosses, basis, wide_adj, search, image = state
            count = len(crosses)

            def kernel_mix(p, m, *refs):
                mix_kernel(p, m, refs[:count], *refs[count:])

            mine = call(
                kernel_mix, mine_outs, [place, mixing] + crosses + [image], smem=(0,), limit=limit
            )
        own_out = ((vecs, edge), f32)
        pack_out = ((vecs, 2 * vecs), f32)
        if state is None:
            pack, = call(gram_kernel, [pack_out], [stack, mixing], limit=limit)
        else:

            def kernel_stack(m, *refs):
                stack_kernel(last, m, refs[:count], *refs[count:])

            pack, *rest = call(
                kernel_stack,
                [pack_out] + ([own_out, own_out] if last else [stack_out]),
                [mixing] + crosses + [basis, wide_adj, search] + [seeking] * last,
                limit=limit,
                scratch=[stack_out] * last,
            )
            stack = rest[0]
        if panels == 2:
            other = swap(mine[1], 1, "panel")
            other, pack = lax.optimization_barrier((other, pack))
            rotated_adj = mine[0] + other
        else:
            rotated_adj = lax.psum_scatter(mine[0], "panel", scatter_dimension=0, tiled=True)[0]
        packs = panel_terms(pack)
        pack_count = len(packs)

        def kernel_factor(*refs):
            factor_kernel(nodes, refs[:pack_count], *refs[pack_count:])

        inverse, *scale = call(
            kernel_factor, [((vecs, vecs), f32)] + [((vecs, 2 * vecs), f32)] * last, packs
        )
        if last:
            break
        far_parts = far_values(rotated_adj, near)
        far_parts, inverse = lax.optimization_barrier((far_parts, inverse))
        held, = call(
            functools.partial(solve_kernel, len(far_parts)),
            [((len(far_parts) * vecs, edge), bf16)],
            far_parts + [inverse],
            limit=limit,
        )
        adj_parts = near_values(held, near)
        basis, search, square = call(
            basis_kernel,
            [((3 * vecs, wide), bf16), ((vecs, wide), f32), own_out],
            [inverse, stack, mixing, seeking],
            limit=limit,
        )
        cross, wide_adj = call(
            functools.partial(cross_kernel, nodes, near),
            [pack_out, ((vecs, wide), bf16)],
            adj_parts + [basis, square],
            limit=limit,
        )
        image, = call(
            ahead_kernel,
            [((3 * vecs, blocks * edge), f32)],
            [basis, wide_adj, search, dense],
            limit=limit,
        )
        state = (panel_terms(cross), basis, wide_adj, search, image)

    search, rotated = rest
    terms, = call(terms_kernel, [((vecs, 2 * vecs), f32)], [rotated, rotated_adj])
    far_parts, inverse = lax.optimization_barrier((far_values(terms, near), inverse))
    own_basis, own_dirs, both = call(
        own_kernel,
        [own_out, own_out, ((vecs, 2 * edge), f32)],
        [inverse, *scale, rotated, rotated_adj, search],
    )
    terms = panel_terms(sum(near_values(sum(far_parts), near)[::-1]))
    count = len(terms)

    def kernel_last(*refs):
        last_kernel(nodes, refs[:count], *refs[count:])

    resid, rayleigh = call(
        kernel_last, [own_out, ((vecs, vecs), f32)], terms + [inverse, both]
    )
    return (own_basis, resid, own_dirs, rayleigh)


def solution(mesh):
    return jax.shard_map(
        body,
        mesh=mesh,
        in_specs=(
            P("rows", "panel", None, None, None, None),
            P("rows", "panel", None),
            P("rows", "panel", None, None),
            P(None, ("rows", "panel")),
            P(None, ("rows", "panel")),
            P(None, ("rows", "panel")),
            P(),
            P(),
        ),
        out_specs=(
            P(None, ("rows", "panel")),
            P(None, ("rows", "panel")),
            P(None, ("rows", "panel")),
            P(),
        ),
        check_vma=False,
    )
```

```python
import functools

import jax
import jax.numpy as jnp
from jax import lax
from jax.experimental import pallas as pl
from jax.experimental.pallas import tpu as pltpu
from jax.sharding import PartitionSpec as P

epsilon = 1e-06
highest = lax.Precision.HIGHEST
f32 = jnp.float32
bf16 = jnp.bfloat16


def call(kernel, outs, args, smem=(), limit=16, scratch=()):
    specs = [
        pl.BlockSpec(memory_space=pltpu.SMEM if i in smem else pltpu.VMEM) for i in range(len(args))
    ]
    return pl.pallas_call(
        kernel,
        out_shape=[jax.ShapeDtypeStruct(shape, kind) for shape, kind in outs],
        in_specs=specs,
        out_specs=[pl.BlockSpec(memory_space=pltpu.VMEM) for _ in outs],
        scratch_shapes=[pltpu.VMEM(shape, kind) for shape, kind in scratch],
        compiler_params=pltpu.CompilerParams(vmem_limit_bytes=limit << 20),
    )(*args)


def pieces(value):
    high = value.astype(bf16)
    rest = value - high.astype(f32)
    middle = rest.astype(bf16)
    low = (rest - middle.astype(f32)).astype(bf16)
    return jnp.concatenate([high, middle, low], axis=0)


def halves(value):
    high = value.astype(bf16)
    return high, (value - high.astype(f32)).astype(bf16)


def times_stack(weights, stack):
    rows = weights.shape[0]
    parts = jnp.dot(pieces(weights), stack, preferred_element_type=f32)
    return parts[:rows] + parts[rows : 2 * rows] + parts[2 * rows :]


def dot_nt(left, right):
    return lax.dot_general(
        left, right, (((1,), (1,)), ((), ())), precision=highest, preferred_element_type=f32
    )


def dot_tn(left, right):
    return lax.dot_general(
        left, right, (((0,), (0,)), ((), ())), precision=highest, preferred_element_type=f32
    )


def dot_nn(left, right):
    return jnp.dot(left, right, precision=highest, preferred_element_type=f32)


def layout_kernel(slots_ref, tiles_ref, dense_ref):
    blocks, slots, edge = tiles_ref.shape[:3]
    many = dense_ref.shape[0] // edge
    dense_ref[...] = jnp.zeros_like(dense_ref)
    for b in range(blocks):
        for s in range(slots):

            @pl.when(slots_ref[b, s] < many)
            def _():
                start = pl.multiple_of(slots_ref[b, s] * edge, edge)
                dense_ref[pl.ds(start, edge), b * edge : (b + 1) * edge] = tiles_ref[b, s].T


def send_parts(place_ref, mix_ref, image, mine_refs):
    edge = mine_refs[0].shape[-1]
    vecs = mix_ref.shape[0]
    high, low = halves(image)
    weights = jnp.concatenate(halves(mix_ref[...]), axis=0)
    mixed = jnp.dot(weights, high, preferred_element_type=f32)
    mixed = mixed[:vecs] + mixed[vecs:] + jnp.dot(weights[:vecs], low, preferred_element_type=f32)
    if len(mine_refs) == 2:
        first = place_ref[0] == 0
        low, high = mixed[:, :edge], mixed[:, edge:]
        mine_refs[0][...] = jnp.where(first, low, high)
        mine_refs[1][...] = jnp.where(first, high, low)
    else:
        for b in range(mine_refs[0].shape[0]):
            mine_refs[0][b] = mixed[:, b * edge : (b + 1) * edge]


def first_kernel(parts, place_ref, dense_ref, mix_ref, *refs):
    part_refs, stack_ref, mine_refs = refs[:parts], refs[parts], refs[parts + 1 :]
    edge = mine_refs[0].shape[-1]
    at = 0
    for ref in part_refs:
        far = ref.shape[0]
        for i in range(far):
            stack_ref[:, at : at + edge] = ref[-i % far]
            at += edge
    image = jnp.dot(stack_ref[...], dense_ref[...], preferred_element_type=f32)
    send_parts(place_ref, mix_ref, image, mine_refs)


def residual_scale(q, square):
    return lax.rsqrt(jnp.maximum(square - jnp.sum((q * q).T, axis=1, keepdims=True), 0.0) + epsilon)


def cross_terms(crosses):
    both = sum(ref[...] for ref in crosses)
    vecs = both.shape[0]
    q = both[:, :vecs]
    scale = residual_scale(q, both[:, vecs : vecs + 1])
    at = vecs + vecs // 2
    return q, scale, lax.rsqrt(both[:, at : at + 1] + epsilon)


def ahead_kernel(basis_ref, wide_ref, search_ref, dense_ref, image_ref):
    vecs = wide_ref.shape[0]
    rows = jnp.concatenate([basis_ref[:vecs], wide_ref[...], search_ref[...].astype(bf16)], axis=0)
    image_ref[...] = jnp.dot(rows, dense_ref[...], preferred_element_type=f32)


def mix_kernel(place_ref, mix_ref, crosses, image_ref, *mine_refs):
    vecs = mix_ref.shape[0]
    q, scale, step = cross_terms(crosses)
    basis = image_ref[:vecs]
    q_high, q_low = halves(q)
    high, low = halves(basis)
    raw = lax.dot_general(
        jnp.concatenate([q_high, q_high, q_low], axis=0),
        jnp.concatenate([high, low, high], axis=0),
        (((0,), (0,)), ((), ())),
        preferred_element_type=f32,
    )
    raw = raw - image_ref[vecs : 2 * vecs]
    image = jnp.concatenate([basis, raw * scale, image_ref[2 * vecs :] * step], axis=0)
    send_parts(place_ref, mix_ref, image, mine_refs)


def gram_terms(stack, mix_ref, pack_ref, search_refs):
    vecs = mix_ref.shape[0]
    rotated = times_stack(mix_ref[...], stack)
    square = jnp.zeros((vecs, vecs), f32)
    if search_refs:
        weights_ref, search_out, own_rotated = search_refs
        edge = search_out.shape[1]
        search = times_stack(weights_ref[...], stack[vecs:])
        search_out[...] = search[:, :edge]
        own_rotated[...] = rotated[:, :edge]
        square = jnp.broadcast_to(jnp.sum(search * search, axis=1, keepdims=True), square.shape)
    split = jnp.concatenate(halves(rotated), axis=0)
    gram = lax.dot_general(split, split, (((1,), (1,)), ((), ())), preferred_element_type=f32)
    gram = gram[:vecs] + gram[vecs:]
    pack_ref[...] = jnp.concatenate([gram[:, :vecs] + gram[:, vecs:], square], axis=1)


def gram_kernel(stack_ref, mix_ref, pack_ref):
    gram_terms(stack_ref[...], mix_ref, pack_ref, ())


def stack_kernel(last, mix_ref, crosses, basis_ref, wide_ref, found_ref, *refs):
    vecs = wide_ref.shape[0]
    if last:
        weights, pack_ref, outs, stack_ref = refs[:1], refs[1], refs[2:4], refs[4]
    else:
        weights, pack_ref, outs, stack_ref = (), refs[0], (), refs[1]
    q, scale, step = cross_terms(crosses)
    terms = jnp.concatenate([*halves(q), q.astype(bf16)], axis=0)
    basis = jnp.concatenate([basis_ref[:vecs], basis_ref[:vecs], basis_ref[vecs : 2 * vecs]], axis=0)
    part = lax.dot_general(terms, basis, (((0,), (0,)), ((), ())), preferred_element_type=f32)
    stack_ref[:vecs] = basis_ref[:vecs]
    stack_ref[vecs : 2 * vecs] = ((part - wide_ref[...].astype(f32)) * scale).astype(bf16)
    stack_ref[2 * vecs :] = (found_ref[...] * step).astype(bf16)
    gram_terms(stack_ref[...], mix_ref, pack_ref, (*weights, *outs))


def factor_kernel(nodes, packs, inverse_ref, *scale_ref):
    vecs = inverse_ref.shape[0]
    total = sum(ref[...] for ref in packs) / nodes
    if scale_ref:
        scale_ref[0][...] = lax.rsqrt(jnp.maximum(total, 0.0) + epsilon)
    row_ids = lax.broadcasted_iota(jnp.int32, (vecs, 2 * vecs), 0)
    lane_ids = lax.broadcasted_iota(jnp.int32, (vecs, 2 * vecs), 1)
    diagonal = jnp.where(lane_ids == row_ids, total, 0.0)
    across = lax.rsqrt(jnp.sum(diagonal, axis=0, keepdims=True))
    height, step = 8, 4
    shape = (height, 2 * vecs)
    ids = lax.broadcasted_iota(jnp.int32, shape, 0)
    lanes = lax.broadcasted_iota(jnp.int32, shape, 1)

    def lane(tile, index):
        return jnp.take_along_axis(tile, index, axis=1)

    tiles = []
    for t in range(0, vecs, height):
        tile = total[t : t + height]
        down = lax.rsqrt(lane(tile, ids + t))
        unit = jnp.where(lanes == ids + (t + vecs), down, 0.0)
        tiles.append(jnp.where(lanes < vecs, tile * down * across, unit))
    done = [None] * len(tiles)
    for j in range(0, vecs, step):
        t, s = divmod(j, height)
        rows = [jnp.broadcast_to(tiles[t][s + m : s + m + 1], shape) for m in range(step)]
        columns = [
            [lane(tile, jnp.full(shape, k, jnp.int32)) for k in range(j, j + step)] for tile in tiles[t:]
        ]

        def pivot(m, n):
            return jnp.broadcast_to(columns[0][n][s + m : s + m + 1], shape)

        p00, p10, p11 = pivot(0, 0), pivot(1, 0), pivot(1, 1)
        q20, q21, q30, q31 = pivot(2, 0), pivot(2, 1), pivot(3, 0), pivot(3, 1)
        w22, w32, w33 = pivot(2, 2), pivot(3, 2), pivot(3, 3)
        scale = 1.0 / (p00 * p11 - p10 * p10)
        i00, i10, i11 = p11 * scale, -p10 * scale, p00 * scale
        e20, e21 = q20 * i00 + q21 * i10, q20 * i10 + q21 * i11
        e30, e31 = q30 * i00 + q31 * i10, q30 * i10 + q31 * i11
        s22 = w22 - (e20 * q20 + e21 * q21)
        s32 = w32 - (e30 * q20 + e31 * q21)
        s33 = w33 - (e30 * q30 + e31 * q31)
        scale = 1.0 / (s22 * s33 - s32 * s32)
        u22, u32, u33 = s33 * scale, -s32 * scale, s22 * scale
        below2 = rows[2] - (e20 * rows[0] + e21 * rows[1])
        below3 = rows[3] - (e30 * rows[0] + e31 * rows[1])
        y2, y3 = below2 * u22 + below3 * u32, below2 * u32 + below3 * u33
        z0 = rows[0] - (y2 * q20 + y3 * q30)
        z1 = rows[1] - (y2 * q21 + y3 * q31)
        y0, y1 = z0 * i00 + z1 * i10, z0 * i10 + z1 * i11
        for u in range(t, len(tiles)):
            if u == t and s + step == height:
                continue
            x0, x1, x2, x3 = columns[u - t]
            less = (x0 * y0 + x1 * y1) + (x2 * y2 + x3 * y3)
            if u == t:
                less = jnp.where(ids >= s + step, less, 0.0)
            tiles[u] = tiles[u] - less
        ratio = p10 / p00
        finished = [rows[0], rows[1] - ratio * rows[0], below2, below3 - (s32 / s22) * below2]
        roots = [p00, p11 - ratio * p10, s22, s33 - (s32 / s22) * s32]
        for m in range(step):
            value = finished[m] * lax.rsqrt(roots[m])
            done[t] = value if done[t] is None else jnp.where(ids >= s + m, value, done[t])
    inverse_ref[...] = jnp.concatenate(done, axis=0)[:, vecs:]


def basis_kernel(inverse_ref, stack_ref, mix_ref, weights_ref, basis_ref, search_ref, square_ref):
    vecs = mix_ref.shape[0]
    search = times_stack(weights_ref[...], stack_ref[vecs:])
    search_ref[...] = search
    square_ref[...] = jnp.broadcast_to(jnp.sum(search * search, axis=1, keepdims=True), square_ref.shape)
    basis = times_stack(dot_nn(inverse_ref[...], mix_ref[...]), stack_ref[...])
    basis_ref[...] = pieces(basis)


def terms_kernel(rotated_ref, adj_ref, terms_ref):
    adj = adj_ref[...]
    terms_ref[...] = jnp.concatenate([dot_nt(rotated_ref[...], adj), dot_nt(adj, adj)], axis=1)


def own_kernel(inverse_ref, scale_ref, rotated_ref, adj_ref, search_ref, basis_ref, dirs_ref, both_ref):
    vecs, edge = rotated_ref.shape
    both = dot_nn(inverse_ref[...], jnp.concatenate([rotated_ref[...], adj_ref[...]], axis=1))
    both_ref[...] = both
    basis_ref[...] = both[:, :edge]
    dirs_ref[...] = search_ref[...] * scale_ref[:, vecs : vecs + 1]


def last_kernel(nodes, terms, inverse_ref, both_ref, resid_ref, rayleigh_ref):
    vecs, edge = resid_ref.shape
    inverse = inverse_ref[...]
    total = sum(ref[...] for ref in terms) / nodes
    turned = dot_nn(inverse, total[:, :vecs])
    square = jnp.sum(dot_nn(inverse, total[:, vecs:]) * inverse, axis=1, keepdims=True)
    q = dot_nt(turned, inverse)
    raw = dot_tn(q, both_ref[:, :edge]) - both_ref[:, edge:]
    resid_ref[...] = raw * residual_scale(q, square)
    row_ids = lax.broadcasted_iota(jnp.int32, (vecs, vecs), 0)
    lane_ids = lax.broadcasted_iota(jnp.int32, (vecs, vecs), 1)
    rayleigh_ref[...] = jnp.where(row_ids == lane_ids, 1.0, 0.0) - q


def solve_kernel(parts, *refs):
    part_refs, inverse_ref, blocks_ref = refs[:parts], refs[parts], refs[parts + 1]
    vecs, edge = part_refs[0].shape
    solved = dot_nn(inverse_ref[...], jnp.concatenate([ref[...] for ref in part_refs], axis=1))
    for i in range(parts):
        blocks_ref[i * vecs : (i + 1) * vecs, :] = solved[:, i * edge : (i + 1) * edge].astype(bf16)


def cross_kernel(nodes, parts, *refs):
    part_refs, (basis_ref, search_ref, cross_ref, wide_ref) = refs[:parts], refs[parts:]
    vecs = wide_ref.shape[0]
    edge = part_refs[0].shape[1]
    at = 0
    for ref in part_refs:
        for i in range(ref.shape[0] // vecs):
            wide_ref[:, at : at + edge] = ref[i * vecs : (i + 1) * vecs, :]
            at += edge
    cross = lax.dot_general(
        basis_ref[...], wide_ref[...], (((1,), (1,)), ((), ())), preferred_element_type=f32
    )
    cross = cross[:vecs] + cross[vecs : 2 * vecs] + cross[2 * vecs :]
    values = wide_ref[...].astype(f32)
    square = jnp.sum(values * values, axis=1, keepdims=True)
    half = (vecs, vecs // 2)
    squares = [jnp.broadcast_to(square, half), jnp.broadcast_to(search_ref[:, :1], half)]
    cross_ref[...] = jnp.concatenate([cross, *squares], axis=1) / nodes


def swap(value, by, axis):
    size = lax.axis_size(axis)
    return lax.ppermute(value, axis, [(i, i ^ by) for i in range(size)])


def panel_terms(value):
    if lax.axis_size("panel") == 2:
        return [value, swap(value, 1, "panel")]
    return [lax.psum(value, "panel")]


def far_values(value, near):
    far = lax.axis_size("rows") // near
    return [value] + [swap(value, near * i, "rows") for i in range(far - 1, 0, -1)]


def near_values(held, near):
    return [held] + [swap(held, i, "rows") for i in range(near - 1, 0, -1)]


def body(
    adj_tiles,
    row_counts,
    tile_cols,
    start_basis,
    start_resid,
    start_search,
    ritz_basis,
    ritz_search,
):
    tile_set = adj_tiles[0, 0]
    counts = row_counts[0, 0]
    columns = tile_cols[0, 0]
    blocks, slots, edge = tile_set.shape[:3]
    vecs = start_basis.shape[0]
    rows, panels = lax.axis_size("rows"), lax.axis_size("panel")
    nodes = start_basis.shape[1] * rows * panels
    wide = rows * edge
    near = 4
    place = lax.axis_index("panel").astype(jnp.int32).reshape(1)

    if panels == 2:
        mine_outs = [((vecs, edge), f32)] * 2
    else:
        mine_outs = [((blocks, vecs, edge), f32)]
    stack_out = ((3 * vecs, wide), bf16)
    limit = 16 if wide <= 4096 else 56

    start = jnp.concatenate([start_basis, start_resid, start_search], axis=0)[None]
    sweeps = ritz_basis.shape[0]
    first_parts = far_values(start, near)
    held = jnp.concatenate(first_parts[:1] + first_parts[:0:-1], axis=0)
    held, counts, columns, tile_set, ritz_basis, ritz_search = lax.optimization_barrier(
        (held, counts, columns, tile_set, ritz_basis, ritz_search)
    )
    away = columns ^ lax.axis_index("rows")
    far = rows // near
    position = (-away % near) * far + -(away // near) % far
    in_use = jnp.arange(slots, dtype=jnp.int32)[None, :] < counts[:, None]
    slot_ids = jnp.where(in_use, position, rows).astype(jnp.int32)
    parts = near_values(held, near)
    dense, = call(
        layout_kernel, [((wide, blocks * edge), bf16)], [slot_ids, tile_set], smem=(0,), limit=limit
    )
    ritz = [(ritz_basis[sweep], ritz_search[sweep]) for sweep in range(sweeps)]
    parts, dense, ritz = lax.optimization_barrier((parts, dense, ritz))
    state = None
    for sweep in range(sweeps):
        last = sweep == sweeps - 1
        mixing, seeking = ritz[sweep]
        if state is None:
            stack, *mine = call(
                functools.partial(first_kernel, near),
                [stack_out] + mine_outs,
                [place, dense, mixing] + parts,
                smem=(0,),
                limit=limit,
            )
        else:
            crosses, basis, wide_adj, search, image = state
            count = len(crosses)

            def kernel_mix(p, m, *refs):
                mix_kernel(p, m, refs[:count], *refs[count:])

            mine = call(
                kernel_mix, mine_outs, [place, mixing] + crosses + [image], smem=(0,), limit=limit
            )
        own_out = ((vecs, edge), f32)
        pack_out = ((vecs, 2 * vecs), f32)
        if state is None:
            pack, = call(gram_kernel, [pack_out], [stack, mixing], limit=limit)
        else:

            def kernel_stack(m, *refs):
                stack_kernel(last, m, refs[:count], *refs[count:])

            pack, *rest = call(
                kernel_stack,
                [pack_out] + ([own_out, own_out] if last else [stack_out]),
                [mixing] + crosses + [basis, wide_adj, search] + [seeking] * last,
                limit=limit,
                scratch=[stack_out] * last,
            )
            stack = rest[0]
        if panels == 2:
            other = swap(mine[1], 1, "panel")
            other, pack = lax.optimization_barrier((other, pack))
            rotated_adj = mine[0] + other
        else:
            rotated_adj = lax.psum_scatter(mine[0], "panel", scatter_dimension=0, tiled=True)[0]
        packs = panel_terms(pack)
        pack_count = len(packs)

        def kernel_factor(*refs):
            factor_kernel(nodes, refs[:pack_count], *refs[pack_count:])

        inverse, *scale = call(
            kernel_factor, [((vecs, vecs), f32)] + [((vecs, 2 * vecs), f32)] * last, packs
        )
        if last:
            break
        far_parts = far_values(rotated_adj, near)
        far_parts, inverse = lax.optimization_barrier((far_parts, inverse))
        held, = call(
            functools.partial(solve_kernel, len(far_parts)),
            [((len(far_parts) * vecs, edge), bf16)],
            far_parts + [inverse],
            limit=limit,
        )
        adj_parts = near_values(held, near)
        basis, search, square = call(
            basis_kernel,
            [((3 * vecs, wide), bf16), ((vecs, wide), f32), own_out],
            [inverse, stack, mixing, seeking],
            limit=limit,
        )
        cross, wide_adj = call(
            functools.partial(cross_kernel, nodes, near),
            [pack_out, ((vecs, wide), bf16)],
            adj_parts + [basis, square],
            limit=limit,
        )
        image, = call(
            ahead_kernel,
            [((3 * vecs, blocks * edge), f32)],
            [basis, wide_adj, search, dense],
            limit=limit,
        )
        state = (panel_terms(cross), basis, wide_adj, search, image)

    search, rotated = rest
    terms, = call(terms_kernel, [((vecs, 2 * vecs), f32)], [rotated, rotated_adj])
    far_parts, inverse = lax.optimization_barrier((far_values(terms, near), inverse))
    own_basis, own_dirs, both = call(
        own_kernel,
        [own_out, own_out, ((vecs, 2 * edge), f32)],
        [inverse, *scale, rotated, rotated_adj, search],
    )
    terms = panel_terms(sum(near_values(sum(far_parts), near)[::-1]))
    count = len(terms)

    def kernel_last(*refs):
        last_kernel(nodes, refs[:count], *refs[count:])

    resid, rayleigh = call(
        kernel_last, [own_out, ((vecs, vecs), f32)], terms + [inverse, both]
    )
    return (own_basis, resid, own_dirs, rayleigh)


def solution(mesh):
    return jax.shard_map(
        body,
        mesh=mesh,
        in_specs=(
            P("rows", "panel", None, None, None, None),
            P("rows", "panel", None),
            P("rows", "panel", None, None),
            P(None, ("rows", "panel")),
            P(None, ("rows", "panel")),
            P(None, ("rows", "panel")),
            P(),
            P(),
        ),
        out_specs=(
            P(None, ("rows", "panel")),
            P(None, ("rows", "panel")),
            P(None, ("rows", "panel")),
            P(),
        ),
        check_vma=False,
    )
```

```python
import functools

import jax
import jax.numpy as jnp
from jax import lax
from jax.experimental import pallas as pl
from jax.experimental.pallas import tpu as pltpu
from jax.sharding import PartitionSpec as P

epsilon = 1e-06
highest = lax.Precision.HIGHEST
f32 = jnp.float32
bf16 = jnp.bfloat16


def call(kernel, outs, args, smem=(), limit=16, scratch=()):
    specs = [
        pl.BlockSpec(memory_space=pltpu.SMEM if i in smem else pltpu.VMEM) for i in range(len(args))
    ]
    return pl.pallas_call(
        kernel,
        out_shape=[jax.ShapeDtypeStruct(shape, kind) for shape, kind in outs],
        in_specs=specs,
        out_specs=[pl.BlockSpec(memory_space=pltpu.VMEM) for _ in outs],
        scratch_shapes=[pltpu.VMEM(shape, kind) for shape, kind in scratch],
        compiler_params=pltpu.CompilerParams(vmem_limit_bytes=limit << 20),
    )(*args)


def pieces(value):
    high = value.astype(bf16)
    rest = value - high.astype(f32)
    middle = rest.astype(bf16)
    low = (rest - middle.astype(f32)).astype(bf16)
    return jnp.concatenate([high, middle, low], axis=0)


def halves(value):
    high = value.astype(bf16)
    return high, (value - high.astype(f32)).astype(bf16)


def times_stack(weights, stack):
    rows = weights.shape[0]
    parts = jnp.dot(pieces(weights), stack, preferred_element_type=f32)
    return parts[:rows] + parts[rows : 2 * rows] + parts[2 * rows :]


def dot_nt(left, right):
    return lax.dot_general(
        left, right, (((1,), (1,)), ((), ())), precision=highest, preferred_element_type=f32
    )


def dot_tn(left, right):
    return lax.dot_general(
        left, right, (((0,), (0,)), ((), ())), precision=highest, preferred_element_type=f32
    )


def dot_nn(left, right):
    return jnp.dot(left, right, precision=highest, preferred_element_type=f32)


def layout_kernel(slots_ref, tiles_ref, dense_ref):
    blocks, slots, edge = tiles_ref.shape[:3]
    many = dense_ref.shape[0] // edge
    dense_ref[...] = jnp.zeros_like(dense_ref)
    for b in range(blocks):
        for s in range(slots):

            @pl.when(slots_ref[b, s] < many)
            def _():
                start = pl.multiple_of(slots_ref[b, s] * edge, edge)
                dense_ref[pl.ds(start, edge), b * edge : (b + 1) * edge] = tiles_ref[b, s].T


def send_parts(place_ref, mix_ref, image, mine_refs):
    edge = mine_refs[0].shape[-1]
    vecs = mix_ref.shape[0]
    high, low = halves(image)
    weights = jnp.concatenate(halves(mix_ref[...]), axis=0)
    mixed = jnp.dot(weights, high, preferred_element_type=f32)
    mixed = mixed[:vecs] + mixed[vecs:] + jnp.dot(weights[:vecs], low, preferred_element_type=f32)
    if len(mine_refs) == 2:
        first = place_ref[0] == 0
        low, high = mixed[:, :edge], mixed[:, edge:]
        mine_refs[0][...] = jnp.where(first, low, high)
        mine_refs[1][...] = jnp.where(first, high, low)
    else:
        for b in range(mine_refs[0].shape[0]):
            mine_refs[0][b] = mixed[:, b * edge : (b + 1) * edge]


def first_kernel(parts, place_ref, dense_ref, mix_ref, *refs):
    part_refs, stack_ref, mine_refs = refs[:parts], refs[parts], refs[parts + 1 :]
    edge = mine_refs[0].shape[-1]
    at = 0
    for ref in part_refs:
        far = ref.shape[0]
        for i in range(far):
            stack_ref[:, at : at + edge] = ref[-i % far]
            at += edge
    image = jnp.dot(stack_ref[...], dense_ref[...], preferred_element_type=f32)
    send_parts(place_ref, mix_ref, image, mine_refs)


def residual_scale(q, square):
    return lax.rsqrt(jnp.maximum(square - jnp.sum((q * q).T, axis=1, keepdims=True), 0.0) + epsilon)


def cross_terms(crosses):
    both = sum(ref[...] for ref in crosses)
    vecs = both.shape[0]
    q = both[:, :vecs]
    scale = residual_scale(q, both[:, vecs : vecs + 1])
    at = vecs + vecs // 2
    return q, scale, lax.rsqrt(both[:, at : at + 1] + epsilon)


def ahead_kernel(basis_ref, wide_ref, search_ref, dense_ref, image_ref):
    vecs = wide_ref.shape[0]
    rows = jnp.concatenate([basis_ref[:vecs], wide_ref[...], search_ref[...].astype(bf16)], axis=0)
    image_ref[...] = jnp.dot(rows, dense_ref[...], preferred_element_type=f32)


def mix_kernel(place_ref, mix_ref, crosses, image_ref, *mine_refs):
    vecs = mix_ref.shape[0]
    q, scale, step = cross_terms(crosses)
    basis = image_ref[:vecs]
    q_high, q_low = halves(q)
    high, low = halves(basis)
    raw = lax.dot_general(
        jnp.concatenate([q_high, q_high, q_low], axis=0),
        jnp.concatenate([high, low, high], axis=0),
        (((0,), (0,)), ((), ())),
        preferred_element_type=f32,
    )
    raw = raw - image_ref[vecs : 2 * vecs]
    image = jnp.concatenate([basis, raw * scale, image_ref[2 * vecs :] * step], axis=0)
    send_parts(place_ref, mix_ref, image, mine_refs)


def gram_terms(stack, mix_ref, pack_ref, search_refs):
    vecs = mix_ref.shape[0]
    rotated = times_stack(mix_ref[...], stack)
    square = jnp.zeros((vecs, vecs), f32)
    if search_refs:
        weights_ref, search_out, own_rotated = search_refs
        edge = search_out.shape[1]
        search = times_stack(weights_ref[...], stack[vecs:])
        search_out[...] = search[:, :edge]
        own_rotated[...] = rotated[:, :edge]
        square = jnp.broadcast_to(jnp.sum(search * search, axis=1, keepdims=True), square.shape)
    split = jnp.concatenate(halves(rotated), axis=0)
    gram = lax.dot_general(split, split, (((1,), (1,)), ((), ())), preferred_element_type=f32)
    gram = gram[:vecs] + gram[vecs:]
    pack_ref[...] = jnp.concatenate([gram[:, :vecs] + gram[:, vecs:], square], axis=1)


def gram_kernel(stack_ref, mix_ref, pack_ref):
    gram_terms(stack_ref[...], mix_ref, pack_ref, ())


def stack_kernel(last, mix_ref, crosses, basis_ref, wide_ref, found_ref, *refs):
    vecs = wide_ref.shape[0]
    if last:
        weights, pack_ref, outs, stack_ref = refs[:1], refs[1], refs[2:4], refs[4]
    else:
        weights, pack_ref, outs, stack_ref = (), refs[0], (), refs[1]
    q, scale, step = cross_terms(crosses)
    terms = jnp.concatenate([*halves(q), q.astype(bf16)], axis=0)
    basis = jnp.concatenate([basis_ref[:vecs], basis_ref[:vecs], basis_ref[vecs : 2 * vecs]], axis=0)
    part = lax.dot_general(terms, basis, (((0,), (0,)), ((), ())), preferred_element_type=f32)
    stack_ref[:vecs] = basis_ref[:vecs]
    stack_ref[vecs : 2 * vecs] = ((part - wide_ref[...].astype(f32)) * scale).astype(bf16)
    stack_ref[2 * vecs :] = (found_ref[...] * step).astype(bf16)
    gram_terms(stack_ref[...], mix_ref, pack_ref, (*weights, *outs))


def factor_kernel(nodes, packs, inverse_ref, *scale_ref):
    vecs = inverse_ref.shape[0]
    total = sum(ref[...] for ref in packs) / nodes
    if scale_ref:
        scale_ref[0][...] = lax.rsqrt(jnp.maximum(total, 0.0) + epsilon)
    row_ids = lax.broadcasted_iota(jnp.int32, (vecs, 2 * vecs), 0)
    lane_ids = lax.broadcasted_iota(jnp.int32, (vecs, 2 * vecs), 1)
    diagonal = jnp.where(lane_ids == row_ids, total, 0.0)
    across = lax.rsqrt(jnp.sum(diagonal, axis=0, keepdims=True))
    height, step = 8, 4
    shape = (height, 2 * vecs)
    ids = lax.broadcasted_iota(jnp.int32, shape, 0)
    lanes = lax.broadcasted_iota(jnp.int32, shape, 1)

    def lane(tile, index):
        return jnp.take_along_axis(tile, index, axis=1)

    tiles = []
    for t in range(0, vecs, height):
        tile = total[t : t + height]
        down = lax.rsqrt(lane(tile, ids + t))
        unit = jnp.where(lanes == ids + (t + vecs), down, 0.0)
        tiles.append(jnp.where(lanes < vecs, tile * down * across, unit))
    done = [None] * len(tiles)
    for j in range(0, vecs, step):
        t, s = divmod(j, height)
        rows = [jnp.broadcast_to(tiles[t][s + m : s + m + 1], shape) for m in range(step)]
        columns = [
            [lane(tile, jnp.full(shape, k, jnp.int32)) for k in range(j, j + step)] for tile in tiles[t:]
        ]

        def pivot(m, n):
            return jnp.broadcast_to(columns[0][n][s + m : s + m + 1], shape)

        p00, p10, p11 = pivot(0, 0), pivot(1, 0), pivot(1, 1)
        q20, q21, q30, q31 = pivot(2, 0), pivot(2, 1), pivot(3, 0), pivot(3, 1)
        w22, w32, w33 = pivot(2, 2), pivot(3, 2), pivot(3, 3)
        scale = 1.0 / (p00 * p11 - p10 * p10)
        i00, i10, i11 = p11 * scale, -p10 * scale, p00 * scale
        e20, e21 = q20 * i00 + q21 * i10, q20 * i10 + q21 * i11
        e30, e31 = q30 * i00 + q31 * i10, q30 * i10 + q31 * i11
        s22 = w22 - (e20 * q20 + e21 * q21)
        s32 = w32 - (e30 * q20 + e31 * q21)
        s33 = w33 - (e30 * q30 + e31 * q31)
        scale = 1.0 / (s22 * s33 - s32 * s32)
        u22, u32, u33 = s33 * scale, -s32 * scale, s22 * scale
        below2 = rows[2] - (e20 * rows[0] + e21 * rows[1])
        below3 = rows[3] - (e30 * rows[0] + e31 * rows[1])
        y2, y3 = below2 * u22 + below3 * u32, below2 * u32 + below3 * u33
        z0 = rows[0] - (y2 * q20 + y3 * q30)
        z1 = rows[1] - (y2 * q21 + y3 * q31)
        y0, y1 = z0 * i00 + z1 * i10, z0 * i10 + z1 * i11
        for u in range(t, len(tiles)):
            if u == t and s + step == height:
                continue
            x0, x1, x2, x3 = columns[u - t]
            less = (x0 * y0 + x1 * y1) + (x2 * y2 + x3 * y3)
            if u == t:
                less = jnp.where(ids >= s + step, less, 0.0)
            tiles[u] = tiles[u] - less
        ratio = p10 / p00
        finished = [rows[0], rows[1] - ratio * rows[0], below2, below3 - (s32 / s22) * below2]
        roots = [p00, p11 - ratio * p10, s22, s33 - (s32 / s22) * s32]
        for m in range(step):
            value = finished[m] * lax.rsqrt(roots[m])
            done[t] = value if done[t] is None else jnp.where(ids >= s + m, value, done[t])
    inverse_ref[...] = jnp.concatenate(done, axis=0)[:, vecs:]


def basis_kernel(inverse_ref, stack_ref, mix_ref, weights_ref, basis_ref, search_ref, square_ref):
    vecs = mix_ref.shape[0]
    search = times_stack(weights_ref[...], stack_ref[vecs:])
    search_ref[...] = search
    square_ref[...] = jnp.broadcast_to(jnp.sum(search * search, axis=1, keepdims=True), square_ref.shape)
    basis = times_stack(dot_nn(inverse_ref[...], mix_ref[...]), stack_ref[...])
    basis_ref[...] = jnp.concatenate(halves(basis), axis=0)


def terms_kernel(rotated_ref, adj_ref, terms_ref):
    adj = adj_ref[...]
    terms_ref[...] = jnp.concatenate([dot_nt(rotated_ref[...], adj), dot_nt(adj, adj)], axis=1)


def own_kernel(inverse_ref, scale_ref, rotated_ref, adj_ref, search_ref, basis_ref, dirs_ref, both_ref):
    vecs, edge = rotated_ref.shape
    both = dot_nn(inverse_ref[...], jnp.concatenate([rotated_ref[...], adj_ref[...]], axis=1))
    both_ref[...] = both
    basis_ref[...] = both[:, :edge]
    dirs_ref[...] = search_ref[...] * scale_ref[:, vecs : vecs + 1]


def last_kernel(nodes, terms, inverse_ref, both_ref, resid_ref, rayleigh_ref):
    vecs, edge = resid_ref.shape
    inverse = inverse_ref[...]
    total = sum(ref[...] for ref in terms) / nodes
    turned = dot_nn(inverse, total[:, :vecs])
    square = jnp.sum(dot_nn(inverse, total[:, vecs:]) * inverse, axis=1, keepdims=True)
    q = dot_nt(turned, inverse)
    raw = dot_tn(q, both_ref[:, :edge]) - both_ref[:, edge:]
    resid_ref[...] = raw * residual_scale(q, square)
    row_ids = lax.broadcasted_iota(jnp.int32, (vecs, vecs), 0)
    lane_ids = lax.broadcasted_iota(jnp.int32, (vecs, vecs), 1)
    rayleigh_ref[...] = jnp.where(row_ids == lane_ids, 1.0, 0.0) - q


def solve_kernel(parts, *refs):
    part_refs, inverse_ref, blocks_ref = refs[:parts], refs[parts], refs[parts + 1]
    vecs, edge = part_refs[0].shape
    solved = dot_nn(inverse_ref[...], jnp.concatenate([ref[...] for ref in part_refs], axis=1))
    for i in range(parts):
        blocks_ref[i * vecs : (i + 1) * vecs, :] = solved[:, i * edge : (i + 1) * edge].astype(bf16)


def cross_kernel(nodes, parts, *refs):
    part_refs, (basis_ref, search_ref, cross_ref, wide_ref) = refs[:parts], refs[parts:]
    vecs = wide_ref.shape[0]
    edge = part_refs[0].shape[1]
    at = 0
    for ref in part_refs:
        for i in range(ref.shape[0] // vecs):
            wide_ref[:, at : at + edge] = ref[i * vecs : (i + 1) * vecs, :]
            at += edge
    cross = lax.dot_general(
        basis_ref[...], wide_ref[...], (((1,), (1,)), ((), ())), preferred_element_type=f32
    )
    cross = cross[:vecs] + cross[vecs:]
    values = wide_ref[...].astype(f32)
    square = jnp.sum(values * values, axis=1, keepdims=True)
    half = (vecs, vecs // 2)
    squares = [jnp.broadcast_to(square, half), jnp.broadcast_to(search_ref[:, :1], half)]
    cross_ref[...] = jnp.concatenate([cross, *squares], axis=1) / nodes


def swap(value, by, axis):
    size = lax.axis_size(axis)
    return lax.ppermute(value, axis, [(i, i ^ by) for i in range(size)])


def panel_terms(value):
    if lax.axis_size("panel") == 2:
        return [value, swap(value, 1, "panel")]
    return [lax.psum(value, "panel")]


def far_values(value, near):
    far = lax.axis_size("rows") // near
    return [value] + [swap(value, near * i, "rows") for i in range(far - 1, 0, -1)]


def near_values(held, near):
    return [held] + [swap(held, i, "rows") for i in range(near - 1, 0, -1)]


def body(
    adj_tiles,
    row_counts,
    tile_cols,
    start_basis,
    start_resid,
    start_search,
    ritz_basis,
    ritz_search,
):
    tile_set = adj_tiles[0, 0]
    counts = row_counts[0, 0]
    columns = tile_cols[0, 0]
    blocks, slots, edge = tile_set.shape[:3]
    vecs = start_basis.shape[0]
    rows, panels = lax.axis_size("rows"), lax.axis_size("panel")
    nodes = start_basis.shape[1] * rows * panels
    wide = rows * edge
    near = 4
    place = lax.axis_index("panel").astype(jnp.int32).reshape(1)

    if panels == 2:
        mine_outs = [((vecs, edge), f32)] * 2
    else:
        mine_outs = [((blocks, vecs, edge), f32)]
    stack_out = ((3 * vecs, wide), bf16)
    limit = 16 if wide <= 4096 else 56

    start = jnp.concatenate([start_basis, start_resid, start_search], axis=0)[None]
    sweeps = ritz_basis.shape[0]
    first_parts = far_values(start, near)
    held = jnp.concatenate(first_parts[:1] + first_parts[:0:-1], axis=0)
    held, counts, columns, tile_set, ritz_basis, ritz_search = lax.optimization_barrier(
        (held, counts, columns, tile_set, ritz_basis, ritz_search)
    )
    away = columns ^ lax.axis_index("rows")
    far = rows // near
    position = (-away % near) * far + -(away // near) % far
    in_use = jnp.arange(slots, dtype=jnp.int32)[None, :] < counts[:, None]
    slot_ids = jnp.where(in_use, position, rows).astype(jnp.int32)
    parts = near_values(held, near)
    dense, = call(
        layout_kernel, [((wide, blocks * edge), bf16)], [slot_ids, tile_set], smem=(0,), limit=limit
    )
    ritz = [(ritz_basis[sweep], ritz_search[sweep]) for sweep in range(sweeps)]
    parts, dense, ritz = lax.optimization_barrier((parts, dense, ritz))
    state = None
    for sweep in range(sweeps):
        last = sweep == sweeps - 1
        mixing, seeking = ritz[sweep]
        if state is None:
            stack, *mine = call(
                functools.partial(first_kernel, near),
                [stack_out] + mine_outs,
                [place, dense, mixing] + parts,
                smem=(0,),
                limit=limit,
            )
        else:
            crosses, basis, wide_adj, search, image = state
            count = len(crosses)

            def kernel_mix(p, m, *refs):
                mix_kernel(p, m, refs[:count], *refs[count:])

            mine = call(
                kernel_mix, mine_outs, [place, mixing] + crosses + [image], smem=(0,), limit=limit
            )
        own_out = ((vecs, edge), f32)
        pack_out = ((vecs, 2 * vecs), f32)
        if state is None:
            pack, = call(gram_kernel, [pack_out], [stack, mixing], limit=limit)
        else:

            def kernel_stack(m, *refs):
                stack_kernel(last, m, refs[:count], *refs[count:])

            pack, *rest = call(
                kernel_stack,
                [pack_out] + ([own_out, own_out] if last else [stack_out]),
                [mixing] + crosses + [basis, wide_adj, search] + [seeking] * last,
                limit=limit,
                scratch=[stack_out] * last,
            )
            stack = rest[0]
        if panels == 2:
            other = swap(mine[1], 1, "panel")
            other, pack = lax.optimization_barrier((other, pack))
            rotated_adj = mine[0] + other
        else:
            rotated_adj = lax.psum_scatter(mine[0], "panel", scatter_dimension=0, tiled=True)[0]
        packs = panel_terms(pack)
        pack_count = len(packs)

        def kernel_factor(*refs):
            factor_kernel(nodes, refs[:pack_count], *refs[pack_count:])

        inverse, *scale = call(
            kernel_factor, [((vecs, vecs), f32)] + [((vecs, 2 * vecs), f32)] * last, packs
        )
        if last:
            break
        far_parts = far_values(rotated_adj, near)
        far_parts, inverse = lax.optimization_barrier((far_parts, inverse))
        held, = call(
            functools.partial(solve_kernel, len(far_parts)),
            [((len(far_parts) * vecs, edge), bf16)],
            far_parts + [inverse],
            limit=limit,
        )
        adj_parts = near_values(held, near)
        basis, search, square = call(
            basis_kernel,
            [((2 * vecs, wide), bf16), ((vecs, wide), f32), own_out],
            [inverse, stack, mixing, seeking],
            limit=limit,
        )
        cross, wide_adj = call(
            functools.partial(cross_kernel, nodes, near),
            [pack_out, ((vecs, wide), bf16)],
            adj_parts + [basis, square],
            limit=limit,
        )
        image, = call(
            ahead_kernel,
            [((3 * vecs, blocks * edge), f32)],
            [basis, wide_adj, search, dense],
            limit=limit,
        )
        state = (panel_terms(cross), basis, wide_adj, search, image)

    search, rotated = rest
    terms, = call(terms_kernel, [((vecs, 2 * vecs), f32)], [rotated, rotated_adj])
    far_parts, inverse = lax.optimization_barrier((far_values(terms, near), inverse))
    own_basis, own_dirs, both = call(
        own_kernel,
        [own_out, own_out, ((vecs, 2 * edge), f32)],
        [inverse, *scale, rotated, rotated_adj, search],
    )
    terms = panel_terms(sum(near_values(sum(far_parts), near)[::-1]))
    count = len(terms)

    def kernel_last(*refs):
        last_kernel(nodes, refs[:count], *refs[count:])

    resid, rayleigh = call(
        kernel_last, [own_out, ((vecs, vecs), f32)], terms + [inverse, both]
    )
    return (own_basis, resid, own_dirs, rayleigh)


def solution(mesh):
    return jax.shard_map(
        body,
        mesh=mesh,
        in_specs=(
            P("rows", "panel", None, None, None, None),
            P("rows", "panel", None),
            P("rows", "panel", None, None),
            P(None, ("rows", "panel")),
            P(None, ("rows", "panel")),
            P(None, ("rows", "panel")),
            P(),
            P(),
        ),
        out_specs=(
            P(None, ("rows", "panel")),
            P(None, ("rows", "panel")),
            P(None, ("rows", "panel")),
            P(),
        ),
        check_vma=False,
    )
```

```python
import functools

import jax
import jax.numpy as jnp
from jax import lax
from jax.experimental import pallas as pl
from jax.experimental.pallas import tpu as pltpu
from jax.sharding import PartitionSpec as P

epsilon = 1e-06
highest = lax.Precision.HIGHEST
f32 = jnp.float32
bf16 = jnp.bfloat16


def call(kernel, outs, args, smem=(), limit=16, scratch=()):
    specs = [
        pl.BlockSpec(memory_space=pltpu.SMEM if i in smem else pltpu.VMEM) for i in range(len(args))
    ]
    return pl.pallas_call(
        kernel,
        out_shape=[jax.ShapeDtypeStruct(shape, kind) for shape, kind in outs],
        in_specs=specs,
        out_specs=[pl.BlockSpec(memory_space=pltpu.VMEM) for _ in outs],
        scratch_shapes=[pltpu.VMEM(shape, kind) for shape, kind in scratch],
        compiler_params=pltpu.CompilerParams(vmem_limit_bytes=limit << 20),
    )(*args)


def pieces(value):
    high = value.astype(bf16)
    rest = value - high.astype(f32)
    middle = rest.astype(bf16)
    low = (rest - middle.astype(f32)).astype(bf16)
    return jnp.concatenate([high, middle, low], axis=0)


def halves(value):
    high = value.astype(bf16)
    return high, (value - high.astype(f32)).astype(bf16)


def times_stack(weights, stack):
    rows = weights.shape[0]
    parts = jnp.dot(pieces(weights), stack, preferred_element_type=f32)
    return parts[:rows] + parts[rows : 2 * rows] + parts[2 * rows :]


def dot_nt(left, right):
    return lax.dot_general(
        left, right, (((1,), (1,)), ((), ())), precision=highest, preferred_element_type=f32
    )


def dot_tn(left, right):
    return lax.dot_general(
        left, right, (((0,), (0,)), ((), ())), precision=highest, preferred_element_type=f32
    )


def dot_nn(left, right):
    return jnp.dot(left, right, precision=highest, preferred_element_type=f32)


def layout_kernel(slots_ref, tiles_ref, dense_ref):
    blocks, slots, edge = tiles_ref.shape[:3]
    many = dense_ref.shape[0] // edge
    dense_ref[...] = jnp.zeros_like(dense_ref)
    for b in range(blocks):
        for s in range(slots):

            @pl.when(slots_ref[b, s] < many)
            def _():
                start = pl.multiple_of(slots_ref[b, s] * edge, edge)
                dense_ref[pl.ds(start, edge), b * edge : (b + 1) * edge] = tiles_ref[b, s].T


def send_parts(place_ref, mix_ref, image, mine_refs):
    edge = mine_refs[0].shape[-1]
    vecs = mix_ref.shape[0]
    high, low = halves(image)
    weights = jnp.concatenate(halves(mix_ref[...]), axis=0)
    mixed = jnp.dot(weights, high, preferred_element_type=f32)
    mixed = mixed[:vecs] + mixed[vecs:] + jnp.dot(weights[:vecs], low, preferred_element_type=f32)
    if len(mine_refs) == 2:
        first = place_ref[0] == 0
        low, high = mixed[:, :edge], mixed[:, edge:]
        mine_refs[0][...] = jnp.where(first, low, high)
        mine_refs[1][...] = jnp.where(first, high, low)
    else:
        for b in range(mine_refs[0].shape[0]):
            mine_refs[0][b] = mixed[:, b * edge : (b + 1) * edge]


def first_kernel(parts, place_ref, dense_ref, mix_ref, *refs):
    part_refs, stack_ref, mine_refs = refs[:parts], refs[parts], refs[parts + 1 :]
    edge = mine_refs[0].shape[-1]
    at = 0
    for ref in part_refs:
        far = ref.shape[0]
        for i in range(far):
            stack_ref[:, at : at + edge] = ref[-i % far]
            at += edge
    image = jnp.dot(stack_ref[...], dense_ref[...], preferred_element_type=f32)
    send_parts(place_ref, mix_ref, image, mine_refs)


def residual_scale(q, square):
    return lax.rsqrt(jnp.maximum(square - jnp.sum((q * q).T, axis=1, keepdims=True), 0.0) + epsilon)


def cross_terms(crosses):
    both = sum(ref[...] for ref in crosses)
    vecs = both.shape[0]
    q = both[:, :vecs]
    scale = residual_scale(q, both[:, vecs : vecs + 1])
    at = vecs + vecs // 2
    return q, scale, lax.rsqrt(both[:, at : at + 1] + epsilon)


def ahead_kernel(basis_ref, wide_ref, search_ref, dense_ref, image_ref):
    vecs = wide_ref.shape[0]
    rows = jnp.concatenate([basis_ref[:vecs], wide_ref[...], search_ref[...].astype(bf16)], axis=0)
    image_ref[...] = jnp.dot(rows, dense_ref[...], preferred_element_type=f32)


def mix_kernel(place_ref, mix_ref, crosses, image_ref, *mine_refs):
    vecs = mix_ref.shape[0]
    q, scale, step = cross_terms(crosses)
    basis = image_ref[:vecs]
    q_high, q_low = halves(q)
    high, low = halves(basis)
    raw = lax.dot_general(
        jnp.concatenate([q_high, q_high, q_low], axis=0),
        jnp.concatenate([high, low, high], axis=0),
        (((0,), (0,)), ((), ())),
        preferred_element_type=f32,
    )
    raw = raw - image_ref[vecs : 2 * vecs]
    image = jnp.concatenate([basis, raw * scale, image_ref[2 * vecs :] * step], axis=0)
    send_parts(place_ref, mix_ref, image, mine_refs)


def gram_terms(stack, mix_ref, pack_ref, search_refs):
    vecs = mix_ref.shape[0]
    weights = jnp.concatenate(halves(mix_ref[...]), axis=0)
    rotated = jnp.dot(weights, stack, preferred_element_type=f32)
    rotated = rotated[:vecs] + rotated[vecs:]
    square = jnp.zeros((vecs, vecs), f32)
    if search_refs:
        weights_ref, search_out, own_rotated = search_refs
        edge = search_out.shape[1]
        search = times_stack(weights_ref[...], stack[vecs:])
        search_out[...] = search[:, :edge]
        own_rotated[...] = rotated[:, :edge]
        square = jnp.broadcast_to(jnp.sum(search * search, axis=1, keepdims=True), square.shape)
    split = jnp.concatenate(halves(rotated), axis=0)
    gram = lax.dot_general(split, split, (((1,), (1,)), ((), ())), preferred_element_type=f32)
    gram = gram[:vecs] + gram[vecs:]
    pack_ref[...] = jnp.concatenate([gram[:, :vecs] + gram[:, vecs:], square], axis=1)


def gram_kernel(stack_ref, mix_ref, pack_ref):
    gram_terms(stack_ref[...], mix_ref, pack_ref, ())


def stack_kernel(last, mix_ref, crosses, basis_ref, wide_ref, found_ref, *refs):
    vecs = wide_ref.shape[0]
    if last:
        weights, pack_ref, outs, stack_ref = refs[:1], refs[1], refs[2:4], refs[4]
    else:
        weights, pack_ref, outs, stack_ref = (), refs[0], (), refs[1]
    q, scale, step = cross_terms(crosses)
    terms = jnp.concatenate([*halves(q), q.astype(bf16)], axis=0)
    basis = jnp.concatenate([basis_ref[:vecs], basis_ref[:vecs], basis_ref[vecs : 2 * vecs]], axis=0)
    part = lax.dot_general(terms, basis, (((0,), (0,)), ((), ())), preferred_element_type=f32)
    stack_ref[:vecs] = basis_ref[:vecs]
    stack_ref[vecs : 2 * vecs] = ((part - wide_ref[...].astype(f32)) * scale).astype(bf16)
    stack_ref[2 * vecs :] = (found_ref[...] * step).astype(bf16)
    gram_terms(stack_ref[...], mix_ref, pack_ref, (*weights, *outs))


def factor_kernel(nodes, packs, inverse_ref, *scale_ref):
    vecs = inverse_ref.shape[0]
    total = sum(ref[...] for ref in packs) / nodes
    if scale_ref:
        scale_ref[0][...] = lax.rsqrt(jnp.maximum(total, 0.0) + epsilon)
    row_ids = lax.broadcasted_iota(jnp.int32, (vecs, 2 * vecs), 0)
    lane_ids = lax.broadcasted_iota(jnp.int32, (vecs, 2 * vecs), 1)
    diagonal = jnp.where(lane_ids == row_ids, total, 0.0)
    across = lax.rsqrt(jnp.sum(diagonal, axis=0, keepdims=True))
    height, step = 8, 4
    shape = (height, 2 * vecs)
    ids = lax.broadcasted_iota(jnp.int32, shape, 0)
    lanes = lax.broadcasted_iota(jnp.int32, shape, 1)

    def lane(tile, index):
        return jnp.take_along_axis(tile, index, axis=1)

    tiles = []
    for t in range(0, vecs, height):
        tile = total[t : t + height]
        down = lax.rsqrt(lane(tile, ids + t))
        unit = jnp.where(lanes == ids + (t + vecs), down, 0.0)
        tiles.append(jnp.where(lanes < vecs, tile * down * across, unit))
    done = [None] * len(tiles)
    for j in range(0, vecs, step):
        t, s = divmod(j, height)
        rows = [jnp.broadcast_to(tiles[t][s + m : s + m + 1], shape) for m in range(step)]
        columns = [
            [lane(tile, jnp.full(shape, k, jnp.int32)) for k in range(j, j + step)] for tile in tiles[t:]
        ]

        def pivot(m, n):
            return jnp.broadcast_to(columns[0][n][s + m : s + m + 1], shape)

        p00, p10, p11 = pivot(0, 0), pivot(1, 0), pivot(1, 1)
        q20, q21, q30, q31 = pivot(2, 0), pivot(2, 1), pivot(3, 0), pivot(3, 1)
        w22, w32, w33 = pivot(2, 2), pivot(3, 2), pivot(3, 3)
        scale = 1.0 / (p00 * p11 - p10 * p10)
        i00, i10, i11 = p11 * scale, -p10 * scale, p00 * scale
        e20, e21 = q20 * i00 + q21 * i10, q20 * i10 + q21 * i11
        e30, e31 = q30 * i00 + q31 * i10, q30 * i10 + q31 * i11
        s22 = w22 - (e20 * q20 + e21 * q21)
        s32 = w32 - (e30 * q20 + e31 * q21)
        s33 = w33 - (e30 * q30 + e31 * q31)
        scale = 1.0 / (s22 * s33 - s32 * s32)
        u22, u32, u33 = s33 * scale, -s32 * scale, s22 * scale
        below2 = rows[2] - (e20 * rows[0] + e21 * rows[1])
        below3 = rows[3] - (e30 * rows[0] + e31 * rows[1])
        y2, y3 = below2 * u22 + below3 * u32, below2 * u32 + below3 * u33
        z0 = rows[0] - (y2 * q20 + y3 * q30)
        z1 = rows[1] - (y2 * q21 + y3 * q31)
        y0, y1 = z0 * i00 + z1 * i10, z0 * i10 + z1 * i11
        for u in range(t, len(tiles)):
            if u == t and s + step == height:
                continue
            x0, x1, x2, x3 = columns[u - t]
            less = (x0 * y0 + x1 * y1) + (x2 * y2 + x3 * y3)
            if u == t:
                less = jnp.where(ids >= s + step, less, 0.0)
            tiles[u] = tiles[u] - less
        ratio = p10 / p00
        finished = [rows[0], rows[1] - ratio * rows[0], below2, below3 - (s32 / s22) * below2]
        roots = [p00, p11 - ratio * p10, s22, s33 - (s32 / s22) * s32]
        for m in range(step):
            value = finished[m] * lax.rsqrt(roots[m])
            done[t] = value if done[t] is None else jnp.where(ids >= s + m, value, done[t])
    inverse_ref[...] = jnp.concatenate(done, axis=0)[:, vecs:]


def basis_kernel(inverse_ref, stack_ref, mix_ref, weights_ref, basis_ref, search_ref, square_ref):
    vecs = mix_ref.shape[0]
    search = times_stack(weights_ref[...], stack_ref[vecs:])
    search_ref[...] = search
    square_ref[...] = jnp.broadcast_to(jnp.sum(search * search, axis=1, keepdims=True), square_ref.shape)
    basis = times_stack(dot_nn(inverse_ref[...], mix_ref[...]), stack_ref[...])
    basis_ref[...] = jnp.concatenate(halves(basis), axis=0)


def terms_kernel(rotated_ref, adj_ref, terms_ref):
    adj = adj_ref[...]
    terms_ref[...] = jnp.concatenate([dot_nt(rotated_ref[...], adj), dot_nt(adj, adj)], axis=1)


def own_kernel(inverse_ref, scale_ref, rotated_ref, adj_ref, search_ref, basis_ref, dirs_ref, both_ref):
    vecs, edge = rotated_ref.shape
    both = dot_nn(inverse_ref[...], jnp.concatenate([rotated_ref[...], adj_ref[...]], axis=1))
    both_ref[...] = both
    basis_ref[...] = both[:, :edge]
    dirs_ref[...] = search_ref[...] * scale_ref[:, vecs : vecs + 1]


def last_kernel(nodes, terms, inverse_ref, both_ref, resid_ref, rayleigh_ref):
    vecs, edge = resid_ref.shape
    inverse = inverse_ref[...]
    total = sum(ref[...] for ref in terms) / nodes
    turned = dot_nn(inverse, total[:, :vecs])
    square = jnp.sum(dot_nn(inverse, total[:, vecs:]) * inverse, axis=1, keepdims=True)
    q = dot_nt(turned, inverse)
    raw = dot_tn(q, both_ref[:, :edge]) - both_ref[:, edge:]
    resid_ref[...] = raw * residual_scale(q, square)
    row_ids = lax.broadcasted_iota(jnp.int32, (vecs, vecs), 0)
    lane_ids = lax.broadcasted_iota(jnp.int32, (vecs, vecs), 1)
    rayleigh_ref[...] = jnp.where(row_ids == lane_ids, 1.0, 0.0) - q


def solve_kernel(parts, *refs):
    part_refs, inverse_ref, blocks_ref = refs[:parts], refs[parts], refs[parts + 1]
    vecs, edge = part_refs[0].shape
    solved = dot_nn(inverse_ref[...], jnp.concatenate([ref[...] for ref in part_refs], axis=1))
    for i in range(parts):
        blocks_ref[i * vecs : (i + 1) * vecs, :] = solved[:, i * edge : (i + 1) * edge].astype(bf16)


def cross_kernel(nodes, parts, *refs):
    part_refs, (basis_ref, search_ref, cross_ref, wide_ref) = refs[:parts], refs[parts:]
    vecs = wide_ref.shape[0]
    edge = part_refs[0].shape[1]
    at = 0
    for ref in part_refs:
        for i in range(ref.shape[0] // vecs):
            wide_ref[:, at : at + edge] = ref[i * vecs : (i + 1) * vecs, :]
            at += edge
    cross = lax.dot_general(
        basis_ref[...], wide_ref[...], (((1,), (1,)), ((), ())), preferred_element_type=f32
    )
    cross = cross[:vecs] + cross[vecs:]
    values = wide_ref[...].astype(f32)
    square = jnp.sum(values * values, axis=1, keepdims=True)
    half = (vecs, vecs // 2)
    squares = [jnp.broadcast_to(square, half), jnp.broadcast_to(search_ref[:, :1], half)]
    cross_ref[...] = jnp.concatenate([cross, *squares], axis=1) / nodes


def swap(value, by, axis):
    size = lax.axis_size(axis)
    return lax.ppermute(value, axis, [(i, i ^ by) for i in range(size)])


def panel_terms(value):
    if lax.axis_size("panel") == 2:
        return [value, swap(value, 1, "panel")]
    return [lax.psum(value, "panel")]


def far_values(value, near):
    far = lax.axis_size("rows") // near
    return [value] + [swap(value, near * i, "rows") for i in range(far - 1, 0, -1)]


def near_values(held, near):
    return [held] + [swap(held, i, "rows") for i in range(near - 1, 0, -1)]


def body(
    adj_tiles,
    row_counts,
    tile_cols,
    start_basis,
    start_resid,
    start_search,
    ritz_basis,
    ritz_search,
):
    tile_set = adj_tiles[0, 0]
    counts = row_counts[0, 0]
    columns = tile_cols[0, 0]
    blocks, slots, edge = tile_set.shape[:3]
    vecs = start_basis.shape[0]
    rows, panels = lax.axis_size("rows"), lax.axis_size("panel")
    nodes = start_basis.shape[1] * rows * panels
    wide = rows * edge
    near = 4
    place = lax.axis_index("panel").astype(jnp.int32).reshape(1)

    if panels == 2:
        mine_outs = [((vecs, edge), f32)] * 2
    else:
        mine_outs = [((blocks, vecs, edge), f32)]
    stack_out = ((3 * vecs, wide), bf16)
    limit = 16 if wide <= 4096 else 56

    start = jnp.concatenate([start_basis, start_resid, start_search], axis=0)[None]
    sweeps = ritz_basis.shape[0]
    first_parts = far_values(start, near)
    held = jnp.concatenate(first_parts[:1] + first_parts[:0:-1], axis=0)
    held, counts, columns, tile_set, ritz_basis, ritz_search = lax.optimization_barrier(
        (held, counts, columns, tile_set, ritz_basis, ritz_search)
    )
    away = columns ^ lax.axis_index("rows")
    far = rows // near
    position = (-away % near) * far + -(away // near) % far
    in_use = jnp.arange(slots, dtype=jnp.int32)[None, :] < counts[:, None]
    slot_ids = jnp.where(in_use, position, rows).astype(jnp.int32)
    parts = near_values(held, near)
    dense, = call(
        layout_kernel, [((wide, blocks * edge), bf16)], [slot_ids, tile_set], smem=(0,), limit=limit
    )
    ritz = [(ritz_basis[sweep], ritz_search[sweep]) for sweep in range(sweeps)]
    parts, dense, ritz = lax.optimization_barrier((parts, dense, ritz))
    state = None
    for sweep in range(sweeps):
        last = sweep == sweeps - 1
        mixing, seeking = ritz[sweep]
        if state is None:
            stack, *mine = call(
                functools.partial(first_kernel, near),
                [stack_out] + mine_outs,
                [place, dense, mixing] + parts,
                smem=(0,),
                limit=limit,
            )
        else:
            crosses, basis, wide_adj, search, image = state
            count = len(crosses)

            def kernel_mix(p, m, *refs):
                mix_kernel(p, m, refs[:count], *refs[count:])

            mine = call(
                kernel_mix, mine_outs, [place, mixing] + crosses + [image], smem=(0,), limit=limit
            )
        own_out = ((vecs, edge), f32)
        pack_out = ((vecs, 2 * vecs), f32)
        if state is None:
            pack, = call(gram_kernel, [pack_out], [stack, mixing], limit=limit)
        else:

            def kernel_stack(m, *refs):
                stack_kernel(last, m, refs[:count], *refs[count:])

            pack, *rest = call(
                kernel_stack,
                [pack_out] + ([own_out, own_out] if last else [stack_out]),
                [mixing] + crosses + [basis, wide_adj, search] + [seeking] * last,
                limit=limit,
                scratch=[stack_out] * last,
            )
            stack = rest[0]
        if panels == 2:
            other = swap(mine[1], 1, "panel")
            other, pack = lax.optimization_barrier((other, pack))
            rotated_adj = mine[0] + other
        else:
            rotated_adj = lax.psum_scatter(mine[0], "panel", scatter_dimension=0, tiled=True)[0]
        packs = panel_terms(pack)
        pack_count = len(packs)

        def kernel_factor(*refs):
            factor_kernel(nodes, refs[:pack_count], *refs[pack_count:])

        inverse, *scale = call(
            kernel_factor, [((vecs, vecs), f32)] + [((vecs, 2 * vecs), f32)] * last, packs
        )
        if last:
            break
        far_parts = far_values(rotated_adj, near)
        far_parts, inverse = lax.optimization_barrier((far_parts, inverse))
        held, = call(
            functools.partial(solve_kernel, len(far_parts)),
            [((len(far_parts) * vecs, edge), bf16)],
            far_parts + [inverse],
            limit=limit,
        )
        adj_parts = near_values(held, near)
        basis, search, square = call(
            basis_kernel,
            [((2 * vecs, wide), bf16), ((vecs, wide), f32), own_out],
            [inverse, stack, mixing, seeking],
            limit=limit,
        )
        cross, wide_adj = call(
            functools.partial(cross_kernel, nodes, near),
            [pack_out, ((vecs, wide), bf16)],
            adj_parts + [basis, square],
            limit=limit,
        )
        image, = call(
            ahead_kernel,
            [((3 * vecs, blocks * edge), f32)],
            [basis, wide_adj, search, dense],
            limit=limit,
        )
        state = (panel_terms(cross), basis, wide_adj, search, image)

    search, rotated = rest
    terms, = call(terms_kernel, [((vecs, 2 * vecs), f32)], [rotated, rotated_adj])
    far_parts, inverse = lax.optimization_barrier((far_values(terms, near), inverse))
    own_basis, own_dirs, both = call(
        own_kernel,
        [own_out, own_out, ((vecs, 2 * edge), f32)],
        [inverse, *scale, rotated, rotated_adj, search],
    )
    terms = panel_terms(sum(near_values(sum(far_parts), near)[::-1]))
    count = len(terms)

    def kernel_last(*refs):
        last_kernel(nodes, refs[:count], *refs[count:])

    resid, rayleigh = call(
        kernel_last, [own_out, ((vecs, vecs), f32)], terms + [inverse, both]
    )
    return (own_basis, resid, own_dirs, rayleigh)


def solution(mesh):
    return jax.shard_map(
        body,
        mesh=mesh,
        in_specs=(
            P("rows", "panel", None, None, None, None),
            P("rows", "panel", None),
            P("rows", "panel", None, None),
            P(None, ("rows", "panel")),
            P(None, ("rows", "panel")),
            P(None, ("rows", "panel")),
            P(),
            P(),
        ),
        out_specs=(
            P(None, ("rows", "panel")),
            P(None, ("rows", "panel")),
            P(None, ("rows", "panel")),
            P(),
        ),
        check_vma=False,
    )
```
